128 devices in a mesh: tile: 16 (over y_hi, z, core), sub: 8 (over y_lo, x).
Axes of the slice: x: 4, y: 4 (y_hi: 2, y_lo: 2; y = y_hi * 2 + y_lo), z: 4, core: 2. Of those that a mesh axis runs over, the one named last changes fastest.
Arguments:
- adjoint_final: float32 [2, 16, 8192, 512], P(None, None, ('tile', 'sub')), may hold values from -6 to 6
- diff_scale: float32 [16, 8192, 512], P(None, ('tile', 'sub')), may hold values from 0.5 to 1
- vert_coupling: float32 [15, 8192, 512], P(None, ('tile', 'sub')), may hold values from 0.1 to 4
- column_depth: int32 [8192, 512], P(('tile', 'sub')), may hold values from 0 to 16
- seam_table: int32 [16, 4, 3], replicated, may hold values from 0 to 15, as said below
- tile_owner: int32 [16], replicated, may hold values from 0 to 15, each once
- prof_face: int32 [32768], P(('tile', 'sub')), may hold values from 0 to 15, as said below
- prof_cell: int32 [32768], P(('tile', 'sub')), may hold values from 0 to 262143
- prof_time: int32 [32768], P(('tile', 'sub')), may hold values from 1 to 2
- misfit: float32 [2, 16, 32768], P(None, None, ('tile', 'sub')), may hold values from -6 to 6
Outputs:
- adjoint_initial: float32 [2, 16, 8192, 512], P(None, None, ('tile', 'sub'))
The draws below stay inside these ranges and needn't reach their ends.
Inputs may be any that keep to these rules, and one draw needn't show every extreme that they name: seam_table[f, e] = (g, e2, r) pairs every edge with a different edge and the pairing is mutual with the same r; r is 0 or 1. `prof_face`: among the 256 rows of one device, at most 4 name the same face tile and the same block of 64 tile rows; one such pair is named exactly 4 times by the rows of every device. `tile_owner`: a permutation.
All inputs are finite; a program needn't handle non-finite values.
Results may differ from the reference program's by a relative error of at most 0.000062.
Values sent between devices are 32-bit elements; how exact they have to be, the bound alone decides.
No kernel may reach another device: no remote copies, remote signals or barrier semaphores. Data moves between devices by JAX's collectives and lax.ppermute only.
A program may use at most 128 MiB of HBM per device.

```python
import math
import jax
import jax.numpy as jnp

LEVELS = 16
ROWS_DEV = 64
CAP = 4
TILE_COLS = 512
FACES = 16
GRID_ROWS = 8192
PROFILES_DEV = 256
PROFILES = 32768
N_TILE = 16
N_SUB = 8


def profile_table(key):
    base_key = jax.random.fold_in(key, 7001)
    pair_count = FACES * N_SUB
    slot_total = pair_count * CAP
    busiest = jax.random.randint(jax.random.fold_in(base_key, 1), (), 0, pair_count)

    def one_block(block_index):
        block_key = jax.random.fold_in(base_key, 100 + block_index)
        shuffle = jax.random.permutation(jax.random.fold_in(block_key, 1), slot_total)
        slot_ids = jnp.arange(slot_total, dtype=jnp.int32)
        slot_rank = jnp.zeros((slot_total,), jnp.int32).at[shuffle].set(slot_ids)
        slot_score = jnp.where(slot_ids // CAP == busiest, -1, slot_rank)
        chosen = jnp.argsort(slot_score, stable=True)[:PROFILES_DEV].astype(jnp.int32)
        shuffled = jax.random.permutation(jax.random.fold_in(block_key, 2), chosen)
        pair_index = shuffled // CAP
        face_index = pair_index // N_SUB
        row_block = pair_index % N_SUB
        tile_row = row_block * ROWS_DEV + jax.random.randint(jax.random.fold_in(block_key, 3), (PROFILES_DEV,), 0, ROWS_DEV)
        tile_col = jax.random.randint(jax.random.fold_in(block_key, 4), (PROFILES_DEV,), 0, TILE_COLS)
        return (face_index.astype(jnp.int32), (tile_row * TILE_COLS + tile_col).astype(jnp.int32))
    face_rows, cell_rows = jax.vmap(one_block)(jnp.arange(N_TILE * N_SUB, dtype=jnp.int32))
    return (face_rows.reshape(-1), cell_rows.reshape(-1))


def draw_prof_face(key, part):
    return profile_table(key)[0]


def draw_prof_cell(key, part):
    return profile_table(key)[1]


def draw_seam_table(key, part):
    base_key = jax.random.fold_in(key, 5003)
    edge_total = 4 * FACES
    shuffle = jax.random.permutation(jax.random.fold_in(base_key, 1), edge_total).astype(jnp.int32)
    first_half = shuffle[0::2]
    second = shuffle[1::2]
    reversal = jax.random.randint(jax.random.fold_in(base_key, 2), (2 * FACES,), 0, 2).astype(jnp.int32)
    partner = jnp.zeros((edge_total,), jnp.int32).at[first_half].set(second).at[second].set(first_half)
    orientation = jnp.zeros((edge_total,), jnp.int32).at[first_half].set(reversal).at[second].set(reversal)
    table = jnp.stack([partner // 4, partner % 4, orientation], axis=1)
    return table.reshape(FACES, 4, 3)


def plant(drawn, own_key, smallest, largest):
    spot = [jax.random.randint(jax.random.fold_in(own_key, axis), (), 0, length) for axis, length in enumerate(drawn.shape)]
    main_axis = drawn.shape.index(max(drawn.shape))
    beside = spot[:main_axis] + [(spot[main_axis] + 1) % drawn.shape[main_axis]] + spot[main_axis + 1:]
    return drawn.at[tuple(spot)].set(smallest).at[tuple(beside)].set(largest)


def shard_levels(key, shape, split, least, high):
    factor_of = 1.0
    for dim, blocks in split:
        heights = jax.random.uniform(jax.random.fold_in(jax.random.fold_in(key, 6), dim), (blocks,), jnp.float32, least / len(split), high / len(split))
        factor_of = factor_of * jnp.repeat(jnp.exp(heights), shape[dim] // blocks).reshape((-1,) + (1,) * (len(shape) - 1 - dim))
    return factor_of


def gaussian(rng, dims, deviation, bound, cuts=(), held_as=jnp.bfloat16):
    entries = jax.random.normal(rng, dims, jnp.float32) * deviation
    if len(cuts) > 0:
        entries = shard_levels(rng, dims, cuts, -0.22, 0.18) * entries
    return jnp.clip(entries, min=-bound, max=bound).astype(held_as)


def setup_inputs(seed: int = 0) -> dict:
    seeds = jax.random.split(jax.random.key(seed), 11)
    return {
        "adjoint_final": gaussian(seeds[0], (2, LEVELS, GRID_ROWS, TILE_COLS), 1.0, 6.0, ((2, 128),), jnp.float32),
        "diff_scale": jnp.clip(jnp.exp(math.log(1.0) - 0.6931472 * jax.random.uniform(seeds[1], (LEVELS, GRID_ROWS, TILE_COLS), jnp.float32) ** shard_levels(seeds[1], (LEVELS, GRID_ROWS, TILE_COLS), ((1, 128),), -0.2, 0.2)), 0.5, 1.0),
        "vert_coupling": jnp.clip(jnp.exp(math.log(4.0) - 3.6888794 * jax.random.uniform(seeds[2], (LEVELS - 1, GRID_ROWS, TILE_COLS), jnp.float32) ** shard_levels(seeds[2], (LEVELS - 1, GRID_ROWS, TILE_COLS), ((1, 128),), -0.2, 0.2)), 0.1, 4.0),
        "column_depth": plant(jax.random.randint(seeds[3], (GRID_ROWS, TILE_COLS), 0, LEVELS + 1), jax.random.fold_in(seeds[3], 1), 0, LEVELS).astype(jnp.int32),
        "seam_table": draw_seam_table(jax.random.fold_in(seeds[10], 71), 0),
        "tile_owner": jax.random.permutation(seeds[5], FACES).astype(jnp.int32),
        "prof_face": draw_prof_face(jax.random.fold_in(seeds[10], 71), 0),
        "prof_cell": draw_prof_cell(jax.random.fold_in(seeds[10], 71), 0),
        "prof_time": plant(jax.random.randint(seeds[8], (PROFILES,), 1, 3), jax.random.fold_in(seeds[8], 1), 1, 2).astype(jnp.int32),
        "misfit": gaussian(seeds[9], (2, LEVELS, PROFILES), 1.0, 6.0, ((2, 128),), jnp.float32),
    }


explicit_rate = 0.2


def wet_levels(column_depth, levels):
    level_ids = jnp.arange(levels, dtype=jnp.int32)[:, None, None]
    return jnp.where(level_ids < column_depth[None, :, :], 1.0, 0.0).astype(jnp.float32)


def vertical_solve(adjoint, coupling, wet_cells):
    levels = adjoint.shape[1]
    couplings = [coupling[level] * wet_cells[level] * wet_cells[level + 1] for level in range(levels - 1)]
    nothing = jnp.zeros_like(wet_cells[0])
    lower_link = [nothing] + couplings
    upper_link = couplings + [nothing]
    ratio_list = []
    partial_list = []
    for level in range(levels):
        diagonal = 1.0 + lower_link[level] + upper_link[level]
        if level == 0:
            pivot_value = diagonal
            partial_value = adjoint[:, 0] / pivot_value
        else:
            pivot_value = diagonal - lower_link[level] * ratio_list[level - 1]
            partial_value = (adjoint[:, level] + lower_link[level] * partial_list[level - 1]) / pivot_value
        ratio_list.append(upper_link[level] / pivot_value)
        partial_list.append(partial_value)
    result = [None] * levels
    result[levels - 1] = partial_list[levels - 1]
    for level in range(levels - 2, -1, -1):
        result[level] = partial_list[level] + ratio_list[level] * result[level + 1]
    return jnp.stack(result, axis=1)


def adjoint_step(adjoint, weight, coupling, wet_cells, seam_table, tile_owner):
    solved = vertical_solve(adjoint, coupling, wet_cells)
    weighted = weight * solved
    levels = adjoint.shape[1]
    tiles = weighted.reshape(2, levels, N_TILE, TILE_COLS, TILE_COLS)
    tile_edges = jnp.stack([tiles[:, :, :, 0, :], tiles[:, :, :, -1, :], tiles[:, :, :, :, 0], tiles[:, :, :, :, -1]], axis=3)
    tile_ids = jnp.arange(N_TILE, dtype=jnp.int32)
    face_of_tile = jnp.zeros((N_TILE,), jnp.int32).at[tile_owner].set(tile_ids)
    seam_rows = seam_table[face_of_tile]
    border_tile = tile_owner[seam_rows[:, :, 0]]
    strips = tile_edges[:, :, border_tile, seam_rows[:, :, 1], :]
    reversed_flag = (seam_rows[:, :, 2] == 1)[None, None, :, :, None]
    strips = jnp.where(reversed_flag, strips[..., ::-1], strips)
    above_rows = jnp.concatenate([strips[:, :, :, 0, None, :], tiles[:, :, :, :-1, :]], axis=3)
    below_rows = jnp.concatenate([tiles[:, :, :, 1:, :], strips[:, :, :, 1, None, :]], axis=3)
    west_cols = jnp.concatenate([strips[:, :, :, 2, :, None], tiles[..., :-1]], axis=4)
    east_cols = jnp.concatenate([tiles[..., 1:], strips[:, :, :, 3, :, None]], axis=4)
    laplace = above_rows + below_rows + west_cols + east_cols - 4.0 * tiles
    laplace = laplace.reshape(weighted.shape)
    return solved + explicit_rate * weight * laplace


def observation_forcing(tile_owner, prof_face, prof_cell, prof_time, misfit, moment):
    grid_row = tile_owner[prof_face] * TILE_COLS + prof_cell // TILE_COLS
    flat_cell = grid_row * TILE_COLS + prof_cell % TILE_COLS
    total_cells = GRID_ROWS * TILE_COLS
    target_cell = jnp.where(prof_time == moment, flat_cell, total_cells).astype(jnp.int32)
    values = misfit.reshape(2 * LEVELS, PROFILES)
    forcing = jnp.zeros((2 * LEVELS, total_cells), jnp.float32).at[:, target_cell].add(values, mode="drop")
    return forcing.reshape(2, LEVELS, GRID_ROWS, TILE_COLS)


def reference(adjoint_final, diff_scale, vert_coupling, column_depth, seam_table, tile_owner, prof_face, prof_cell, prof_time, misfit):
    wet_cells = wet_levels(column_depth, LEVELS)
    weight = wet_cells * diff_scale
    forcing_early = observation_forcing(tile_owner, prof_face, prof_cell, prof_time, misfit, 1)
    forcing_late = observation_forcing(tile_owner, prof_face, prof_cell, prof_time, misfit, 2)
    adjoint = adjoint_final + forcing_late
    adjoint = adjoint_step(adjoint, weight, vert_coupling, wet_cells, seam_table, tile_owner) + forcing_early
    return adjoint_step(adjoint, weight, vert_coupling, wet_cells, seam_table, tile_owner)
```

```python
import functools

import jax
import jax.numpy as jnp
from jax import lax
from jax.experimental import pallas as pl
from jax.experimental.pallas import tpu as pltpu
from jax.sharding import PartitionSpec as P

CAP = 4
LEVELS = 16
PLANES = 2 * LEVELS
ROWS = 64
COLS = 512
CELLS = ROWS * COLS
N_TILE = 16
N_SUB = 8
DEVICES = N_TILE * N_SUB
FACES = 16
explicit_rate = 0.2
HIGHEST = lax.Precision.HIGHEST
VMEM = pl.BlockSpec(memory_space=pltpu.VMEM)
SMEM = pl.BlockSpec(memory_space=pltpu.SMEM)
META = 16


def iota(shape, axis):
    return lax.broadcasted_iota(jnp.int32, shape, axis)


def params(mib):
    return pltpu.CompilerParams(vmem_limit_bytes=mib * 1024 * 1024)


def f32(*shape):
    return jax.ShapeDtypeStruct(shape, jnp.float32)


def pack_kernel(ids, owner, seam, face, cell, time, misfit, out, meta):
    tile = ids[0]
    sub = ids[1]
    my_face = jnp.int32(0)
    for f in range(FACES):
        my_face = my_face + jnp.where(owner[f] == tile, f, 0)
    meta[12] = tile
    meta[13] = sub
    for edge in range(4):
        other = owner[seam[my_face, edge, 0]]
        away = (
            ((other & 1) ^ (tile & 1)) * 8
            + (((other >> 3) & 1) ^ ((tile >> 3) & 1)) * 4
            + ((((tile >> 1) & 3) + 4 - ((other >> 1) & 3)) & 3)
        )
        meta[3 * edge] = away
        meta[3 * edge + 1] = seam[my_face, edge, 1]
        meta[3 * edge + 2] = seam[my_face, edge, 2]

    rows = face.shape[1]
    faces = face[...]
    home = jnp.zeros_like(faces)
    for f in range(FACES):
        home = jnp.where(faces == f, owner[f], home)
    cells = cell[...]
    tile_row = cells >> 9
    target = home * N_SUB + (tile_row >> 6)
    code = (time[...] - 1) * CELLS + (tile_row & (ROWS - 1)) * COLS + (cells & (COLS - 1))
    first = iota((rows, rows), 0)
    second = iota((rows, rows), 1)
    target_row = jnp.broadcast_to(target.astype(jnp.float32), (rows, rows))
    target_col = jnp.sum(jnp.where(first == second, target_row, 0.0), axis=1, keepdims=True)
    rank = jnp.sum(
        jnp.where((target_col == target_row) & (first < second), 1.0, 0.0), axis=0, keepdims=True
    )
    rank = rank.astype(jnp.int32)
    values = misfit[...]
    tag = code.astype(jnp.float32) + 1.0
    dest = iota((DEVICES, rows), 0)
    total = jnp.zeros((DEVICES, 2 * DEVICES), jnp.float32)
    for k in range(CAP):
        hit = jnp.where((dest == target) & (rank == k), 1.0, 0.0)
        pieces = []
        if k > 0:
            pieces.append(jnp.zeros((PLANES * k, rows), jnp.float32))
        pieces.append(values)
        if k < CAP - 1:
            pieces.append(jnp.zeros((PLANES * (CAP - 1 - k), rows), jnp.float32))
        pieces.append(jnp.where(dest == k, tag, 0.0))
        stacked = jnp.concatenate(pieces, axis=0)
        total = total + lax.dot_general(
            hit, stacked, (((1,), (1,)), ((), ())), precision=HIGHEST,
            preferred_element_type=jnp.float32,
        )
    out[:, 0, :] = total[:, :DEVICES]
    out[:, 1, :] = total[:, DEVICES:] - 1.0


def pack(ids, owner, seam, face, cell, time, misfit):
    return pl.pallas_call(
        pack_kernel,
        out_shape=(f32(DEVICES, 2, DEVICES), jax.ShapeDtypeStruct((META,), jnp.int32)),
        in_specs=[SMEM, SMEM, SMEM, VMEM, VMEM, VMEM, VMEM],
        out_specs=(VMEM, SMEM),
        compiler_params=params(32),
        name="pack",
    )(ids, owner, seam, face, cell, time, misfit)


def forcing_kernel(moment, slots, out, parts, place):
    values = jnp.transpose(slots[:, 0, :])
    tags = (slots[:, 1, :] + 0.5).astype(jnp.int32)
    tags = jnp.where(slots[:, 1, :] < 0.0, -1, tags)
    tags_t = jnp.transpose(tags.astype(jnp.float32)).astype(jnp.int32)
    tag_row = jnp.concatenate([tags_t[k : k + 1, :] for k in range(CAP)], axis=1)
    valid = (tag_row >= moment * CELLS) & (tag_row < (moment + 1) * CELLS)
    row_of = jnp.where(valid, (tag_row & (CELLS - 1)) >> 9, -1)
    on_row = iota((ROWS, CAP * DEVICES), 0) == row_of
    wide = jnp.concatenate([values[PLANES * k : PLANES * (k + 1), :] for k in range(CAP)], axis=1)
    high = wide.astype(jnp.bfloat16).astype(jnp.float32)
    rest = wide - high
    middle = rest.astype(jnp.bfloat16).astype(jnp.float32)
    parts[0] = high
    parts[1] = middle
    parts[2] = rest - middle
    for k in range(CAP):
        col = tags[:, k : k + 1] & (COLS - 1)
        place[k * DEVICES : (k + 1) * DEVICES, :] = jnp.where(
            iota((DEVICES, COLS), 1) == col, 1.0, 0.0
        ).astype(jnp.bfloat16)
    group = 4

    def step(g, carry):
        total = None
        for part in range(3):
            left = []
            for q in range(group):
                row = parts[part, pl.ds(g * group + q, 1), :]
                left.append(jnp.where(on_row, row, 0.0).astype(jnp.bfloat16))
            got = jnp.dot(
                jnp.concatenate(left, axis=0), place[...], preferred_element_type=jnp.float32
            )
            total = got if total is None else total + got
        out[pl.ds(pl.multiple_of(g * group * ROWS, 8), group * ROWS), :] = total
        return carry

    lax.fori_loop(0, PLANES // group, step, 0)


def forcing(slots, moment):
    return pl.pallas_call(
        functools.partial(forcing_kernel, moment),
        out_shape=f32(PLANES * ROWS, COLS),
        in_specs=[VMEM],
        out_specs=VMEM,
        scratch_shapes=[
            pltpu.VMEM((3, PLANES, CAP * DEVICES), jnp.float32),
            pltpu.VMEM((CAP * DEVICES, COLS), jnp.bfloat16),
        ],
        compiler_params=params(32),
        cost_estimate=pl.CostEstimate(flops=3221225472, bytes_accessed=4325376, transcendentals=0),
        name=f"forcing_{moment}",
    )(slots)


QUARTER = PLANES * ROWS


def tile_rows(quarter, plane, block):
    return pl.ds(pl.multiple_of(quarter * QUARTER + plane * ROWS + block * 8, 8), 8)


def eliminate(value, coupling, depth, at):
    links = []
    for k in range(LEVELS - 1):
        links.append(jnp.where(k + 1 < depth, coupling[at(k)], 0.0))
    ratio = []
    partial = [[], []]
    for k in range(LEVELS):
        pivot = jnp.float32(1.0)
        if k > 0:
            pivot = pivot + links[k - 1]
        if k < LEVELS - 1:
            pivot = pivot + links[k]
        if k > 0:
            pivot = pivot - links[k - 1] * ratio[k - 1]
        inverse = 1.0 / pivot
        for tracer in range(2):
            right = value(tracer * LEVELS + k)
            if k > 0:
                right = right + links[k - 1] * partial[tracer][k - 1]
            partial[tracer].append(right * inverse)
        if k < LEVELS - 1:
            ratio.append(links[k] * inverse)
    for k in range(LEVELS - 2, -1, -1):
        for tracer in range(2):
            partial[tracer][k] = partial[tracer][k] + ratio[k] * partial[tracer][k + 1]
    return partial


def solve_tile(value, coupling, scale, depth_ref, solved, weighted, sides, block, quarter):
    columns = slice(quarter * 128, (quarter + 1) * 128)

    def at(plane):
        return (pl.ds(pl.multiple_of(plane * ROWS + block * 8, 8), 8), columns)

    depth = depth_ref[pl.ds(pl.multiple_of(block * 8, 8), 8), columns]
    result = eliminate(value, coupling, depth, at)
    lane = iota((8, 128), 1)
    column = jnp.zeros((8, 128), jnp.float32)
    for k in range(LEVELS):
        weight = jnp.where(k < depth, scale[at(k)], 0.0)
        for tracer in range(2):
            plane = tracer * LEVELS + k
            found = result[tracer][k]
            heavy = weight * found
            solved[tile_rows(quarter, plane, block), :] = found
            weighted[tile_rows(quarter, plane, block), :] = heavy
            if quarter == 0:
                moved = heavy if plane == 0 else pltpu.roll(heavy, plane, 1)
                column = jnp.where(lane == plane, moved, column)
            if quarter == 3:
                column = jnp.where(lane == plane, pltpu.roll(heavy, plane + 1, 1), column)
    if quarter == 0:
        sides[pl.ds(pl.multiple_of(block * 8, 8), 8), :] = column
    if quarter == 3:
        sides[pl.ds(pl.multiple_of(ROWS + block * 8, 8), 8), :] = column


def send_edges(meta, weighted, sides, payload, first_row, last_row):
    sub = meta[13]
    payload[0] = jnp.transpose(sides[...])[:PLANES, :]
    for b in range(4):
        top = weighted[pl.ds(b * PLANES * ROWS, PLANES, stride=ROWS), :]
        bottom = weighted[pl.ds(b * PLANES * ROWS + ROWS - 1, PLANES, stride=ROWS), :]
        payload[1 + b] = jnp.where(sub == N_SUB - 1, bottom, top)
        first_row[b] = top
        last_row[b] = bottom


EDGES = (f32(5, PLANES, 128), f32(4, PLANES, 128), f32(4, PLANES, 128))


def first_kernel(meta, adjoint, force, coupling, scale, depth, solved, weighted, payload,
                 first_row, last_row, sides):
    def step(block, carry):
        for quarter in range(4):
            columns = slice(quarter * 128, (quarter + 1) * 128)

            def value(plane):
                at = (pl.ds(pl.multiple_of(plane * ROWS + block * 8, 8), 8), columns)
                return adjoint[at] + force[at]

            solve_tile(value, coupling, scale, depth, solved, weighted, sides, block, quarter)
        return carry

    lax.fori_loop(0, ROWS // 8, step, 0)
    send_edges(meta, weighted, sides, payload, first_row, last_row)


def first_solve(meta, adjoint, force, coupling, scale, depth):
    big = f32(4 * QUARTER, 128)
    return pl.pallas_call(
        first_kernel,
        out_shape=(big, big) + EDGES,
        in_specs=[SMEM] + [VMEM] * 5,
        out_specs=(VMEM,) * 5,
        scratch_shapes=[pltpu.VMEM((128, 128), jnp.float32)],
        compiler_params=params(32),
        cost_estimate=pl.CostEstimate(flops=30000000, bytes_accessed=20000000, transcendentals=0),
        name="first_solve",
    )(meta, adjoint, force, coupling, scale, depth)


def route_kernel(meta, gathered, send, here, across):
    sub = meta[13]
    lane = iota((PLANES, 128), 1)

    def half(edge, dest, wanted):
        place, other_edge, turned = meta[3 * edge], meta[3 * edge + 1], meta[3 * edge + 2]
        chunk = jnp.where(turned == 1, N_SUB - 1 - dest, dest)
        block = jnp.where(other_edge < 2, 1 + (chunk >> 1), 0)
        side = jnp.where(other_edge < 2, chunk & 1, other_edge - 2)
        found = gathered[place, block]
        return jnp.where(side == wanted, found, pltpu.roll(found, 64, 1))

    for dest in range(N_SUB):
        send[dest, 0] = jnp.where(lane < 64, half(2, dest, 0), half(3, dest, 1))
        send[dest, 1] = jnp.zeros((PLANES, 128), jnp.float32)
    for edge, dest in ((0, 0), (1, N_SUB - 1)):
        found = gathered[meta[3 * edge], 0]
        send[dest, 1] = jnp.where(
            meta[3 * edge + 1] == 2, found, pltpu.roll(found, 64, 1)
        )
    own = jnp.where(sub == N_SUB - 1, 1, 0)
    place_here = meta[3 * own]
    place_across = meta[3 * (1 - own)]
    for b in range(4):
        here[b] = gathered[place_here, 1 + b]
        across[b] = gathered[place_across, 1 + b]


def route(meta, gathered):
    return pl.pallas_call(
        route_kernel,
        out_shape=(f32(N_SUB, 2, PLANES, 128), f32(4, PLANES, 128), f32(4, PLANES, 128)),
        in_specs=[SMEM, VMEM],
        out_specs=(VMEM,) * 3,
        compiler_params=params(16),
        cost_estimate=pl.CostEstimate(flops=1000000, bytes_accessed=1000000, transcendentals=0),
        name="route",
    )(meta, gathered)


def exchange(meta, payload, first_row, last_row):
    def turn(k):
        return [
            (y * 8 + z * 2 + c, y * 8 + ((z + k) % 4) * 2 + c)
            for y in range(2)
            for z in range(4)
            for c in range(2)
        ]

    all_parts = payload[None]
    all_parts = jnp.concatenate(
        [all_parts] + [lax.ppermute(all_parts, "tile", turn(k)) for k in (1, 2, 3)], axis=0
    )
    all_parts = jnp.concatenate(
        [all_parts, lax.ppermute(all_parts, "tile", [(i, i ^ 8) for i in range(N_TILE)])], axis=0
    )
    all_parts = jnp.concatenate(
        [all_parts, lax.ppermute(all_parts, "tile", [(i, i ^ 1) for i in range(N_TILE)])], axis=0
    )
    above = lax.ppermute(last_row, "sub", [(i, i + 1) for i in range(N_SUB - 1)])
    below = lax.ppermute(first_row, "sub", [(i + 1, i) for i in range(N_SUB - 1)])
    send, here, across = route(meta, all_parts)
    got = lax.all_to_all(send, "sub", split_axis=0, concat_axis=0, tiled=True)
    across = lax.ppermute(across, "sub", [(0, N_SUB - 1), (N_SUB - 1, 0)])
    return got, here, across, above, below


def place_halo(meta, got, here, across, above, below, halo, strips):
    sub = meta[13]
    lane = iota((PLANES, 128), 1)

    def source(edge):
        other_edge, turned = meta[3 * edge + 1], meta[3 * edge + 2]
        same = jnp.where(turned == 1, N_SUB - 1 - sub, sub)
        return jnp.where(other_edge == 0, 0, jnp.where(other_edge == 1, N_SUB - 1, same))

    sides = jnp.where(lane < 64, got[source(2), 0], got[source(3), 0])
    to = iota((128, 128), 0)
    of = iota((128, 128), 1)
    turned = jnp.where(to < 64, meta[8], meta[11])
    wanted = jnp.where(turned == 1, (to & 64) + 63 - (to & 63), to)
    pick = jnp.where(of == wanted, 1.0, 0.0)
    strips[:, :PLANES] = lax.dot_general(
        pick, sides, (((1,), (1,)), ((), ())), precision=HIGHEST, preferred_element_type=jnp.float32
    )

    own = jnp.where(sub == N_SUB - 1, 1, 0)
    other_edge, turned = meta[3 * own + 1], meta[3 * own + 2]
    flip = jnp.where(of == jnp.where(turned == 1, 127 - to, to), 1.0, 0.0)
    row = []
    for b in range(4):
        joined = jnp.where(lane < 64, got[2 * b, 1], pltpu.roll(got[2 * b + 1, 1], 64, 1))
        joined = jnp.where(other_edge < 2, across[b], joined)
        row.append(jnp.where(other_edge == own, here[b], joined))
    for b in range(4):
        ordered = jnp.where(turned == 1, row[3 - b], row[b])
        strip = jnp.dot(ordered, flip, precision=HIGHEST, preferred_element_type=jnp.float32)
        at = b * PLANES * 16
        halo[pl.ds(at + 7, PLANES, stride=16), :] = jnp.where(sub == 0, strip, above[b])
        halo[pl.ds(at + 8, PLANES, stride=16), :] = jnp.where(sub == N_SUB - 1, strip, below[b])


def stepped(solved, weighted, scale, depth_ref, halo, strips, block, quarter):
    columns = slice(quarter * 128, (quarter + 1) * 128)
    lane = iota((8, 128), 1)
    row = iota((8, 128), 0)

    here = pl.ds(pl.multiple_of(block * 8, 8), 8)
    depth = depth_ref[here, columns]
    west = strips[here, :]
    east = strips[pl.ds(pl.multiple_of(ROWS + block * 8, 8), 8), :]
    before = jnp.maximum(block - 1, 0)
    after = jnp.minimum(block + 1, ROWS // 8 - 1)

    def value(plane):
        level = plane % LEVELS
        near = (quarter * PLANES + plane) * 16
        center = weighted[tile_rows(quarter, plane, block), :]
        up = jnp.where(block == 0, halo[near : near + 8, :],
                       weighted[tile_rows(quarter, plane, before), :])
        down = jnp.where(block == ROWS // 8 - 1, halo[near + 8 : near + 16, :],
                         weighted[tile_rows(quarter, plane, after), :])
        if quarter == 0:
            left = pltpu.roll(west, 127 - plane, 1)
        else:
            left = weighted[tile_rows(quarter - 1, plane, block), :]
        if quarter == 3:
            right = east if plane == 0 else pltpu.roll(east, 128 - plane, 1)
        else:
            right = weighted[tile_rows(quarter + 1, plane, block), :]
        total = pltpu.roll(jnp.where(row == 7, up, center), 1, 0)
        total = total + pltpu.roll(jnp.where(row == 0, down, center), 7, 0)
        total = total + pltpu.roll(jnp.where(lane == 127, left, center), 1, 1)
        total = total + pltpu.roll(jnp.where(lane == 0, right, center), 127, 1)
        at = pl.ds(pl.multiple_of(level * ROWS + block * 8, 8), 8)
        weight = jnp.where(level < depth, scale[at, columns], 0.0)
        return solved[tile_rows(quarter, plane, block), :] + explicit_rate * weight * (
            total - 4.0 * center
        )

    return value


def second_kernel(meta, got, here, across, above, below, solved_in, weighted_in, force, coupling,
                  scale, depth, solved, weighted, payload, first_row, last_row, sides, halo,
                  strips):
    place_halo(meta, got, here, across, above, below, halo, strips)

    def step(block, carry):
        for quarter in range(4):
            columns = slice(quarter * 128, (quarter + 1) * 128)
            late = stepped(solved_in, weighted_in, scale, depth, halo, strips, block, quarter)

            def value(plane):
                at = (pl.ds(pl.multiple_of(plane * ROWS + block * 8, 8), 8), columns)
                return late(plane) + force[at]

            solve_tile(value, coupling, scale, depth, solved, weighted, sides, block, quarter)
        return carry

    lax.fori_loop(0, ROWS // 8, step, 0)
    send_edges(meta, weighted, sides, payload, first_row, last_row)


HALO = [
    pltpu.VMEM((4 * PLANES * 16, 128), jnp.float32),
    pltpu.VMEM((128, 128), jnp.float32),
]


def second_solve(meta, halos, solved, weighted, force, coupling, scale, depth):
    big = f32(4 * QUARTER, 128)
    return pl.pallas_call(
        second_kernel,
        out_shape=(big, big) + EDGES,
        in_specs=[SMEM] + [VMEM] * 11,
        out_specs=(VMEM,) * 5,
        scratch_shapes=[pltpu.VMEM((128, 128), jnp.float32)] + HALO,
        compiler_params=params(32),
        cost_estimate=pl.CostEstimate(flops=50000000, bytes_accessed=30000000, transcendentals=0),
        name="second_solve",
    )(meta, *halos, solved, weighted, force, coupling, scale, depth)


def last_kernel(meta, got, here, across, above, below, solved, weighted, scale, depth, out, halo,
                strips):
    place_halo(meta, got, here, across, above, below, halo, strips)

    def step(block, carry):
        for quarter in range(4):
            columns = slice(quarter * 128, (quarter + 1) * 128)
            value = stepped(solved, weighted, scale, depth, halo, strips, block, quarter)
            for plane in range(PLANES):
                at = (pl.ds(pl.multiple_of(plane * ROWS + block * 8, 8), 8), columns)
                out[at] = value(plane)
        return carry

    lax.fori_loop(0, ROWS // 8, step, 0)


def last_step(meta, halos, solved, weighted, scale, depth):
    return pl.pallas_call(
        last_kernel,
        out_shape=f32(PLANES * ROWS, COLS),
        in_specs=[SMEM] + [VMEM] * 9,
        out_specs=VMEM,
        scratch_shapes=HALO,
        compiler_params=params(32),
        cost_estimate=pl.CostEstimate(flops=20000000, bytes_accessed=20000000, transcendentals=0),
        name="last_step",
    )(meta, *halos, solved, weighted, scale, depth)


def body(
    adjoint_final,
    diff_scale,
    vert_coupling,
    column_depth,
    seam_table,
    tile_owner,
    prof_face,
    prof_cell,
    prof_time,
    misfit,
):
    ids = jnp.stack([lax.axis_index("tile"), lax.axis_index("sub")]).astype(jnp.int32)
    rows = prof_face.shape[0]
    slots, meta = pack(
        ids,
        tile_owner,
        seam_table,
        prof_face.reshape(1, rows),
        prof_cell.reshape(1, rows),
        prof_time.reshape(1, rows),
        misfit.reshape(PLANES, rows),
    )
    slots = lax.all_to_all(slots, ("tile", "sub"), split_axis=0, concat_axis=0, tiled=True)
    adjoint = adjoint_final.reshape(PLANES * ROWS, COLS)
    scale = diff_scale.reshape(LEVELS * ROWS, COLS)
    coupling = vert_coupling.reshape((LEVELS - 1) * ROWS, COLS)
    late = forcing(slots, 1)
    solved, weighted, *edges = first_solve(meta, adjoint, late, coupling, scale, column_depth)
    early = forcing(slots, 0)
    halos = exchange(meta, *edges)
    solved, weighted, *edges = second_solve(
        meta, halos, solved, weighted, early, coupling, scale, column_depth
    )
    halos = exchange(meta, *edges)
    out = last_step(meta, halos, solved, weighted, scale, column_depth)
    return out.reshape(adjoint_final.shape)


def solution(mesh):
    return jax.shard_map(
        body,
        mesh=mesh,
        in_specs=(
            P(None, None, ("tile", "sub"), None),
            P(None, ("tile", "sub"), None),
            P(None, ("tile", "sub"), None),
            P(("tile", "sub"), None),
            P(),
            P(),
            P(("tile", "sub")),
            P(("tile", "sub")),
            P(("tile", "sub")),
            P(None, None, ("tile", "sub")),
        ),
        out_specs=P(None, None, ("tile", "sub"), None),
        check_vma=False,
    )
```

```python
import functools

import jax
import jax.numpy as jnp
from jax import lax
from jax.experimental import pallas as pl
from jax.experimental.pallas import tpu as pltpu
from jax.sharding import PartitionSpec as P

CAP = 4
LEVELS = 16
PLANES = 2 * LEVELS
ROWS = 64
COLS = 512
CELLS = ROWS * COLS
N_TILE = 16
N_SUB = 8
DEVICES = N_TILE * N_SUB
FACES = 16
explicit_rate = 0.2
HIGHEST = lax.Precision.HIGHEST
VMEM = pl.BlockSpec(memory_space=pltpu.VMEM)
SMEM = pl.BlockSpec(memory_space=pltpu.SMEM)
META = 16


def iota(shape, axis):
    return lax.broadcasted_iota(jnp.int32, shape, axis)


def params(mib):
    return pltpu.CompilerParams(vmem_limit_bytes=mib * 1024 * 1024)


def f32(*shape):
    return jax.ShapeDtypeStruct(shape, jnp.float32)


def pack_kernel(owner_in, seam_in, face_in, cell_in, time_in, misfit_in, out, meta, owner, seam,
                face, cell, time, misfit, sems):
    copies = [
        pltpu.make_async_copy(source, target, sems.at[i])
        for i, (source, target) in enumerate(
            (
                (owner_in, owner),
                (seam_in, seam),
                (face_in, face),
                (cell_in, cell),
                (time_in, time),
                (misfit_in, misfit),
            )
        )
    ]
    for copy in copies:
        copy.start()
    for copy in copies:
        copy.wait()
    tile = lax.axis_index("tile")
    sub = lax.axis_index("sub")
    my_face = jnp.int32(0)
    for f in range(FACES):
        my_face = my_face + jnp.where(owner[f] == tile, f, 0)
    meta[12] = tile
    meta[13] = sub
    for edge in range(4):
        other = owner[seam[0, edge, my_face]]
        away = (
            ((other & 1) ^ (tile & 1)) * 8
            + (((other >> 3) & 1) ^ ((tile >> 3) & 1)) * 4
            + ((((tile >> 1) & 3) + 4 - ((other >> 1) & 3)) & 3)
        )
        meta[3 * edge] = away
        meta[3 * edge + 1] = seam[1, edge, my_face]
        meta[3 * edge + 2] = seam[2, edge, my_face]

    rows = face.shape[1]
    faces = face[...]
    home = jnp.zeros_like(faces)
    for f in range(FACES):
        home = jnp.where(faces == f, owner[f], home)
    cells = cell[...]
    tile_row = cells >> 9
    target = home * N_SUB + (tile_row >> 6)
    code = (time[...] - 1) * CELLS + (tile_row & (ROWS - 1)) * COLS + (cells & (COLS - 1))
    first = iota((rows, rows), 0)
    second = iota((rows, rows), 1)
    target_row = jnp.broadcast_to(target.astype(jnp.float32), (rows, rows))
    target_col = jnp.sum(jnp.where(first == second, target_row, 0.0), axis=1, keepdims=True)
    rank = jnp.sum(
        jnp.where((target_col == target_row) & (first < second), 1.0, 0.0), axis=0, keepdims=True
    )
    rank = rank.astype(jnp.int32)
    values = misfit[...]
    tag = code.astype(jnp.float32) + 1.0
    dest = iota((DEVICES, rows), 0)
    total = jnp.zeros((DEVICES, 2 * DEVICES), jnp.float32)
    for k in range(CAP):
        hit = jnp.where((dest == target) & (rank == k), 1.0, 0.0)
        pieces = []
        if k > 0:
            pieces.append(jnp.zeros((PLANES * k, rows), jnp.float32))
        pieces.append(values)
        if k < CAP - 1:
            pieces.append(jnp.zeros((PLANES * (CAP - 1 - k), rows), jnp.float32))
        pieces.append(jnp.where(dest == k, tag, 0.0))
        stacked = jnp.concatenate(pieces, axis=0)
        total = total + lax.dot_general(
            hit, stacked, (((1,), (1,)), ((), ())), precision=HIGHEST,
            preferred_element_type=jnp.float32,
        )
    out[:, 0, :] = total[:, :DEVICES]
    out[:, 1, :] = total[:, DEVICES:] - 1.0


def pack(owner, seam, face, cell, time, misfit):
    rows = face.shape[1]
    line = pltpu.VMEM((1, rows), jnp.int32)
    return pl.pallas_call(
        pack_kernel,
        out_shape=(f32(DEVICES, 2, DEVICES), jax.ShapeDtypeStruct((META,), jnp.int32)),
        in_specs=[pl.BlockSpec(memory_space=pltpu.HBM)] * 6,
        out_specs=(VMEM, SMEM),
        scratch_shapes=[
            pltpu.SMEM(owner.shape, jnp.int32),
            pltpu.SMEM(seam.shape, jnp.int32),
            line,
            line,
            line,
            pltpu.VMEM(misfit.shape, jnp.float32),
            pltpu.SemaphoreType.DMA((6,)),
        ],
        compiler_params=params(8),
        name="pack",
    )(owner, seam, face, cell, time, misfit)


def forcing_kernel(moment, slots, out, parts, place):
    values = jnp.transpose(slots[:, 0, :])
    tags = (slots[:, 1, :] + 0.5).astype(jnp.int32)
    tags = jnp.where(slots[:, 1, :] < 0.0, -1, tags)
    tags_t = jnp.transpose(tags.astype(jnp.float32)).astype(jnp.int32)
    tag_row = jnp.concatenate([tags_t[k : k + 1, :] for k in range(CAP)], axis=1)
    valid = (tag_row >= moment * CELLS) & (tag_row < (moment + 1) * CELLS)
    row_of = jnp.where(valid, (tag_row & (CELLS - 1)) >> 9, -1)
    on_row = iota((ROWS, CAP * DEVICES), 0) == row_of
    wide = jnp.concatenate([values[PLANES * k : PLANES * (k + 1), :] for k in range(CAP)], axis=1)
    high = wide.astype(jnp.bfloat16).astype(jnp.float32)
    rest = wide - high
    middle = rest.astype(jnp.bfloat16).astype(jnp.float32)
    parts[0] = high
    parts[1] = middle
    parts[2] = rest - middle
    for k in range(CAP):
        col = tags[:, k : k + 1] & (COLS - 1)
        place[k * DEVICES : (k + 1) * DEVICES, :] = jnp.where(
            iota((DEVICES, COLS), 1) == col, 1.0, 0.0
        ).astype(jnp.bfloat16)
    group = 4

    def step(g, carry):
        total = None
        for part in range(3):
            left = []
            for q in range(group):
                row = parts[part, pl.ds(g * group + q, 1), :]
                left.append(jnp.where(on_row, row, 0.0).astype(jnp.bfloat16))
            got = jnp.dot(
                jnp.concatenate(left, axis=0), place[...], preferred_element_type=jnp.float32
            )
            total = got if total is None else total + got
        out[pl.ds(pl.multiple_of(g * group * ROWS, 8), group * ROWS), :] = total
        return carry

    lax.fori_loop(0, PLANES // group, step, 0)


def forcing(slots, moment):
    return pl.pallas_call(
        functools.partial(forcing_kernel, moment),
        out_shape=f32(PLANES * ROWS, COLS),
        in_specs=[VMEM],
        out_specs=VMEM,
        scratch_shapes=[
            pltpu.VMEM((3, PLANES, CAP * DEVICES), jnp.float32),
            pltpu.VMEM((CAP * DEVICES, COLS), jnp.bfloat16),
        ],
        compiler_params=params(8),
        cost_estimate=pl.CostEstimate(flops=3221225472, bytes_accessed=4325376, transcendentals=0),
        name=f"forcing_{moment}",
    )(slots)


QUARTER = PLANES * ROWS


def tile_rows(quarter, plane, block):
    return pl.ds(pl.multiple_of(quarter * QUARTER + plane * ROWS + block * 8, 8), 8)


PITCH = ROWS + 16


def wide_rows(quarter, plane, block, shift=0):
    start = (quarter * PLANES + plane) * PITCH + 8
    if shift:
        return pl.ds(start + shift + block * 8, 8)
    return pl.ds(pl.multiple_of(start + block * 8, 8), 8)


def eliminate(value, coupling, depth, at):
    links = []
    for k in range(LEVELS - 1):
        links.append(jnp.where(k + 1 < depth, coupling[at(k)], 0.0))
    ratio = []
    partial = [[], []]
    for k in range(LEVELS):
        pivot = jnp.float32(1.0)
        if k > 0:
            pivot = pivot + links[k - 1]
        if k < LEVELS - 1:
            pivot = pivot + links[k]
        if k > 0:
            pivot = pivot - links[k - 1] * ratio[k - 1]
        inverse = 1.0 / pivot
        for tracer in range(2):
            right = value(tracer * LEVELS + k)
            if k > 0:
                right = right + links[k - 1] * partial[tracer][k - 1]
            partial[tracer].append(right * inverse)
        if k < LEVELS - 1:
            ratio.append(links[k] * inverse)
    for k in range(LEVELS - 2, -1, -1):
        for tracer in range(2):
            partial[tracer][k] = partial[tracer][k] + ratio[k] * partial[tracer][k + 1]
    return partial


def solve_tile(value, coupling, scale, depth_ref, solved, weighted, sides, block, quarter):
    columns = slice(quarter * 128, (quarter + 1) * 128)

    def at(plane):
        return (pl.ds(pl.multiple_of(plane * ROWS + block * 8, 8), 8), columns)

    depth = depth_ref[pl.ds(pl.multiple_of(block * 8, 8), 8), columns]
    result = eliminate(value, coupling, depth, at)
    lane = iota((8, 128), 1)
    column = jnp.zeros((8, 128), jnp.float32)
    for k in range(LEVELS):
        weight = jnp.where(k < depth, scale[at(k)], 0.0)
        for tracer in range(2):
            plane = tracer * LEVELS + k
            found = result[tracer][k]
            heavy = weight * found
            solved[tile_rows(quarter, plane, block), :] = found
            weighted[wide_rows(quarter, plane, block), :] = heavy
            if quarter == 0:
                moved = heavy if plane == 0 else pltpu.roll(heavy, plane, 1)
                column = jnp.where(lane == plane, moved, column)
            if quarter == 3:
                column = jnp.where(lane == plane, pltpu.roll(heavy, plane + 1, 1), column)
    if quarter == 0:
        sides[pl.ds(pl.multiple_of(block * 8, 8), 8), :] = column
    if quarter == 3:
        sides[pl.ds(pl.multiple_of(ROWS + block * 8, 8), 8), :] = column


def send_edges(meta, weighted, sides, payload, first_row, last_row):
    sub = meta[13]
    payload[0] = jnp.transpose(sides[...])[:PLANES, :]
    for b in range(4):
        top = weighted[pl.ds(b * PLANES * PITCH + 8, PLANES, stride=PITCH), :]
        bottom = weighted[pl.ds(b * PLANES * PITCH + ROWS + 7, PLANES, stride=PITCH), :]
        payload[1 + b] = jnp.where(sub == N_SUB - 1, bottom, top)
        first_row[b] = top
        last_row[b] = bottom


BIG = (f32(4 * QUARTER, 128), f32(4 * PLANES * PITCH, 128))
EDGES = (f32(5, PLANES, 128), f32(4, PLANES, 128), f32(4, PLANES, 128))


def first_kernel(meta, adjoint, force, coupling, scale, depth, solved, weighted, payload,
                 first_row, last_row, sides):
    def step(block, carry):
        for quarter in range(4):
            columns = slice(quarter * 128, (quarter + 1) * 128)

            def value(plane):
                at = (pl.ds(pl.multiple_of(plane * ROWS + block * 8, 8), 8), columns)
                return adjoint[at] + force[at]

            solve_tile(value, coupling, scale, depth, solved, weighted, sides, block, quarter)
        return carry

    lax.fori_loop(0, ROWS // 8, step, 0)
    send_edges(meta, weighted, sides, payload, first_row, last_row)


def first_solve(meta, adjoint, force, coupling, scale, depth):
    return pl.pallas_call(
        first_kernel,
        out_shape=BIG + EDGES,
        in_specs=[SMEM] + [VMEM] * 5,
        out_specs=(VMEM,) * 5,
        scratch_shapes=[pltpu.VMEM((128, 128), jnp.float32)],
        compiler_params=params(8),
        cost_estimate=pl.CostEstimate(flops=30000000, bytes_accessed=20000000, transcendentals=0),
        name="first_solve",
    )(meta, adjoint, force, coupling, scale, depth)


def route_kernel(meta, gathered, send, here, across):
    sub = meta[13]
    lane = iota((PLANES, 128), 1)

    def half(edge, dest, wanted):
        place, other_edge, turned = meta[3 * edge], meta[3 * edge + 1], meta[3 * edge + 2]
        chunk = jnp.where(turned == 1, N_SUB - 1 - dest, dest)
        block = jnp.where(other_edge < 2, 1 + (chunk >> 1), 0)
        side = jnp.where(other_edge < 2, chunk & 1, other_edge - 2)
        found = gathered[place, block]
        return jnp.where(side == wanted, found, pltpu.roll(found, 64, 1))

    for dest in range(N_SUB):
        send[dest, 0] = jnp.where(lane < 64, half(2, dest, 0), half(3, dest, 1))
        send[dest, 1] = jnp.zeros((PLANES, 128), jnp.float32)
    for edge, dest in ((0, 0), (1, N_SUB - 1)):
        found = gathered[meta[3 * edge], 0]
        send[dest, 1] = jnp.where(
            meta[3 * edge + 1] == 2, found, pltpu.roll(found, 64, 1)
        )
    own = jnp.where(sub == N_SUB - 1, 1, 0)
    place_here = meta[3 * own]
    place_across = meta[3 * (1 - own)]
    for b in range(4):
        here[b] = gathered[place_here, 1 + b]
        across[b] = gathered[place_across, 1 + b]


def route(meta, gathered):
    return pl.pallas_call(
        route_kernel,
        out_shape=(f32(N_SUB, 2, PLANES, 128), f32(4, PLANES, 128), f32(4, PLANES, 128)),
        in_specs=[SMEM, VMEM],
        out_specs=(VMEM,) * 3,
        compiler_params=params(8),
        cost_estimate=pl.CostEstimate(flops=1000000, bytes_accessed=1000000, transcendentals=0),
        name="route",
    )(meta, gathered)


def exchange(meta, payload, first_row, last_row, beside=None):
    def turn(k):
        return [
            (y * 8 + z * 2 + c, y * 8 + ((z + k) % 4) * 2 + c)
            for y in range(2)
            for z in range(4)
            for c in range(2)
        ]

    all_parts = payload[None]
    all_parts = jnp.concatenate(
        [all_parts] + [lax.ppermute(all_parts, "tile", turn(k)) for k in (1, 2, 3)], axis=0
    )
    all_parts, first_row, last_row = lax.optimization_barrier((all_parts, first_row, last_row))
    extra = () if beside is None else (beside(),)
    above = lax.ppermute(last_row, "sub", [(i, i + 1) for i in range(N_SUB - 1)])
    below = lax.ppermute(first_row, "sub", [(i + 1, i) for i in range(N_SUB - 1)])
    all_parts = jnp.concatenate(
        [all_parts, lax.ppermute(all_parts, "tile", [(i, i ^ 8) for i in range(N_TILE)])], axis=0
    )
    all_parts, above, below, *extra = lax.optimization_barrier((all_parts, above, below, *extra))
    all_parts = jnp.concatenate(
        [all_parts, lax.ppermute(all_parts, "tile", [(i, i ^ 1) for i in range(N_TILE)])], axis=0
    )
    send, here, across = route(meta, all_parts)
    across = lax.ppermute(across, "sub", [(0, N_SUB - 1), (N_SUB - 1, 0)])
    send, across = lax.optimization_barrier((send, across))
    got = lax.all_to_all(send, "sub", split_axis=0, concat_axis=0, tiled=True)
    return (got, here, across, above, below), extra


def place_halo(meta, got, here, across, above, below, weighted, strips):
    sub = meta[13]
    lane = iota((PLANES, 128), 1)

    def source(edge):
        other_edge, turned = meta[3 * edge + 1], meta[3 * edge + 2]
        same = jnp.where(turned == 1, N_SUB - 1 - sub, sub)
        return jnp.where(other_edge == 0, 0, jnp.where(other_edge == 1, N_SUB - 1, same))

    sides = jnp.where(lane < 64, got[source(2), 0], got[source(3), 0])
    to = iota((128, 128), 0)
    of = iota((128, 128), 1)
    turned = jnp.where(to < 64, meta[8], meta[11])
    wanted = jnp.where(turned == 1, (to & 64) + 63 - (to & 63), to)
    pick = jnp.where(of == wanted, 1.0, 0.0)
    strips[:, :PLANES] = lax.dot_general(
        pick, sides, (((1,), (1,)), ((), ())), precision=HIGHEST, preferred_element_type=jnp.float32
    )

    own = jnp.where(sub == N_SUB - 1, 1, 0)
    other_edge, turned = meta[3 * own + 1], meta[3 * own + 2]
    flip = jnp.where(of == jnp.where(turned == 1, 127 - to, to), 1.0, 0.0)
    row = []
    for b in range(4):
        joined = jnp.where(lane < 64, got[2 * b, 1], pltpu.roll(got[2 * b + 1, 1], 64, 1))
        joined = jnp.where(other_edge < 2, across[b], joined)
        row.append(jnp.where(other_edge == own, here[b], joined))
    for b in range(4):
        ordered = jnp.where(turned == 1, row[3 - b], row[b])
        strip = jnp.dot(ordered, flip, precision=HIGHEST, preferred_element_type=jnp.float32)
        at = b * PLANES * PITCH
        above_row = jnp.where(sub == 0, strip, above[b])
        below_row = jnp.where(sub == N_SUB - 1, strip, below[b])
        weighted[pl.ds(at + 7, PLANES, stride=PITCH), :] = above_row
        weighted[pl.ds(at + ROWS + 8, PLANES, stride=PITCH), :] = below_row


def stepped(solved, weighted, scale, depth_ref, strips, block, quarter):
    columns = slice(quarter * 128, (quarter + 1) * 128)
    lane = iota((8, 128), 1)
    here = pl.ds(pl.multiple_of(block * 8, 8), 8)
    depth = depth_ref[here, columns]
    west = strips[here, :]
    east = strips[pl.ds(pl.multiple_of(ROWS + block * 8, 8), 8), :]
    weights = {}

    def value(plane):
        level = plane % LEVELS
        if level not in weights:
            at = pl.ds(pl.multiple_of(level * ROWS + block * 8, 8), 8)
            weights[level] = jnp.where(level < depth, scale[at, columns], 0.0) * explicit_rate
        center = weighted[wide_rows(quarter, plane, block), :]
        if quarter == 0:
            left = pltpu.roll(west, 127 - plane, 1)
        else:
            left = weighted[wide_rows(quarter - 1, plane, block), :]
        if quarter == 3:
            right = east if plane == 0 else pltpu.roll(east, 128 - plane, 1)
        else:
            right = weighted[wide_rows(quarter + 1, plane, block), :]
        total = weighted[wide_rows(quarter, plane, block, -1), :]
        total = total + weighted[wide_rows(quarter, plane, block, 1), :]
        total = total + pltpu.roll(jnp.where(lane == 127, left, center), 1, 1)
        total = total + pltpu.roll(jnp.where(lane == 0, right, center), 127, 1)
        return solved[tile_rows(quarter, plane, block), :] + weights[level] * (
            total - 4.0 * center
        )

    return value


def second_kernel(meta, got, here, across, above, below, solved_in, weighted_in, force, coupling,
                  scale, depth, solved, weighted, payload, first_row, last_row, weighted_late,
                  sides, strips):
    place_halo(meta, got, here, across, above, below, weighted_late, strips)

    def step(block, carry):
        for quarter in range(4):
            columns = slice(quarter * 128, (quarter + 1) * 128)
            late = stepped(solved_in, weighted_late, scale, depth, strips, block, quarter)

            def value(plane):
                at = (pl.ds(pl.multiple_of(plane * ROWS + block * 8, 8), 8), columns)
                return late(plane) + force[at]

            solve_tile(value, coupling, scale, depth, solved, weighted, sides, block, quarter)
        return carry

    lax.fori_loop(0, ROWS // 8, step, 0)
    send_edges(meta, weighted, sides, payload, first_row, last_row)


def second_solve(meta, halos, solved, weighted, force, coupling, scale, depth):
    return pl.pallas_call(
        second_kernel,
        out_shape=BIG + EDGES + BIG[1:],
        in_specs=[SMEM] + [VMEM] * 11,
        out_specs=(VMEM,) * 6,
        input_output_aliases={7: 5},
        scratch_shapes=[pltpu.VMEM((128, 128), jnp.float32)] * 2,
        compiler_params=params(8),
        cost_estimate=pl.CostEstimate(flops=50000000, bytes_accessed=30000000, transcendentals=0),
        name="second_solve",
    )(meta, *halos, solved, weighted, force, coupling, scale, depth)


def last_kernel(meta, got, here, across, above, below, solved, weighted_in, scale, depth, out,
                weighted, strips, ready, sems):
    place_halo(meta, got, here, across, above, below, weighted, strips)

    def copy(block):
        return pltpu.make_async_copy(
            ready.at[block],
            out.at[:, pl.ds(pl.multiple_of(block * 8, 8), 8), :],
            sems.at[block],
        )

    def step(block, carry):
        for quarter in range(4):
            columns = slice(quarter * 128, (quarter + 1) * 128)
            value = stepped(solved, weighted, scale, depth, strips, block, quarter)
            for level in range(LEVELS):
                for plane in (level, LEVELS + level):
                    ready[block, plane, :, columns] = value(plane)
        copy(block).start()
        return carry

    lax.fori_loop(0, ROWS // 8, step, 0)
    for block in range(ROWS // 8):
        copy(block).wait()


def last_step(meta, halos, solved, weighted, scale, depth):
    return pl.pallas_call(
        last_kernel,
        out_shape=(f32(PLANES, ROWS, COLS), BIG[1]),
        in_specs=[SMEM] + [VMEM] * 9,
        out_specs=(pl.BlockSpec(memory_space=pl.ANY), VMEM),
        input_output_aliases={7: 1},
        scratch_shapes=[
            pltpu.VMEM((128, 128), jnp.float32),
            pltpu.VMEM((ROWS // 8, PLANES, 8, COLS), jnp.float32),
            pltpu.SemaphoreType.DMA((ROWS // 8,)),
        ],
        compiler_params=params(8),
        cost_estimate=pl.CostEstimate(flops=20000000, bytes_accessed=20000000, transcendentals=0),
        name="last_step",
    )(meta, *halos, solved, weighted, scale, depth)[0]


def body(
    adjoint_final,
    diff_scale,
    vert_coupling,
    column_depth,
    seam_table,
    tile_owner,
    prof_face,
    prof_cell,
    prof_time,
    misfit,
):
    rows = prof_face.shape[0]
    slots, meta = pack(
        tile_owner,
        jnp.transpose(seam_table, (2, 1, 0)),
        prof_face.reshape(1, rows),
        prof_cell.reshape(1, rows),
        prof_time.reshape(1, rows),
        misfit.reshape(PLANES, rows),
    )
    slots = lax.all_to_all(slots, ("tile", "sub"), split_axis=0, concat_axis=0, tiled=True)
    adjoint = adjoint_final.reshape(PLANES * ROWS, COLS)
    scale = diff_scale.reshape(LEVELS * ROWS, COLS)
    coupling = vert_coupling.reshape((LEVELS - 1) * ROWS, COLS)
    late = forcing(slots, 1)
    solved, weighted, *edges = first_solve(meta, adjoint, late, coupling, scale, column_depth)
    halos, (early,) = exchange(meta, *edges, lambda: forcing(slots, 0))
    solved, weighted, *edges, _ = second_solve(
        meta, halos, solved, weighted, early, coupling, scale, column_depth
    )
    halos, _ = exchange(meta, *edges)
    out = last_step(meta, halos, solved, weighted, scale, column_depth)
    return out.reshape(adjoint_final.shape)


def solution(mesh):
    return jax.shard_map(
        body,
        mesh=mesh,
        in_specs=(
            P(None, None, ("tile", "sub"), None),
            P(None, ("tile", "sub"), None),
            P(None, ("tile", "sub"), None),
            P(("tile", "sub"), None),
            P(),
            P(),
            P(("tile", "sub")),
            P(("tile", "sub")),
            P(("tile", "sub")),
            P(None, None, ("tile", "sub")),
        ),
        out_specs=P(None, None, ("tile", "sub"), None),
        check_vma=False,
    )
```

```python
import functools

import jax
import jax.numpy as jnp
from jax import lax
from jax.experimental import pallas as pl
from jax.experimental.pallas import tpu as pltpu
from jax.sharding import PartitionSpec as P

CAP = 4
LEVELS = 16
PLANES = 2 * LEVELS
ROWS = 64
COLS = 512
CELLS = ROWS * COLS
N_TILE = 16
N_SUB = 8
DEVICES = N_TILE * N_SUB
FACES = 16
explicit_rate = 0.2
HIGHEST = lax.Precision.HIGHEST
VMEM = pl.BlockSpec(memory_space=pltpu.VMEM)
SMEM = pl.BlockSpec(memory_space=pltpu.SMEM)
META = 16
PARTS = 2


def iota(shape, axis):
    return lax.broadcasted_iota(jnp.int32, shape, axis)


def params(mib):
    return pltpu.CompilerParams(vmem_limit_bytes=mib * 1024 * 1024)


def f32(*shape):
    return jax.ShapeDtypeStruct(shape, jnp.float32)


def pack_kernel(seam_table, numbers, misfit, out, meta, small):
    def owner(f):
        return small[0, f]

    def seam(part, edge, f):
        return seam_table[part, edge, f]

    pltpu.sync_copy(numbers.at[pl.ds(3, 1), :], small)

    tile = lax.axis_index("tile")
    sub = lax.axis_index("sub")
    my_face = jnp.int32(0)
    for f in range(FACES):
        my_face = my_face + jnp.where(owner(f) == tile, f, 0)
    meta[12] = tile
    meta[13] = sub
    for edge in range(4):
        other = owner(seam(0, edge, my_face))
        away = (
            ((other & 1) ^ (tile & 1)) * 8
            + (((other >> 3) & 1) ^ ((tile >> 3) & 1)) * 4
            + ((((tile >> 1) & 3) + 4 - ((other >> 1) & 3)) & 3)
        )
        meta[3 * edge] = away
        meta[3 * edge + 1] = seam(1, edge, my_face)
        meta[3 * edge + 2] = seam(2, edge, my_face)

    rows = numbers.shape[1]
    faces = numbers[0:1, :]
    home = jnp.zeros_like(faces)
    for f in range(FACES):
        home = jnp.where(faces == f, owner(f), home)
    cells = numbers[1:2, :]
    tile_row = cells >> 9
    target = home * N_SUB + (tile_row >> 6)
    code = (numbers[2:3, :] - 1) * CELLS + (tile_row & (ROWS - 1)) * COLS + (cells & (COLS - 1))
    first = iota((rows, rows), 0)
    second = iota((rows, rows), 1)
    target_row = jnp.broadcast_to(target.astype(jnp.float32), (rows, rows))
    target_col = jnp.sum(jnp.where(first == second, target_row, 0.0), axis=1, keepdims=True)
    rank = jnp.sum(
        jnp.where((target_col == target_row) & (first < second), 1.0, 0.0), axis=0, keepdims=True
    )
    rank = rank.astype(jnp.int32)
    values = misfit[...]
    tag = code.astype(jnp.float32) + 1.0
    dest = iota((DEVICES, rows), 0)
    total = jnp.zeros((DEVICES, 2 * DEVICES), jnp.float32)
    for k in range(CAP):
        hit = jnp.where((dest == target) & (rank == k), 1.0, 0.0)
        pieces = []
        if k > 0:
            pieces.append(jnp.zeros((PLANES * k, rows), jnp.float32))
        pieces.append(values)
        if k < CAP - 1:
            pieces.append(jnp.zeros((PLANES * (CAP - 1 - k), rows), jnp.float32))
        pieces.append(jnp.where(dest == k, tag, 0.0))
        stacked = jnp.concatenate(pieces, axis=0)
        total = total + lax.dot_general(
            hit, stacked, (((1,), (1,)), ((), ())), precision=HIGHEST,
            preferred_element_type=jnp.float32,
        )
    out[:, 0, :] = total[:, :DEVICES]
    out[:, 1, :] = total[:, DEVICES:] - 1.0


def pack(seams, numbers, misfit):
    return pl.pallas_call(
        pack_kernel,
        out_shape=(f32(DEVICES, 2, DEVICES), jax.ShapeDtypeStruct((META,), jnp.int32)),
        in_specs=[SMEM, VMEM, VMEM],
        out_specs=(VMEM, SMEM),
        scratch_shapes=[pltpu.SMEM((1, numbers.shape[1]), jnp.int32)],
        compiler_params=params(8),
        name="pack",
    )(seams, numbers, misfit)


def forcing_kernel(moment, slots, out, parts, place):
    values = jnp.transpose(slots[:, 0, :])
    tags = (slots[:, 1, :] + 0.5).astype(jnp.int32)
    tags = jnp.where(slots[:, 1, :] < 0.0, -1, tags)
    tags_t = jnp.transpose(tags.astype(jnp.float32)).astype(jnp.int32)
    tag_row = jnp.concatenate([tags_t[k : k + 1, :] for k in range(CAP)], axis=1)
    valid = (tag_row >= moment * CELLS) & (tag_row < (moment + 1) * CELLS)
    row_of = jnp.where(valid, (tag_row & (CELLS - 1)) >> 9, -1)
    on_row = iota((ROWS, CAP * DEVICES), 0) == row_of
    wide = jnp.concatenate([values[PLANES * k : PLANES * (k + 1), :] for k in range(CAP)], axis=1)
    high = wide.astype(jnp.bfloat16).astype(jnp.float32)
    parts[0] = high
    parts[1] = wide - high
    for k in range(CAP):
        col = tags[:, k : k + 1] & (COLS - 1)
        place[k * DEVICES : (k + 1) * DEVICES, :] = jnp.where(
            iota((DEVICES, COLS), 1) == col, 1.0, 0.0
        ).astype(jnp.bfloat16)
    group = 4

    def step(g, carry):
        total = None
        for part in range(PARTS):
            left = []
            for q in range(group):
                row = parts[part, pl.ds(g * group + q, 1), :]
                left.append(jnp.where(on_row, row, 0.0).astype(jnp.bfloat16))
            got = jnp.dot(
                jnp.concatenate(left, axis=0), place[...], preferred_element_type=jnp.float32
            )
            total = got if total is None else total + got
        out[pl.ds(pl.multiple_of(g * group * ROWS, 8), group * ROWS), :] = total
        return carry

    lax.fori_loop(0, PLANES // group, step, 0)


def forcing(slots, moment):
    return pl.pallas_call(
        functools.partial(forcing_kernel, moment),
        out_shape=f32(PLANES * ROWS, COLS),
        in_specs=[VMEM],
        out_specs=VMEM,
        scratch_shapes=[
            pltpu.VMEM((PARTS, PLANES, CAP * DEVICES), jnp.float32),
            pltpu.VMEM((CAP * DEVICES, COLS), jnp.bfloat16),
        ],
        compiler_params=params(8),
        cost_estimate=pl.CostEstimate(flops=2147483648, bytes_accessed=4325376, transcendentals=0),
        name=f"forcing_{moment}",
    )(slots)


QUARTER = PLANES * ROWS


def tile_rows(quarter, plane, block):
    return pl.ds(pl.multiple_of(quarter * QUARTER + plane * ROWS + block * 8, 8), 8)


PITCH = ROWS + 16


def wide_rows(quarter, plane, block, shift=0):
    start = (quarter * PLANES + plane) * PITCH + 8
    if shift:
        return pl.ds(start + shift + block * 8, 8)
    return pl.ds(pl.multiple_of(start + block * 8, 8), 8)


def eliminate(value, coupling, depth, at):
    links = []
    for k in range(LEVELS - 1):
        links.append(jnp.where(k + 1 < depth, coupling[at(k)], 0.0))
    ratio = []
    partial = [[], []]
    for k in range(LEVELS):
        pivot = jnp.float32(1.0)
        if k > 0:
            pivot = pivot + links[k - 1]
        if k < LEVELS - 1:
            pivot = pivot + links[k]
        if k > 0:
            pivot = pivot - links[k - 1] * ratio[k - 1]
        inverse = 1.0 / pivot
        for tracer in range(2):
            right = value(tracer * LEVELS + k)
            if k > 0:
                right = right + links[k - 1] * partial[tracer][k - 1]
            partial[tracer].append(right * inverse)
        if k < LEVELS - 1:
            ratio.append(links[k] * inverse)
    for k in range(LEVELS - 2, -1, -1):
        for tracer in range(2):
            partial[tracer][k] = partial[tracer][k] + ratio[k] * partial[tracer][k + 1]
    return partial


def solve_tile(value, coupling, scale, depth_ref, solved, weighted, sides, block, quarter):
    columns = slice(quarter * 128, (quarter + 1) * 128)

    def at(plane):
        return (pl.ds(pl.multiple_of(plane * ROWS + block * 8, 8), 8), columns)

    depth = depth_ref[pl.ds(pl.multiple_of(block * 8, 8), 8), columns]
    result = eliminate(value, coupling, depth, at)
    lane = iota((8, 128), 1)
    column = jnp.zeros((8, 128), jnp.float32)
    for k in range(LEVELS):
        weight = jnp.where(k < depth, scale[at(k)], 0.0)
        for tracer in range(2):
            plane = tracer * LEVELS + k
            found = result[tracer][k]
            heavy = weight * found
            solved[tile_rows(quarter, plane, block), :] = found
            weighted[wide_rows(quarter, plane, block), :] = heavy
            if quarter == 0:
                moved = heavy if plane == 0 else pltpu.roll(heavy, plane, 1)
                column = jnp.where(lane == plane, moved, column)
            if quarter == 3:
                column = jnp.where(lane == plane, pltpu.roll(heavy, plane + 1, 1), column)
    if quarter == 0:
        sides[pl.ds(pl.multiple_of(block * 8, 8), 8), :] = column
    if quarter == 3:
        sides[pl.ds(pl.multiple_of(ROWS + block * 8, 8), 8), :] = column


def send_edges(meta, weighted, sides, payload, first_row, last_row):
    sub = meta[13]
    payload[0] = jnp.transpose(sides[...])[:PLANES, :]
    for b in range(4):
        top = weighted[pl.ds(b * PLANES * PITCH + 8, PLANES, stride=PITCH), :]
        bottom = weighted[pl.ds(b * PLANES * PITCH + ROWS + 7, PLANES, stride=PITCH), :]
        payload[1 + b] = jnp.where(sub == N_SUB - 1, bottom, top)
        first_row[b] = top
        last_row[b] = bottom


BIG = (f32(4 * QUARTER, 128), f32(4 * PLANES * PITCH, 128))
EDGES = (f32(5, PLANES, 128), f32(4, PLANES, 128), f32(4, PLANES, 128))


def first_kernel(meta, adjoint, force, coupling, scale, depth, solved, weighted, payload,
                 first_row, last_row, sides):
    def step(block, carry):
        for quarter in range(4):
            columns = slice(quarter * 128, (quarter + 1) * 128)

            def value(plane):
                at = (pl.ds(pl.multiple_of(plane * ROWS + block * 8, 8), 8), columns)
                return adjoint[at] + force[at]

            solve_tile(value, coupling, scale, depth, solved, weighted, sides, block, quarter)
        return carry

    lax.fori_loop(0, ROWS // 8, step, 0)
    send_edges(meta, weighted, sides, payload, first_row, last_row)


def first_solve(meta, adjoint, force, coupling, scale, depth):
    return pl.pallas_call(
        first_kernel,
        out_shape=BIG + EDGES,
        in_specs=[SMEM] + [VMEM] * 5,
        out_specs=(VMEM,) * 5,
        scratch_shapes=[pltpu.VMEM((128, 128), jnp.float32)],
        compiler_params=params(8),
        cost_estimate=pl.CostEstimate(flops=30000000, bytes_accessed=20000000, transcendentals=0),
        name="first_solve",
    )(meta, adjoint, force, coupling, scale, depth)


def route_kernel(meta, gathered, send, here, across):
    sub = meta[13]
    lane = iota((PLANES, 128), 1)

    def half(edge, dest, wanted):
        place, other_edge, turned = meta[3 * edge], meta[3 * edge + 1], meta[3 * edge + 2]
        chunk = jnp.where(turned == 1, N_SUB - 1 - dest, dest)
        block = jnp.where(other_edge < 2, 1 + (chunk >> 1), 0)
        side = jnp.where(other_edge < 2, chunk & 1, other_edge - 2)
        found = gathered[place, block]
        return jnp.where(side == wanted, found, pltpu.roll(found, 64, 1))

    for dest in range(N_SUB):
        send[dest, 0] = jnp.where(lane < 64, half(2, dest, 0), half(3, dest, 1))
        send[dest, 1] = jnp.zeros((PLANES, 128), jnp.float32)
    for edge, dest in ((0, 0), (1, N_SUB - 1)):
        found = gathered[meta[3 * edge], 0]
        send[dest, 1] = jnp.where(
            meta[3 * edge + 1] == 2, found, pltpu.roll(found, 64, 1)
        )
    own = jnp.where(sub == N_SUB - 1, 1, 0)
    place_here = meta[3 * own]
    place_across = meta[3 * (1 - own)]
    for b in range(4):
        here[b] = gathered[place_here, 1 + b]
        across[b] = gathered[place_across, 1 + b]


def route(meta, gathered):
    return pl.pallas_call(
        route_kernel,
        out_shape=(f32(N_SUB, 2, PLANES, 128), f32(4, PLANES, 128), f32(4, PLANES, 128)),
        in_specs=[SMEM, VMEM],
        out_specs=(VMEM,) * 3,
        compiler_params=params(8),
        cost_estimate=pl.CostEstimate(flops=1000000, bytes_accessed=1000000, transcendentals=0),
        name="route",
    )(meta, gathered)


def exchange(meta, payload, first_row, last_row, beside=None):
    def turn(k):
        return [
            (y * 8 + z * 2 + c, y * 8 + ((z + k) % 4) * 2 + c)
            for y in range(2)
            for z in range(4)
            for c in range(2)
        ]

    all_parts = payload[None]
    all_parts = jnp.concatenate(
        [all_parts] + [lax.ppermute(all_parts, "tile", turn(k)) for k in (1, 2, 3)], axis=0
    )
    all_parts, first_row, last_row = lax.optimization_barrier((all_parts, first_row, last_row))
    extra = () if beside is None else (beside(),)
    above = lax.ppermute(last_row, "sub", [(i, i + 1) for i in range(N_SUB - 1)])
    below = lax.ppermute(first_row, "sub", [(i + 1, i) for i in range(N_SUB - 1)])
    all_parts = jnp.concatenate(
        [all_parts, lax.ppermute(all_parts, "tile", [(i, i ^ 8) for i in range(N_TILE)])], axis=0
    )
    all_parts, above, below, *extra = lax.optimization_barrier((all_parts, above, below, *extra))
    all_parts = jnp.concatenate(
        [all_parts, lax.ppermute(all_parts, "tile", [(i, i ^ 1) for i in range(N_TILE)])], axis=0
    )
    send, here, across = route(meta, all_parts)
    across = lax.ppermute(across, "sub", [(0, N_SUB - 1), (N_SUB - 1, 0)])
    send, across = lax.optimization_barrier((send, across))
    got = lax.all_to_all(send, "sub", split_axis=0, concat_axis=0, tiled=True)
    return (got, here, across, above, below), extra


def place_halo(meta, got, here, across, above, below, weighted, strips):
    sub = meta[13]
    lane = iota((PLANES, 128), 1)

    def source(edge):
        other_edge, turned = meta[3 * edge + 1], meta[3 * edge + 2]
        same = jnp.where(turned == 1, N_SUB - 1 - sub, sub)
        return jnp.where(other_edge == 0, 0, jnp.where(other_edge == 1, N_SUB - 1, same))

    sides = jnp.where(lane < 64, got[source(2), 0], got[source(3), 0])
    to = iota((128, 128), 0)
    of = iota((128, 128), 1)
    turned = jnp.where(to < 64, meta[8], meta[11])
    wanted = jnp.where(turned == 1, (to & 64) + 63 - (to & 63), to)
    pick = jnp.where(of == wanted, 1.0, 0.0)
    strips[:, :PLANES] = lax.dot_general(
        pick, sides, (((1,), (1,)), ((), ())), precision=HIGHEST, preferred_element_type=jnp.float32
    )

    own = jnp.where(sub == N_SUB - 1, 1, 0)
    other_edge, turned = meta[3 * own + 1], meta[3 * own + 2]
    flip = jnp.where(of == jnp.where(turned == 1, 127 - to, to), 1.0, 0.0)
    row = []
    for b in range(4):
        joined = jnp.where(lane < 64, got[2 * b, 1], pltpu.roll(got[2 * b + 1, 1], 64, 1))
        joined = jnp.where(other_edge < 2, across[b], joined)
        row.append(jnp.where(other_edge == own, here[b], joined))
    for b in range(4):
        ordered = jnp.where(turned == 1, row[3 - b], row[b])
        strip = jnp.dot(ordered, flip, precision=HIGHEST, preferred_element_type=jnp.float32)
        at = b * PLANES * PITCH
        above_row = jnp.where(sub == 0, strip, above[b])
        below_row = jnp.where(sub == N_SUB - 1, strip, below[b])
        weighted[pl.ds(at + 7, PLANES, stride=PITCH), :] = above_row
        weighted[pl.ds(at + ROWS + 8, PLANES, stride=PITCH), :] = below_row


def stepped(solved, weighted, scale, depth_ref, strips, block, quarter):
    columns = slice(quarter * 128, (quarter + 1) * 128)
    lane = iota((8, 128), 1)
    here = pl.ds(pl.multiple_of(block * 8, 8), 8)
    depth = depth_ref[here, columns]
    west = strips[here, :]
    east = strips[pl.ds(pl.multiple_of(ROWS + block * 8, 8), 8), :]
    weights = {}

    def value(plane):
        level = plane % LEVELS
        if level not in weights:
            at = pl.ds(pl.multiple_of(level * ROWS + block * 8, 8), 8)
            weights[level] = jnp.where(level < depth, scale[at, columns], 0.0) * explicit_rate
        center = weighted[wide_rows(quarter, plane, block), :]
        total = weighted[wide_rows(quarter, plane, block, -1), :]
        total = total + weighted[wide_rows(quarter, plane, block, 1), :]
        if quarter == 0:
            edge = west if plane == 0 else pltpu.roll(west, 128 - plane, 1)
            total = total + jnp.where(lane == 0, edge, pltpu.roll(center, 1, 1))
        else:
            left = weighted[wide_rows(quarter - 1, plane, block), :]
            total = total + pltpu.roll(jnp.where(lane == 127, left, center), 1, 1)
        if quarter == 3:
            edge = pltpu.roll(east, 127 - plane, 1)
            total = total + jnp.where(lane == 127, edge, pltpu.roll(center, 127, 1))
        else:
            right = weighted[wide_rows(quarter + 1, plane, block), :]
            total = total + pltpu.roll(jnp.where(lane == 0, right, center), 127, 1)
        return solved[tile_rows(quarter, plane, block), :] + weights[level] * (
            total - 4.0 * center
        )

    return value


def second_kernel(meta, got, here, across, above, below, solved_in, weighted_in, force, coupling,
                  scale, depth, solved, weighted, payload, first_row, last_row, weighted_late,
                  sides, strips):
    place_halo(meta, got, here, across, above, below, weighted_late, strips)

    def step(block, carry):
        for quarter in range(4):
            columns = slice(quarter * 128, (quarter + 1) * 128)
            late = stepped(solved_in, weighted_late, scale, depth, strips, block, quarter)

            def value(plane):
                at = (pl.ds(pl.multiple_of(plane * ROWS + block * 8, 8), 8), columns)
                return late(plane) + force[at]

            solve_tile(value, coupling, scale, depth, solved, weighted, sides, block, quarter)
        return carry

    lax.fori_loop(0, ROWS // 8, step, 0)
    send_edges(meta, weighted, sides, payload, first_row, last_row)


def second_solve(meta, halos, solved, weighted, force, coupling, scale, depth):
    return pl.pallas_call(
        second_kernel,
        out_shape=BIG + EDGES + BIG[1:],
        in_specs=[SMEM] + [VMEM] * 11,
        out_specs=(VMEM,) * 6,
        input_output_aliases={7: 5},
        scratch_shapes=[pltpu.VMEM((128, 128), jnp.float32)] * 2,
        compiler_params=params(8),
        cost_estimate=pl.CostEstimate(flops=50000000, bytes_accessed=30000000, transcendentals=0),
        name="second_solve",
    )(meta, *halos, solved, weighted, force, coupling, scale, depth)


def last_kernel(meta, got, here, across, above, below, solved, weighted_in, scale, depth, out,
                weighted, strips, ready, sems):
    place_halo(meta, got, here, across, above, below, weighted, strips)

    def copy(block):
        return pltpu.make_async_copy(
            ready.at[block],
            out.at[:, pl.ds(pl.multiple_of(block * 8, 8), 8), :],
            sems.at[block],
        )

    def step(block, carry):
        for quarter in range(4):
            columns = slice(quarter * 128, (quarter + 1) * 128)
            value = stepped(solved, weighted, scale, depth, strips, block, quarter)
            for level in range(LEVELS):
                for plane in (level, LEVELS + level):
                    ready[block, plane, :, columns] = value(plane)
        copy(block).start()
        return carry

    lax.fori_loop(0, ROWS // 8, step, 0)
    for block in range(ROWS // 8):
        copy(block).wait()


def last_step(meta, halos, solved, weighted, scale, depth):
    return pl.pallas_call(
        last_kernel,
        out_shape=(f32(PLANES, ROWS, COLS), BIG[1]),
        in_specs=[SMEM] + [VMEM] * 9,
        out_specs=(pl.BlockSpec(memory_space=pl.ANY), VMEM),
        input_output_aliases={7: 1},
        scratch_shapes=[
            pltpu.VMEM((128, 128), jnp.float32),
            pltpu.VMEM((ROWS // 8, PLANES, 8, COLS), jnp.float32),
            pltpu.SemaphoreType.DMA((ROWS // 8,)),
        ],
        compiler_params=params(8),
        cost_estimate=pl.CostEstimate(flops=20000000, bytes_accessed=20000000, transcendentals=0),
        name="last_step",
    )(meta, *halos, solved, weighted, scale, depth)[0]


def body(
    adjoint_final,
    diff_scale,
    vert_coupling,
    column_depth,
    seam_table,
    tile_owner,
    prof_face,
    prof_cell,
    prof_time,
    misfit,
):
    rows = prof_face.shape[0]
    seams = jnp.transpose(seam_table, (2, 1, 0))
    owners = jnp.pad(tile_owner, (0, rows - tile_owner.shape[0]))
    numbers = jnp.stack([prof_face, prof_cell, prof_time, owners])
    slots, meta = pack(seams, numbers, misfit.reshape(PLANES, rows))
    slots = lax.all_to_all(slots, ("tile", "sub"), split_axis=0, concat_axis=0, tiled=True)
    adjoint = adjoint_final.reshape(PLANES * ROWS, COLS)
    scale = diff_scale.reshape(LEVELS * ROWS, COLS)
    coupling = vert_coupling.reshape((LEVELS - 1) * ROWS, COLS)
    late = forcing(slots, 1)
    solved, weighted, *edges = first_solve(meta, adjoint, late, coupling, scale, column_depth)
    halos, (early,) = exchange(meta, *edges, lambda: forcing(slots, 0))
    solved, weighted, *edges, _ = second_solve(
        meta, halos, solved, weighted, early, coupling, scale, column_depth
    )
    halos, _ = exchange(meta, *edges)
    out = last_step(meta, halos, solved, weighted, scale, column_depth)
    return out.reshape(adjoint_final.shape)


def solution(mesh):
    return jax.shard_map(
        body,
        mesh=mesh,
        in_specs=(
            P(None, None, ("tile", "sub"), None),
            P(None, ("tile", "sub"), None),
            P(None, ("tile", "sub"), None),
            P(("tile", "sub"), None),
            P(),
            P(),
            P(("tile", "sub")),
            P(("tile", "sub")),
            P(("tile", "sub")),
            P(None, None, ("tile", "sub")),
        ),
        out_specs=P(None, None, ("tile", "sub"), None),
        check_vma=False,
    )
```

```python
import functools

import jax
import jax.numpy as jnp
from jax import lax
from jax.experimental import pallas as pl
from jax.experimental.pallas import tpu as pltpu
from jax.sharding import PartitionSpec as P

CAP = 4
LEVELS = 16
PLANES = 2 * LEVELS
ROWS = 64
COLS = 512
CELLS = ROWS * COLS
N_TILE = 16
N_SUB = 8
DEVICES = N_TILE * N_SUB
FACES = 16
explicit_rate = 0.2
HIGHEST = lax.Precision.HIGHEST
VMEM = pl.BlockSpec(memory_space=pltpu.VMEM)
SMEM = pl.BlockSpec(memory_space=pltpu.SMEM)
META = 16
PARTS = 2


def iota(shape, axis):
    return lax.broadcasted_iota(jnp.int32, shape, axis)


def params(mib):
    return pltpu.CompilerParams(vmem_limit_bytes=mib * 1024 * 1024)


def f32(*shape):
    return jax.ShapeDtypeStruct(shape, jnp.float32)


def pack_kernel(owner_in, seam_in, face_in, cell_in, time_in, misfit_in, out, meta, owners, seams,
                face, cell, time, misfit, sems):
    copies = [
        pltpu.make_async_copy(source, target, sems.at[i])
        for i, (source, target) in enumerate(
            (
                (owner_in, owners),
                (seam_in, seams),
                (face_in, face),
                (cell_in, cell),
                (time_in, time),
                (misfit_in, misfit),
            )
        )
    ]
    for copy in copies:
        copy.start()
    for copy in copies:
        copy.wait()

    def owner(f):
        return owners[f]

    def seam(part, edge, f):
        return seams[part, edge, f]


    tile = lax.axis_index("tile")
    sub = lax.axis_index("sub")
    my_face = jnp.int32(0)
    for f in range(FACES):
        my_face = my_face + jnp.where(owner(f) == tile, f, 0)
    meta[12] = tile
    meta[13] = sub
    for edge in range(4):
        other = owner(seam(0, edge, my_face))
        away = (
            ((other & 1) ^ (tile & 1)) * 8
            + (((other >> 3) & 1) ^ ((tile >> 3) & 1)) * 4
            + ((((tile >> 1) & 3) + 4 - ((other >> 1) & 3)) & 3)
        )
        meta[3 * edge] = away
        meta[3 * edge + 1] = seam(1, edge, my_face)
        meta[3 * edge + 2] = seam(2, edge, my_face)

    rows = face.shape[1]
    faces = face[...]
    home = jnp.zeros_like(faces)
    for f in range(FACES):
        home = jnp.where(faces == f, owner(f), home)
    cells = cell[...]
    tile_row = cells >> 9
    target = home * N_SUB + (tile_row >> 6)
    code = (time[...] - 1) * CELLS + (tile_row & (ROWS - 1)) * COLS + (cells & (COLS - 1))
    first = iota((rows, rows), 0)
    second = iota((rows, rows), 1)
    target_row = jnp.broadcast_to(target.astype(jnp.float32), (rows, rows))
    target_col = jnp.sum(jnp.where(first == second, target_row, 0.0), axis=1, keepdims=True)
    rank = jnp.sum(
        jnp.where((target_col == target_row) & (first < second), 1.0, 0.0), axis=0, keepdims=True
    )
    rank = rank.astype(jnp.int32)
    values = misfit[...]
    tag = code.astype(jnp.float32) + 1.0
    dest = iota((DEVICES, rows), 0)
    total = jnp.zeros((DEVICES, 2 * DEVICES), jnp.float32)
    for k in range(CAP):
        hit = jnp.where((dest == target) & (rank == k), 1.0, 0.0)
        pieces = []
        if k > 0:
            pieces.append(jnp.zeros((PLANES * k, rows), jnp.float32))
        pieces.append(values)
        if k < CAP - 1:
            pieces.append(jnp.zeros((PLANES * (CAP - 1 - k), rows), jnp.float32))
        pieces.append(jnp.where(dest == k, tag, 0.0))
        stacked = jnp.concatenate(pieces, axis=0)
        total = total + lax.dot_general(
            hit, stacked, (((1,), (1,)), ((), ())), precision=HIGHEST,
            preferred_element_type=jnp.float32,
        )
    out[:, 0, :] = total[:, :DEVICES]
    out[:, 1, :] = total[:, DEVICES:] - 1.0


def pack(owner, seam, face, cell, time, misfit):
    line = pltpu.VMEM(face.shape, jnp.int32)
    return pl.pallas_call(
        pack_kernel,
        out_shape=(f32(DEVICES, 2, DEVICES), jax.ShapeDtypeStruct((META,), jnp.int32)),
        in_specs=[pl.BlockSpec(memory_space=pl.ANY)] * 6,
        out_specs=(VMEM, SMEM),
        scratch_shapes=[
            pltpu.SMEM(owner.shape, jnp.int32),
            pltpu.SMEM(seam.shape, jnp.int32),
            line,
            line,
            line,
            pltpu.VMEM(misfit.shape, jnp.float32),
            pltpu.SemaphoreType.DMA((6,)),
        ],
        compiler_params=pltpu.CompilerParams(vmem_limit_bytes=66000000),
        name="pack",
    )(owner, seam, face, cell, time, misfit)


def forcing_kernel(moment, slots, out, parts, place):
    values = jnp.transpose(slots[:, 0, :])
    tags = (slots[:, 1, :] + 0.5).astype(jnp.int32)
    tags = jnp.where(slots[:, 1, :] < 0.0, -1, tags)
    tags_t = jnp.transpose(tags.astype(jnp.float32)).astype(jnp.int32)
    tag_row = jnp.concatenate([tags_t[k : k + 1, :] for k in range(CAP)], axis=1)
    valid = (tag_row >= moment * CELLS) & (tag_row < (moment + 1) * CELLS)
    row_of = jnp.where(valid, (tag_row & (CELLS - 1)) >> 9, -1)
    on_row = iota((ROWS, CAP * DEVICES), 0) == row_of
    wide = jnp.concatenate([values[PLANES * k : PLANES * (k + 1), :] for k in range(CAP)], axis=1)
    high = wide.astype(jnp.bfloat16).astype(jnp.float32)
    parts[0] = high
    parts[1] = wide - high
    for k in range(CAP):
        col = tags[:, k : k + 1] & (COLS - 1)
        place[k * DEVICES : (k + 1) * DEVICES, :] = jnp.where(
            iota((DEVICES, COLS), 1) == col, 1.0, 0.0
        ).astype(jnp.bfloat16)
    group = 4

    def step(g, carry):
        total = None
        for part in range(PARTS):
            left = []
            for q in range(group):
                row = parts[part, pl.ds(g * group + q, 1), :]
                left.append(jnp.where(on_row, row, 0.0).astype(jnp.bfloat16))
            got = jnp.dot(
                jnp.concatenate(left, axis=0), place[...], preferred_element_type=jnp.float32
            )
            total = got if total is None else total + got
        out[pl.ds(pl.multiple_of(g * group * ROWS, 8), group * ROWS), :] = total
        return carry

    lax.fori_loop(0, PLANES // group, step, 0)


def forcing(slots, moment):
    return pl.pallas_call(
        functools.partial(forcing_kernel, moment),
        out_shape=f32(PLANES * ROWS, COLS),
        in_specs=[VMEM],
        out_specs=VMEM,
        scratch_shapes=[
            pltpu.VMEM((PARTS, PLANES, CAP * DEVICES), jnp.float32),
            pltpu.VMEM((CAP * DEVICES, COLS), jnp.bfloat16),
        ],
        compiler_params=params(8),
        cost_estimate=pl.CostEstimate(flops=2147483648, bytes_accessed=4325376, transcendentals=0),
        name=f"forcing_{moment}",
    )(slots)


QUARTER = PLANES * ROWS


def tile_rows(quarter, plane, block):
    return pl.ds(pl.multiple_of(quarter * QUARTER + plane * ROWS + block * 8, 8), 8)


PITCH = ROWS + 16


def wide_rows(quarter, plane, block, shift=0):
    start = (quarter * PLANES + plane) * PITCH + 8
    if shift:
        return pl.ds(start + shift + block * 8, 8)
    return pl.ds(pl.multiple_of(start + block * 8, 8), 8)


def eliminate(value, coupling, depth, at):
    links = []
    for k in range(LEVELS - 1):
        links.append(jnp.where(k + 1 < depth, coupling[at(k)], 0.0))
    ratio = []
    partial = [[], []]
    for k in range(LEVELS):
        pivot = jnp.float32(1.0)
        if k > 0:
            pivot = pivot + links[k - 1]
        if k < LEVELS - 1:
            pivot = pivot + links[k]
        if k > 0:
            pivot = pivot - links[k - 1] * ratio[k - 1]
        inverse = 1.0 / pivot
        for tracer in range(2):
            right = value(tracer * LEVELS + k)
            if k > 0:
                right = right + links[k - 1] * partial[tracer][k - 1]
            partial[tracer].append(right * inverse)
        if k < LEVELS - 1:
            ratio.append(links[k] * inverse)
    for k in range(LEVELS - 2, -1, -1):
        for tracer in range(2):
            partial[tracer][k] = partial[tracer][k] + ratio[k] * partial[tracer][k + 1]
    return partial


def solve_tile(value, coupling, scale, depth_ref, solved, weighted, sides, block, quarter):
    columns = slice(quarter * 128, (quarter + 1) * 128)

    def at(plane):
        return (pl.ds(pl.multiple_of(plane * ROWS + block * 8, 8), 8), columns)

    depth = depth_ref[pl.ds(pl.multiple_of(block * 8, 8), 8), columns]
    result = eliminate(value, coupling, depth, at)
    lane = iota((8, 128), 1)
    column = jnp.zeros((8, 128), jnp.float32)
    for k in range(LEVELS):
        weight = jnp.where(k < depth, scale[at(k)], 0.0)
        for tracer in range(2):
            plane = tracer * LEVELS + k
            found = result[tracer][k]
            heavy = weight * found
            solved[tile_rows(quarter, plane, block), :] = found
            weighted[wide_rows(quarter, plane, block), :] = heavy
            if quarter == 0:
                moved = heavy if plane == 0 else pltpu.roll(heavy, plane, 1)
                column = jnp.where(lane == plane, moved, column)
            if quarter == 3:
                column = jnp.where(lane == plane, pltpu.roll(heavy, plane + 1, 1), column)
    if quarter == 0:
        sides[pl.ds(pl.multiple_of(block * 8, 8), 8), :] = column
    if quarter == 3:
        sides[pl.ds(pl.multiple_of(ROWS + block * 8, 8), 8), :] = column


def send_edges(meta, weighted, sides, payload, first_row, last_row):
    sub = meta[13]
    payload[0] = jnp.transpose(sides[...])[:PLANES, :]
    for b in range(4):
        top = weighted[pl.ds(b * PLANES * PITCH + 8, PLANES, stride=PITCH), :]
        bottom = weighted[pl.ds(b * PLANES * PITCH + ROWS + 7, PLANES, stride=PITCH), :]
        payload[1 + b] = jnp.where(sub == N_SUB - 1, bottom, top)
        first_row[b] = top
        last_row[b] = bottom


BIG = (f32(4 * QUARTER, 128), f32(4 * PLANES * PITCH, 128))
EDGES = (f32(5, PLANES, 128), f32(4, PLANES, 128), f32(4, PLANES, 128))


def first_kernel(meta, adjoint, force, coupling, scale, depth, solved, weighted, payload,
                 first_row, last_row, sides):
    def step(block, carry):
        for quarter in range(4):
            columns = slice(quarter * 128, (quarter + 1) * 128)

            def value(plane):
                at = (pl.ds(pl.multiple_of(plane * ROWS + block * 8, 8), 8), columns)
                return adjoint[at] + force[at]

            solve_tile(value, coupling, scale, depth, solved, weighted, sides, block, quarter)
        return carry

    lax.fori_loop(0, ROWS // 8, step, 0)
    send_edges(meta, weighted, sides, payload, first_row, last_row)


def first_solve(meta, adjoint, force, coupling, scale, depth):
    return pl.pallas_call(
        first_kernel,
        out_shape=BIG + EDGES,
        in_specs=[SMEM] + [VMEM] * 5,
        out_specs=(VMEM,) * 5,
        scratch_shapes=[pltpu.VMEM((128, 128), jnp.float32)],
        compiler_params=params(8),
        cost_estimate=pl.CostEstimate(flops=30000000, bytes_accessed=20000000, transcendentals=0),
        name="first_solve",
    )(meta, adjoint, force, coupling, scale, depth)


def route_kernel(meta, gathered, first_row, last_row, send, here):
    sub = meta[13]
    lane = iota((PLANES, 128), 1)

    def half(edge, dest, wanted):
        place, other_edge, turned = meta[3 * edge], meta[3 * edge + 1], meta[3 * edge + 2]
        chunk = jnp.where(turned == 1, N_SUB - 1 - dest, dest)
        block = jnp.where(other_edge < 2, 1 + (chunk >> 1), 0)
        side = jnp.where(other_edge < 2, chunk & 1, other_edge - 2)
        found = gathered[place, block]
        return jnp.where(side == wanted, found, pltpu.roll(found, 64, 1))

    for dest in range(N_SUB):
        send[dest, 0] = jnp.where(lane < 64, half(2, dest, 0), half(3, dest, 1))
        send[dest, 1] = jnp.zeros((PLANES, 128), jnp.float32)
    for edge, dest in ((0, 0), (1, N_SUB - 1)):
        found = gathered[meta[3 * edge], 0]
        send[dest, 1] = jnp.where(
            meta[3 * edge + 1] == 2, found, pltpu.roll(found, 64, 1)
        )
    own = jnp.where(sub == N_SUB - 1, 1, 0)
    place_here = meta[3 * own]
    place_across = meta[3 * (1 - own)]
    for b in range(4):
        here[b] = gathered[place_here, 1 + b]
        across = gathered[place_across, 1 + b]
        first = first_row[b]
        last = last_row[b]
        for dest in range(N_SUB):
            if dest == 0:
                row = jnp.where(sub == N_SUB - 1, across, first)
            elif dest == N_SUB - 1:
                row = jnp.where(sub == 0, across, last)
            else:
                row = jnp.where(sub == dest - 1, last, first)
            send[dest, 2 + b] = row


def route(meta, gathered, first_row, last_row):
    return pl.pallas_call(
        route_kernel,
        out_shape=(f32(N_SUB, 6, PLANES, 128), f32(4, PLANES, 128)),
        in_specs=[SMEM] + [VMEM] * 3,
        out_specs=(VMEM,) * 2,
        compiler_params=params(8),
        cost_estimate=pl.CostEstimate(flops=1000000, bytes_accessed=1000000, transcendentals=0),
        name="route",
    )(meta, gathered, first_row, last_row)


def exchange(meta, payload, first_row, last_row, beside=None):
    def turn(k):
        return [
            (y * 8 + z * 2 + c, y * 8 + ((z + k) % 4) * 2 + c)
            for y in range(2)
            for z in range(4)
            for c in range(2)
        ]

    all_parts = payload[None]
    all_parts = jnp.concatenate(
        [all_parts] + [lax.ppermute(all_parts, "tile", turn(k)) for k in (1, 2, 3)], axis=0
    )
    all_parts = jnp.concatenate(
        [all_parts, lax.ppermute(all_parts, "tile", [(i, i ^ 8) for i in range(N_TILE)])], axis=0
    )
    extra = () if beside is None else (beside(),)
    all_parts, *extra = lax.optimization_barrier((all_parts, *extra))
    all_parts = jnp.concatenate(
        [all_parts, lax.ppermute(all_parts, "tile", [(i, i ^ 1) for i in range(N_TILE)])], axis=0
    )
    send, here = route(meta, all_parts, first_row, last_row)
    got = lax.all_to_all(send, "sub", split_axis=0, concat_axis=0, tiled=True)
    return (got, here), extra


def place_halo(meta, got, here, weighted, strips):
    sub = meta[13]
    before = jnp.maximum(sub - 1, 0)
    after = jnp.minimum(sub + 1, N_SUB - 1)
    opposite = jnp.where(sub == 0, N_SUB - 1, 0)
    lane = iota((PLANES, 128), 1)

    def source(edge):
        other_edge, turned = meta[3 * edge + 1], meta[3 * edge + 2]
        same = jnp.where(turned == 1, N_SUB - 1 - sub, sub)
        return jnp.where(other_edge == 0, 0, jnp.where(other_edge == 1, N_SUB - 1, same))

    sides = jnp.where(lane < 64, got[source(2), 0], got[source(3), 0])
    to = iota((128, 128), 0)
    of = iota((128, 128), 1)
    turned = jnp.where(to < 64, meta[8], meta[11])
    wanted = jnp.where(turned == 1, (to & 64) + 63 - (to & 63), to)
    pick = jnp.where(of == wanted, 1.0, 0.0)
    strips[:, :PLANES] = lax.dot_general(
        pick, sides, (((1,), (1,)), ((), ())), precision=HIGHEST, preferred_element_type=jnp.float32
    )

    own = jnp.where(sub == N_SUB - 1, 1, 0)
    other_edge, turned = meta[3 * own + 1], meta[3 * own + 2]
    flip = jnp.where(of == jnp.where(turned == 1, 127 - to, to), 1.0, 0.0)
    row = []
    for b in range(4):
        joined = jnp.where(lane < 64, got[2 * b, 1], pltpu.roll(got[2 * b + 1, 1], 64, 1))
        joined = jnp.where(other_edge < 2, got[opposite, 2 + b], joined)
        row.append(jnp.where(other_edge == own, here[b], joined))
    for b in range(4):
        ordered = jnp.where(turned == 1, row[3 - b], row[b])
        strip = jnp.dot(ordered, flip, precision=HIGHEST, preferred_element_type=jnp.float32)
        at = b * PLANES * PITCH
        above_row = jnp.where(sub == 0, strip, got[before, 2 + b])
        below_row = jnp.where(sub == N_SUB - 1, strip, got[after, 2 + b])
        weighted[pl.ds(at + 7, PLANES, stride=PITCH), :] = above_row
        weighted[pl.ds(at + ROWS + 8, PLANES, stride=PITCH), :] = below_row


def stepped(solved, weighted, scale, depth_ref, strips, block, quarter):
    columns = slice(quarter * 128, (quarter + 1) * 128)
    lane = iota((8, 128), 1)
    here = pl.ds(pl.multiple_of(block * 8, 8), 8)
    depth = depth_ref[here, columns]
    west = strips[here, :]
    east = strips[pl.ds(pl.multiple_of(ROWS + block * 8, 8), 8), :]
    weights = {}

    def value(plane):
        level = plane % LEVELS
        if level not in weights:
            at = pl.ds(pl.multiple_of(level * ROWS + block * 8, 8), 8)
            weights[level] = jnp.where(level < depth, scale[at, columns], 0.0) * explicit_rate
        center = weighted[wide_rows(quarter, plane, block), :]
        total = weighted[wide_rows(quarter, plane, block, -1), :]
        total = total + weighted[wide_rows(quarter, plane, block, 1), :]
        if quarter == 0:
            edge = west if plane == 0 else pltpu.roll(west, 128 - plane, 1)
            total = total + jnp.where(lane == 0, edge, pltpu.roll(center, 1, 1))
        else:
            left = weighted[wide_rows(quarter - 1, plane, block), :]
            total = total + pltpu.roll(jnp.where(lane == 127, left, center), 1, 1)
        if quarter == 3:
            edge = pltpu.roll(east, 127 - plane, 1)
            total = total + jnp.where(lane == 127, edge, pltpu.roll(center, 127, 1))
        else:
            right = weighted[wide_rows(quarter + 1, plane, block), :]
            total = total + pltpu.roll(jnp.where(lane == 0, right, center), 127, 1)
        return solved[tile_rows(quarter, plane, block), :] + weights[level] * (
            total - 4.0 * center
        )

    return value


def second_kernel(meta, got, here, solved_in, weighted_in, force, coupling,
                  scale, depth, solved, weighted, payload, first_row, last_row, weighted_late,
                  sides, strips):
    place_halo(meta, got, here, weighted_late, strips)

    def step(block, carry):
        for quarter in range(4):
            columns = slice(quarter * 128, (quarter + 1) * 128)
            late = stepped(solved_in, weighted_late, scale, depth, strips, block, quarter)

            def value(plane):
                at = (pl.ds(pl.multiple_of(plane * ROWS + block * 8, 8), 8), columns)
                return late(plane) + force[at]

            solve_tile(value, coupling, scale, depth, solved, weighted, sides, block, quarter)
        return carry

    lax.fori_loop(0, ROWS // 8, step, 0)
    send_edges(meta, weighted, sides, payload, first_row, last_row)


def second_solve(meta, halos, solved, weighted, force, coupling, scale, depth):
    return pl.pallas_call(
        second_kernel,
        out_shape=BIG + EDGES + BIG[1:],
        in_specs=[SMEM] + [VMEM] * 8,
        out_specs=(VMEM,) * 6,
        input_output_aliases={4: 5},
        scratch_shapes=[pltpu.VMEM((128, 128), jnp.float32)] * 2,
        compiler_params=params(8),
        cost_estimate=pl.CostEstimate(flops=50000000, bytes_accessed=30000000, transcendentals=0),
        name="second_solve",
    )(meta, *halos, solved, weighted, force, coupling, scale, depth)


def last_kernel(meta, got, here, solved, weighted_in, scale, depth, out,
                weighted, strips, ready, sems):
    place_halo(meta, got, here, weighted, strips)

    def copy(block):
        return pltpu.make_async_copy(
            ready.at[block],
            out.at[:, pl.ds(pl.multiple_of(block * 8, 8), 8), :],
            sems.at[block],
        )

    def step(block, carry):
        for quarter in range(4):
            columns = slice(quarter * 128, (quarter + 1) * 128)
            value = stepped(solved, weighted, scale, depth, strips, block, quarter)
            for level in range(LEVELS):
                for plane in (level, LEVELS + level):
                    ready[block, plane, :, columns] = value(plane)
        copy(block).start()
        return carry

    lax.fori_loop(0, ROWS // 8, step, 0)
    for block in range(ROWS // 8):
        copy(block).wait()


def last_step(meta, halos, solved, weighted, scale, depth):
    return pl.pallas_call(
        last_kernel,
        out_shape=(f32(PLANES, ROWS, COLS), BIG[1]),
        in_specs=[SMEM] + [VMEM] * 6,
        out_specs=(pl.BlockSpec(memory_space=pl.ANY), VMEM),
        input_output_aliases={4: 1},
        scratch_shapes=[
            pltpu.VMEM((128, 128), jnp.float32),
            pltpu.VMEM((ROWS // 8, PLANES, 8, COLS), jnp.float32),
            pltpu.SemaphoreType.DMA((ROWS // 8,)),
        ],
        compiler_params=params(8),
        cost_estimate=pl.CostEstimate(flops=20000000, bytes_accessed=20000000, transcendentals=0),
        name="last_step",
    )(meta, *halos, solved, weighted, scale, depth)[0]


def body(
    adjoint_final,
    diff_scale,
    vert_coupling,
    column_depth,
    seam_table,
    tile_owner,
    prof_face,
    prof_cell,
    prof_time,
    misfit,
):
    rows = prof_face.shape[0]
    slots, meta = pack(
        tile_owner,
        jnp.transpose(seam_table, (2, 1, 0)),
        prof_face.reshape(1, rows),
        prof_cell.reshape(1, rows),
        prof_time.reshape(1, rows),
        misfit.reshape(PLANES, rows),
    )
    slots = lax.all_to_all(slots, ("tile", "sub"), split_axis=0, concat_axis=0, tiled=True)
    adjoint = adjoint_final.reshape(PLANES * ROWS, COLS)
    scale = diff_scale.reshape(LEVELS * ROWS, COLS)
    coupling = vert_coupling.reshape((LEVELS - 1) * ROWS, COLS)
    late = forcing(slots, 1)
    solved, weighted, *edges = first_solve(meta, adjoint, late, coupling, scale, column_depth)
    halos, (early,) = exchange(meta, *edges, lambda: forcing(slots, 0))
    solved, weighted, *edges, _ = second_solve(
        meta, halos, solved, weighted, early, coupling, scale, column_depth
    )
    halos, _ = exchange(meta, *edges)
    out = last_step(meta, halos, solved, weighted, scale, column_depth)
    return out.reshape(adjoint_final.shape)


def solution(mesh):
    return jax.shard_map(
        body,
        mesh=mesh,
        in_specs=(
            P(None, None, ("tile", "sub"), None),
            P(None, ("tile", "sub"), None),
            P(None, ("tile", "sub"), None),
            P(("tile", "sub"), None),
            P(),
            P(),
            P(("tile", "sub")),
            P(("tile", "sub")),
            P(("tile", "sub")),
            P(None, None, ("tile", "sub")),
        ),
        out_specs=P(None, None, ("tile", "sub"), None),
        check_vma=False,
    )
```

```python
import functools

import jax
import jax.numpy as jnp
from jax import lax
from jax.experimental import pallas as pl
from jax.experimental.pallas import tpu as pltpu
from jax.sharding import PartitionSpec as P

CAP = 4
LEVELS = 16
PLANES = 2 * LEVELS
ROWS = 64
COLS = 512
CELLS = ROWS * COLS
N_TILE = 16
N_SUB = 8
DEVICES = N_TILE * N_SUB
FACES = 16
explicit_rate = 0.2
HIGHEST = lax.Precision.HIGHEST
VMEM = pl.BlockSpec(memory_space=pltpu.VMEM)
SMEM = pl.BlockSpec(memory_space=pltpu.SMEM)
META = 16
PARTS = 2


def iota(shape, axis):
    return lax.broadcasted_iota(jnp.int32, shape, axis)


def params(mib):
    return pltpu.CompilerParams(vmem_limit_bytes=mib * 1024 * 1024)


def f32(*shape):
    return jax.ShapeDtypeStruct(shape, jnp.float32)


def pack_kernel(owner_in, seam_in, face_in, cell_in, time_in, misfit_in, out, meta, owners, seams,
                face, cell, time, misfit, sems):
    copies = [
        pltpu.make_async_copy(source, target, sems.at[i])
        for i, (source, target) in enumerate(
            (
                (owner_in, owners),
                (seam_in, seams),
                (face_in, face),
                (cell_in, cell),
                (time_in, time),
                (misfit_in, misfit),
            )
        )
    ]
    for copy in copies:
        copy.start()
    for copy in copies:
        copy.wait()

    def owner(f):
        return owners[f]

    def seam(part, edge, f):
        return seams[part, edge, f]


    tile = lax.axis_index("tile")
    sub = lax.axis_index("sub")
    my_face = jnp.int32(0)
    for f in range(FACES):
        my_face = my_face + jnp.where(owner(f) == tile, f, 0)
    meta[12] = tile
    meta[13] = sub
    for edge in range(4):
        other = owner(seam(0, edge, my_face))
        away = (
            ((other & 1) ^ (tile & 1)) * 8
            + (((other >> 3) & 1) ^ ((tile >> 3) & 1)) * 4
            + ((((tile >> 1) & 3) + 4 - ((other >> 1) & 3)) & 3)
        )
        meta[3 * edge] = away
        meta[3 * edge + 1] = seam(1, edge, my_face)
        meta[3 * edge + 2] = seam(2, edge, my_face)

    rows = face.shape[1]
    faces = face[...]
    home = jnp.zeros_like(faces)
    for f in range(FACES):
        home = jnp.where(faces == f, owner(f), home)
    cells = cell[...]
    tile_row = cells >> 9
    target = home * N_SUB + (tile_row >> 6)
    code = (time[...] - 1) * CELLS + (tile_row & (ROWS - 1)) * COLS + (cells & (COLS - 1))
    first = iota((rows, rows), 0)
    second = iota((rows, rows), 1)
    target_row = jnp.broadcast_to(target.astype(jnp.float32), (rows, rows))
    target_col = jnp.sum(jnp.where(first == second, target_row, 0.0), axis=1, keepdims=True)
    rank = jnp.sum(
        jnp.where((target_col == target_row) & (first < second), 1.0, 0.0), axis=0, keepdims=True
    )
    rank = rank.astype(jnp.int32)
    values = misfit[...]
    tag = code.astype(jnp.float32) + 1.0
    dest = iota((DEVICES, rows), 0)
    total = jnp.zeros((DEVICES, 2 * DEVICES), jnp.float32)
    for k in range(CAP):
        hit = jnp.where((dest == target) & (rank == k), 1.0, 0.0)
        pieces = []
        if k > 0:
            pieces.append(jnp.zeros((PLANES * k, rows), jnp.float32))
        pieces.append(values)
        if k < CAP - 1:
            pieces.append(jnp.zeros((PLANES * (CAP - 1 - k), rows), jnp.float32))
        pieces.append(jnp.where(dest == k, tag, 0.0))
        stacked = jnp.concatenate(pieces, axis=0)
        total = total + lax.dot_general(
            hit, stacked, (((1,), (1,)), ((), ())), precision=HIGHEST,
            preferred_element_type=jnp.float32,
        )
    out[:, 0, :] = total[:, :DEVICES]
    out[:, 1, :] = total[:, DEVICES:] - 1.0


def pack(owner, seam, face, cell, time, misfit):
    line = pltpu.VMEM(face.shape, jnp.int32)
    return pl.pallas_call(
        pack_kernel,
        out_shape=(f32(DEVICES, 2, DEVICES), jax.ShapeDtypeStruct((META,), jnp.int32)),
        in_specs=[pl.BlockSpec(memory_space=pl.ANY)] * 6,
        out_specs=(VMEM, SMEM),
        scratch_shapes=[
            pltpu.SMEM(owner.shape, jnp.int32),
            pltpu.SMEM(seam.shape, jnp.int32),
            line,
            line,
            line,
            pltpu.VMEM(misfit.shape, jnp.float32),
            pltpu.SemaphoreType.DMA((6,)),
        ],
        compiler_params=pltpu.CompilerParams(vmem_limit_bytes=66000000),
        name="pack",
    )(owner, seam, face, cell, time, misfit)


def read_slots(moment, slots, parts, place):
    values = jnp.transpose(slots[:, 0, :])
    tags = (slots[:, 1, :] + 0.5).astype(jnp.int32)
    tags = jnp.where(slots[:, 1, :] < 0.0, -1, tags)
    tags_t = jnp.transpose(tags.astype(jnp.float32)).astype(jnp.int32)
    tag_row = jnp.concatenate([tags_t[k : k + 1, :] for k in range(CAP)], axis=1)
    valid = (tag_row >= moment * CELLS) & (tag_row < (moment + 1) * CELLS)
    wide = jnp.concatenate([values[PLANES * k : PLANES * (k + 1), :] for k in range(CAP)], axis=1)
    high = wide.astype(jnp.bfloat16).astype(jnp.float32)
    parts[0] = high
    parts[1] = wide - high
    for k in range(CAP):
        col = tags[:, k : k + 1] & (COLS - 1)
        place[k * DEVICES : (k + 1) * DEVICES, :] = jnp.where(
            iota((DEVICES, COLS), 1) == col, 1.0, 0.0
        ).astype(jnp.bfloat16)
    return jnp.where(valid, (tag_row & (CELLS - 1)) >> 9, -1)


def place_rows(on_row, planes, parts, place):
    total = None
    for part in range(PARTS):
        left = [jnp.where(on_row, parts[part, p, :], 0.0) for p in planes]
        got = jnp.dot(
            jnp.concatenate(left, axis=0).astype(jnp.bfloat16),
            place[...],
            preferred_element_type=jnp.float32,
        )
        total = got if total is None else total + got
    return total


def forcing_kernel(moment, slots, out, parts, place):
    row_of = read_slots(moment, slots, parts, place)
    on_row = iota((ROWS, CAP * DEVICES), 0) == row_of
    group = 4

    def step(g, carry):
        planes = [pl.ds(g * group + q, 1) for q in range(group)]
        rows = pl.ds(pl.multiple_of(g * group * ROWS, 8), group * ROWS)
        out[rows, :] = place_rows(on_row, planes, parts, place)
        return carry

    lax.fori_loop(0, PLANES // group, step, 0)


SLOT_SCRATCH = [
    pltpu.VMEM((PARTS, PLANES, CAP * DEVICES), jnp.float32),
    pltpu.VMEM((CAP * DEVICES, COLS), jnp.bfloat16),
]


def forcing(slots, moment):
    return pl.pallas_call(
        functools.partial(forcing_kernel, moment),
        out_shape=f32(PLANES * ROWS, COLS),
        in_specs=[VMEM],
        out_specs=VMEM,
        scratch_shapes=SLOT_SCRATCH,
        compiler_params=params(8),
        cost_estimate=pl.CostEstimate(flops=2147483648, bytes_accessed=4325376, transcendentals=0),
        name=f"forcing_{moment}",
    )(slots)


QUARTER = PLANES * ROWS


def tile_rows(quarter, plane, block):
    return pl.ds(pl.multiple_of(quarter * QUARTER + plane * ROWS + block * 8, 8), 8)


PITCH = ROWS + 16


def wide_rows(quarter, plane, block, shift=0):
    start = (quarter * PLANES + plane) * PITCH + 8
    if shift:
        return pl.ds(start + shift + block * 8, 8)
    return pl.ds(pl.multiple_of(start + block * 8, 8), 8)


def eliminate(value, coupling, depth, at):
    links = []
    for k in range(LEVELS - 1):
        links.append(jnp.where(k + 1 < depth, coupling[at(k)], 0.0))
    ratio = []
    partial = [[], []]
    for k in range(LEVELS):
        pivot = jnp.float32(1.0)
        if k > 0:
            pivot = pivot + links[k - 1]
        if k < LEVELS - 1:
            pivot = pivot + links[k]
        if k > 0:
            pivot = pivot - links[k - 1] * ratio[k - 1]
        inverse = 1.0 / pivot
        for tracer in range(2):
            right = value(tracer * LEVELS + k)
            if k > 0:
                right = right + links[k - 1] * partial[tracer][k - 1]
            partial[tracer].append(right * inverse)
        if k < LEVELS - 1:
            ratio.append(links[k] * inverse)
    for k in range(LEVELS - 2, -1, -1):
        for tracer in range(2):
            partial[tracer][k] = partial[tracer][k] + ratio[k] * partial[tracer][k + 1]
    return partial


def solve_tile(value, coupling, scale, depth_ref, solved, weighted, sides, block, quarter):
    columns = slice(quarter * 128, (quarter + 1) * 128)

    def at(level):
        return (level, pl.ds(pl.multiple_of(block * 8, 8), 8), columns)

    depth = depth_ref[pl.ds(pl.multiple_of(block * 8, 8), 8), columns]
    result = eliminate(value, coupling, depth, at)
    lane = iota((8, 128), 1)
    column = jnp.zeros((8, 128), jnp.float32)
    for k in range(LEVELS):
        weight = jnp.where(k < depth, scale[at(k)], 0.0)
        for tracer in range(2):
            plane = tracer * LEVELS + k
            found = result[tracer][k]
            heavy = weight * found
            solved[tile_rows(quarter, plane, block), :] = found
            weighted[wide_rows(quarter, plane, block), :] = heavy
            if quarter == 0:
                moved = heavy if plane == 0 else pltpu.roll(heavy, plane, 1)
                column = jnp.where(lane == plane, moved, column)
            if quarter == 3:
                column = jnp.where(lane == plane, pltpu.roll(heavy, plane + 1, 1), column)
    if quarter == 0:
        sides[pl.ds(pl.multiple_of(block * 8, 8), 8), :] = column
    if quarter == 3:
        sides[pl.ds(pl.multiple_of(ROWS + block * 8, 8), 8), :] = column


def send_edges(sub, weighted, sides, payload, first_row, last_row):
    payload[0] = jnp.transpose(sides[...])[:PLANES, :]
    for b in range(4):
        top = weighted[pl.ds(b * PLANES * PITCH + 8, PLANES, stride=PITCH), :]
        bottom = weighted[pl.ds(b * PLANES * PITCH + ROWS + 7, PLANES, stride=PITCH), :]
        payload[1 + b] = jnp.where(sub == N_SUB - 1, bottom, top)
        first_row[b] = top
        last_row[b] = bottom


BIG = (f32(4 * QUARTER, 128), f32(4 * PLANES * PITCH, 128))
EDGES = (f32(5, PLANES, 128), f32(4, PLANES, 128), f32(4, PLANES, 128))


def first_kernel(slots, adjoint_in, coupling_in, scale_in, depth_in, solved_out, weighted_out,
                 payload, first_row, last_row, solved, weighted, sides, parts, place, adjoint, coupling, scale, depth,
                 even, odd, sems, depth_sem, out_sems):
    blocks = ROWS // 8

    def results(block):
        rows = pl.ds(pl.multiple_of(block * 8, 8), 8)
        wide = pl.ds(pl.multiple_of(block * 8 + 8, 8), 8)
        whole = weighted.reshape(4 * PLANES, PITCH, 128)
        return [
            pltpu.make_async_copy(
                solved.reshape(4 * PLANES, ROWS, 128).at[:, rows, :],
                solved_out.at[:, rows, :],
                out_sems.at[0, block],
            ),
            pltpu.make_async_copy(
                whole.at[:, wide, :], weighted_out.at[:, wide, :], out_sems.at[1, block]
            ),
        ]

    def copies(block):
        rows = pl.ds(pl.multiple_of(block * 8, 8), 8)
        return [
            pltpu.make_async_copy(source.at[:, rows, :], target.at[:, rows, :], sems.at[i, block])
            for i, (source, target) in enumerate(
                ((adjoint_in, adjoint), (coupling_in, coupling), (scale_in, scale))
            )
        ]

    depth_copy = pltpu.make_async_copy(depth_in, depth, depth_sem)
    depth_copy.start()
    for block in range(blocks):
        for copy in copies(block):
            copy.start()
    row_of = read_slots(1, slots, parts, place)
    planes = [slice(p, p + 1) for p in range(PLANES)]

    def force(block, target):
        on_row = iota((8, CAP * DEVICES), 0) + block * 8 == row_of
        target[...] = place_rows(on_row, planes, parts, place)

    def solve(block, source):
        for quarter in range(4):
            columns = slice(quarter * 128, (quarter + 1) * 128)

            def value(plane):
                rows = pl.ds(pl.multiple_of(block * 8, 8), 8)
                return adjoint[plane, rows, columns] + source[plane * 8 : plane * 8 + 8, columns]

            solve_tile(value, coupling, scale, depth, solved, weighted, sides, block, quarter)
        for copy in results(block):
            copy.start()

    force(0, even)
    depth_copy.wait()

    def step(pair, carry):
        block = pair * 2
        for copy in copies(block) + copies(block + 1):
            copy.wait()
        force(block + 1, odd)
        solve(block, even)
        force(jnp.minimum(block + 2, blocks - 1), even)
        solve(block + 1, odd)
        return carry

    lax.fori_loop(0, blocks // 2, step, 0)
    send_edges(lax.axis_index("sub"), weighted, sides, payload, first_row, last_row)
    for block in range(blocks):
        for copy in results(block):
            copy.wait()


def first_solve(slots, adjoint, coupling, scale, depth):
    force = pltpu.VMEM((PLANES * 8, COLS), jnp.float32)
    plain = pl.BlockSpec(memory_space=pl.ANY)
    solved, weighted, *edges = pl.pallas_call(
        first_kernel,
        out_shape=(f32(4 * PLANES, ROWS, 128), f32(4 * PLANES, PITCH, 128)) + EDGES,
        in_specs=[VMEM] + [plain] * 4,
        out_specs=(plain, plain, VMEM, VMEM, VMEM),
        scratch_shapes=[
            pltpu.VMEM(BIG[0].shape, jnp.float32),
            pltpu.VMEM(BIG[1].shape, jnp.float32),
            pltpu.VMEM((128, 128), jnp.float32),
            *SLOT_SCRATCH,
            pltpu.VMEM(adjoint.shape, jnp.float32),
            pltpu.VMEM(coupling.shape, jnp.float32),
            pltpu.VMEM(scale.shape, jnp.float32),
            pltpu.VMEM(depth.shape, jnp.int32),
            force,
            force,
            pltpu.SemaphoreType.DMA((3, ROWS // 8)),
            pltpu.SemaphoreType.DMA,
            pltpu.SemaphoreType.DMA((2, ROWS // 8)),
        ],
        compiler_params=params(62),
        cost_estimate=pl.CostEstimate(
            flops=2200000000, bytes_accessed=20000000, transcendentals=0
        ),
        name="first_solve",
    )(slots, adjoint, coupling, scale, depth)
    return solved.reshape(BIG[0].shape), weighted.reshape(BIG[1].shape), *edges


def route_kernel(meta, gathered, first_row, last_row, send, here):
    sub = meta[13]
    lane = iota((PLANES, 128), 1)

    def half(edge, dest, wanted):
        place, other_edge, turned = meta[3 * edge], meta[3 * edge + 1], meta[3 * edge + 2]
        chunk = jnp.where(turned == 1, N_SUB - 1 - dest, dest)
        block = jnp.where(other_edge < 2, 1 + (chunk >> 1), 0)
        side = jnp.where(other_edge < 2, chunk & 1, other_edge - 2)
        found = gathered[place, block]
        return jnp.where(side == wanted, found, pltpu.roll(found, 64, 1))

    for dest in range(N_SUB):
        send[dest, 0] = jnp.where(lane < 64, half(2, dest, 0), half(3, dest, 1))
        send[dest, 1] = jnp.zeros((PLANES, 128), jnp.float32)
    for edge, dest in ((0, 0), (1, N_SUB - 1)):
        found = gathered[meta[3 * edge], 0]
        send[dest, 1] = jnp.where(
            meta[3 * edge + 1] == 2, found, pltpu.roll(found, 64, 1)
        )
    own = jnp.where(sub == N_SUB - 1, 1, 0)
    place_here = meta[3 * own]
    place_across = meta[3 * (1 - own)]
    for b in range(4):
        here[b] = gathered[place_here, 1 + b]
        across = gathered[place_across, 1 + b]
        first = first_row[b]
        last = last_row[b]
        for dest in range(N_SUB):
            if dest == 0:
                row = jnp.where(sub == N_SUB - 1, across, first)
            elif dest == N_SUB - 1:
                row = jnp.where(sub == 0, across, last)
            else:
                row = jnp.where(sub == dest - 1, last, first)
            send[dest, 2 + b] = row


def route(meta, gathered, first_row, last_row):
    return pl.pallas_call(
        route_kernel,
        out_shape=(f32(N_SUB, 6, PLANES, 128), f32(4, PLANES, 128)),
        in_specs=[SMEM] + [VMEM] * 3,
        out_specs=(VMEM,) * 2,
        compiler_params=params(8),
        cost_estimate=pl.CostEstimate(flops=1000000, bytes_accessed=1000000, transcendentals=0),
        name="route",
    )(meta, gathered, first_row, last_row)


def exchange(meta, payload, first_row, last_row, beside=None):
    def turn(k):
        return [
            (y * 8 + z * 2 + c, y * 8 + ((z + k) % 4) * 2 + c)
            for y in range(2)
            for z in range(4)
            for c in range(2)
        ]

    all_parts = payload[None]
    all_parts = jnp.concatenate(
        [all_parts] + [lax.ppermute(all_parts, "tile", turn(k)) for k in (1, 2, 3)], axis=0
    )
    across_y = [(i, i ^ 8) for i in range(N_TILE)]
    across_y_rows = [(i * N_SUB + s, j * N_SUB + s) for i, j in across_y for s in (0, N_SUB - 1)]
    others = jnp.concatenate(
        [
            lax.ppermute(all_parts[:, 1:], ("tile", "sub"), across_y_rows),
            lax.ppermute(all_parts[:, :1], "tile", across_y),
        ][::-1],
        axis=1,
    )
    all_parts = jnp.concatenate([all_parts, others], axis=0)
    extra = () if beside is None else (beside(),)
    all_parts, *extra = lax.optimization_barrier((all_parts, *extra))
    all_parts = jnp.concatenate(
        [all_parts, lax.ppermute(all_parts, "tile", [(i, i ^ 1) for i in range(N_TILE)])], axis=0
    )
    send, here = route(meta, all_parts, first_row, last_row)
    got = lax.all_to_all(send, "sub", split_axis=0, concat_axis=0, tiled=True)
    return (got, here), extra


def place_halo(meta, got, here, weighted, strips):
    sub = meta[13]
    before = jnp.maximum(sub - 1, 0)
    after = jnp.minimum(sub + 1, N_SUB - 1)
    opposite = jnp.where(sub == 0, N_SUB - 1, 0)
    lane = iota((PLANES, 128), 1)

    def source(edge):
        other_edge, turned = meta[3 * edge + 1], meta[3 * edge + 2]
        same = jnp.where(turned == 1, N_SUB - 1 - sub, sub)
        return jnp.where(other_edge == 0, 0, jnp.where(other_edge == 1, N_SUB - 1, same))

    sides = jnp.where(lane < 64, got[source(2), 0], got[source(3), 0])
    to = iota((128, 128), 0)
    of = iota((128, 128), 1)
    turned = jnp.where(to < 64, meta[8], meta[11])
    wanted = jnp.where(turned == 1, (to & 64) + 63 - (to & 63), to)
    pick = jnp.where(of == wanted, 1.0, 0.0)
    strips[:, :PLANES] = lax.dot_general(
        pick, sides, (((1,), (1,)), ((), ())), precision=HIGHEST, preferred_element_type=jnp.float32
    )

    own = jnp.where(sub == N_SUB - 1, 1, 0)
    other_edge, turned = meta[3 * own + 1], meta[3 * own + 2]
    flip = jnp.where(of == jnp.where(turned == 1, 127 - to, to), 1.0, 0.0)
    row = []
    for b in range(4):
        joined = jnp.where(lane < 64, got[2 * b, 1], pltpu.roll(got[2 * b + 1, 1], 64, 1))
        joined = jnp.where(other_edge < 2, got[opposite, 2 + b], joined)
        row.append(jnp.where(other_edge == own, here[b], joined))
    for b in range(4):
        ordered = jnp.where(turned == 1, row[3 - b], row[b])
        strip = jnp.dot(ordered, flip, precision=HIGHEST, preferred_element_type=jnp.float32)
        at = b * PLANES * PITCH
        above_row = jnp.where(sub == 0, strip, got[before, 2 + b])
        below_row = jnp.where(sub == N_SUB - 1, strip, got[after, 2 + b])
        weighted[pl.ds(at + 7, PLANES, stride=PITCH), :] = above_row
        weighted[pl.ds(at + ROWS + 8, PLANES, stride=PITCH), :] = below_row


def stepped(solved, weighted, scale, depth_ref, strips, block, quarter):
    columns = slice(quarter * 128, (quarter + 1) * 128)
    lane = iota((8, 128), 1)
    here = pl.ds(pl.multiple_of(block * 8, 8), 8)
    depth = depth_ref[here, columns]
    west = strips[here, :]
    east = strips[pl.ds(pl.multiple_of(ROWS + block * 8, 8), 8), :]
    weights = {}

    def value(plane):
        level = plane % LEVELS
        if level not in weights:
            weights[level] = jnp.where(level < depth, scale[level, here, columns], 0.0)
            weights[level] = weights[level] * explicit_rate
        center = weighted[wide_rows(quarter, plane, block), :]
        total = weighted[wide_rows(quarter, plane, block, -1), :]
        total = total + weighted[wide_rows(quarter, plane, block, 1), :]
        if quarter == 0:
            edge = west if plane == 0 else pltpu.roll(west, 128 - plane, 1)
            total = total + jnp.where(lane == 0, edge, pltpu.roll(center, 1, 1))
        else:
            left = weighted[wide_rows(quarter - 1, plane, block), :]
            total = total + pltpu.roll(jnp.where(lane == 127, left, center), 1, 1)
        if quarter == 3:
            edge = pltpu.roll(east, 127 - plane, 1)
            total = total + jnp.where(lane == 127, edge, pltpu.roll(center, 127, 1))
        else:
            right = weighted[wide_rows(quarter + 1, plane, block), :]
            total = total + pltpu.roll(jnp.where(lane == 0, right, center), 127, 1)
        return solved[tile_rows(quarter, plane, block), :] + weights[level] * (
            total - 4.0 * center
        )

    return value


def second_kernel(meta, got, here, solved_in, weighted_in, force, coupling,
                  scale, depth, solved, weighted, payload, first_row, last_row, weighted_late,
                  sides, strips):
    place_halo(meta, got, here, weighted_late, strips)

    def step(block, carry):
        for quarter in range(4):
            columns = slice(quarter * 128, (quarter + 1) * 128)
            late = stepped(solved_in, weighted_late, scale, depth, strips, block, quarter)

            def value(plane):
                at = (pl.ds(pl.multiple_of(plane * ROWS + block * 8, 8), 8), columns)
                return late(plane) + force[at]

            solve_tile(value, coupling, scale, depth, solved, weighted, sides, block, quarter)
        return carry

    lax.fori_loop(0, ROWS // 8, step, 0)
    send_edges(meta[13], weighted, sides, payload, first_row, last_row)


def second_solve(meta, halos, solved, weighted, force, coupling, scale, depth):
    return pl.pallas_call(
        second_kernel,
        out_shape=BIG + EDGES + BIG[1:],
        in_specs=[SMEM] + [VMEM] * 8,
        out_specs=(VMEM,) * 6,
        input_output_aliases={4: 5},
        scratch_shapes=[pltpu.VMEM((128, 128), jnp.float32)] * 2,
        compiler_params=params(8),
        cost_estimate=pl.CostEstimate(flops=50000000, bytes_accessed=30000000, transcendentals=0),
        name="second_solve",
    )(meta, *halos, solved, weighted, force, coupling, scale, depth)


def last_kernel(meta, got, here, solved, weighted_in, scale, depth, out,
                weighted, strips, ready, sems):
    place_halo(meta, got, here, weighted, strips)

    def copy(block):
        return pltpu.make_async_copy(
            ready.at[block],
            out.at[:, pl.ds(pl.multiple_of(block * 8, 8), 8), :],
            sems.at[block],
        )

    def step(block, carry):
        for quarter in range(4):
            columns = slice(quarter * 128, (quarter + 1) * 128)
            value = stepped(solved, weighted, scale, depth, strips, block, quarter)
            for level in range(LEVELS):
                for plane in (level, LEVELS + level):
                    ready[block, plane, :, columns] = value(plane)
        copy(block).start()
        return carry

    lax.fori_loop(0, ROWS // 8, step, 0)
    for block in range(ROWS // 8):
        copy(block).wait()


def last_step(meta, halos, solved, weighted, scale, depth):
    return pl.pallas_call(
        last_kernel,
        out_shape=(f32(PLANES, ROWS, COLS), BIG[1]),
        in_specs=[SMEM] + [VMEM] * 6,
        out_specs=(pl.BlockSpec(memory_space=pl.ANY), VMEM),
        input_output_aliases={4: 1},
        scratch_shapes=[
            pltpu.VMEM((128, 128), jnp.float32),
            pltpu.VMEM((ROWS // 8, PLANES, 8, COLS), jnp.float32),
            pltpu.SemaphoreType.DMA((ROWS // 8,)),
        ],
        compiler_params=params(8),
        cost_estimate=pl.CostEstimate(flops=20000000, bytes_accessed=20000000, transcendentals=0),
        name="last_step",
    )(meta, *halos, solved, weighted, scale, depth)[0]


def body(
    adjoint_final,
    diff_scale,
    vert_coupling,
    column_depth,
    seam_table,
    tile_owner,
    prof_face,
    prof_cell,
    prof_time,
    misfit,
):
    rows = prof_face.shape[0]
    slots, meta = pack(
        tile_owner,
        jnp.transpose(seam_table, (2, 1, 0)),
        prof_face.reshape(1, rows),
        prof_cell.reshape(1, rows),
        prof_time.reshape(1, rows),
        misfit.reshape(PLANES, rows),
    )
    slots = lax.all_to_all(slots, ("tile", "sub"), split_axis=0, concat_axis=0, tiled=True)
    adjoint = adjoint_final.reshape(PLANES, ROWS, COLS)
    scale, coupling = diff_scale, vert_coupling
    solved, weighted, *edges = first_solve(slots, adjoint, coupling, scale, column_depth)
    halos, (early,) = exchange(meta, *edges, lambda: forcing(slots, 0))
    solved, weighted, *edges, _ = second_solve(
        meta, halos, solved, weighted, early, coupling, scale, column_depth
    )
    halos, _ = exchange(meta, *edges)
    out = last_step(meta, halos, solved, weighted, scale, column_depth)
    return out.reshape(adjoint_final.shape)


def solution(mesh):
    return jax.shard_map(
        body,
        mesh=mesh,
        in_specs=(
            P(None, None, ("tile", "sub"), None),
            P(None, ("tile", "sub"), None),
            P(None, ("tile", "sub"), None),
            P(("tile", "sub"), None),
            P(),
            P(),
            P(("tile", "sub")),
            P(("tile", "sub")),
            P(("tile", "sub")),
            P(None, None, ("tile", "sub")),
        ),
        out_specs=P(None, None, ("tile", "sub"), None),
        check_vma=False,
    )
```

```python
import functools

import jax
import jax.numpy as jnp
from jax import lax
from jax.experimental import pallas as pl
from jax.experimental.pallas import tpu as pltpu
from jax.sharding import PartitionSpec as P

CAP = 4
LEVELS = 16
PLANES = 2 * LEVELS
ROWS = 64
COLS = 512
CELLS = ROWS * COLS
N_TILE = 16
N_SUB = 8
DEVICES = N_TILE * N_SUB
FACES = 16
explicit_rate = 0.2
HIGHEST = lax.Precision.HIGHEST
VMEM = pl.BlockSpec(memory_space=pltpu.VMEM)
SMEM = pl.BlockSpec(memory_space=pltpu.SMEM)
META = 16
PARTS = 2


def iota(shape, axis):
    return lax.broadcasted_iota(jnp.int32, shape, axis)


def params(mib):
    return pltpu.CompilerParams(vmem_limit_bytes=mib * 1024 * 1024)


def f32(*shape):
    return jax.ShapeDtypeStruct(shape, jnp.float32)


def pack_kernel(owner_in, seam_in, face_in, cell_in, time_in, misfit_in, out, meta, owners, seams,
                face, cell, time, misfit, sems):
    copies = [
        pltpu.make_async_copy(source, target, sems.at[i])
        for i, (source, target) in enumerate(
            (
                (owner_in, owners),
                (seam_in, seams),
                (face_in, face),
                (cell_in, cell),
                (time_in, time),
                (misfit_in, misfit),
            )
        )
    ]
    for copy in copies:
        copy.start()
    for copy in copies:
        copy.wait()

    def owner(f):
        return owners[f]

    def seam(part, edge, f):
        return seams[part, edge, f]


    tile = lax.axis_index("tile")
    sub = lax.axis_index("sub")
    my_face = jnp.int32(0)
    for f in range(FACES):
        my_face = my_face + jnp.where(owner(f) == tile, f, 0)
    meta[12] = tile
    meta[13] = sub
    for edge in range(4):
        other = owner(seam(0, edge, my_face))
        away = (
            ((other & 1) ^ (tile & 1)) * 8
            + (((other >> 3) & 1) ^ ((tile >> 3) & 1)) * 4
            + ((((tile >> 1) & 3) + 4 - ((other >> 1) & 3)) & 3)
        )
        meta[3 * edge] = away
        meta[3 * edge + 1] = seam(1, edge, my_face)
        meta[3 * edge + 2] = seam(2, edge, my_face)

    rows = face.shape[1]
    faces = face[...]
    home = jnp.zeros_like(faces)
    for f in range(FACES):
        home = jnp.where(faces == f, owner(f), home)
    cells = cell[...]
    tile_row = cells >> 9
    target = home * N_SUB + (tile_row >> 6)
    code = (time[...] - 1) * CELLS + (tile_row & (ROWS - 1)) * COLS + (cells & (COLS - 1))
    first = iota((rows, rows), 0)
    second = iota((rows, rows), 1)
    target_row = jnp.broadcast_to(target.astype(jnp.float32), (rows, rows))
    target_col = jnp.sum(jnp.where(first == second, target_row, 0.0), axis=1, keepdims=True)
    rank = jnp.sum(
        jnp.where((target_col == target_row) & (first < second), 1.0, 0.0), axis=0, keepdims=True
    )
    rank = rank.astype(jnp.int32)
    values = misfit[...]
    tag = code.astype(jnp.float32) + 1.0
    dest = iota((DEVICES, rows), 0)
    total = jnp.zeros((DEVICES, 2 * DEVICES), jnp.float32)
    for k in range(CAP):
        hit = jnp.where((dest == target) & (rank == k), 1.0, 0.0)
        pieces = []
        if k > 0:
            pieces.append(jnp.zeros((PLANES * k, rows), jnp.float32))
        pieces.append(values)
        if k < CAP - 1:
            pieces.append(jnp.zeros((PLANES * (CAP - 1 - k), rows), jnp.float32))
        pieces.append(jnp.where(dest == k, tag, 0.0))
        stacked = jnp.concatenate(pieces, axis=0)
        total = total + lax.dot_general(
            hit, stacked, (((1,), (1,)), ((), ())), precision=HIGHEST,
            preferred_element_type=jnp.float32,
        )
    out[:, 0, :] = total[:, :DEVICES]
    out[:, 1, :] = total[:, DEVICES:] - 1.0


def pack(owner, seam, face, cell, time, misfit):
    line = pltpu.VMEM(face.shape, jnp.int32)
    return pl.pallas_call(
        pack_kernel,
        out_shape=(f32(DEVICES, 2, DEVICES), jax.ShapeDtypeStruct((META,), jnp.int32)),
        in_specs=[pl.BlockSpec(memory_space=pl.ANY)] * 6,
        out_specs=(VMEM, SMEM),
        scratch_shapes=[
            pltpu.SMEM(owner.shape, jnp.int32),
            pltpu.SMEM(seam.shape, jnp.int32),
            line,
            line,
            line,
            pltpu.VMEM(misfit.shape, jnp.float32),
            pltpu.SemaphoreType.DMA((6,)),
        ],
        compiler_params=pltpu.CompilerParams(vmem_limit_bytes=66000000),
        name="pack",
    )(owner, seam, face, cell, time, misfit)


def forcing_kernel(moment, slots, out, parts, place):
    values = jnp.transpose(slots[:, 0, :])
    tags = (slots[:, 1, :] + 0.5).astype(jnp.int32)
    tags = jnp.where(slots[:, 1, :] < 0.0, -1, tags)
    tags_t = jnp.transpose(tags.astype(jnp.float32)).astype(jnp.int32)
    tag_row = jnp.concatenate([tags_t[k : k + 1, :] for k in range(CAP)], axis=1)
    valid = (tag_row >= moment * CELLS) & (tag_row < (moment + 1) * CELLS)
    row_of = jnp.where(valid, (tag_row & (CELLS - 1)) >> 9, -1)
    on_row = iota((ROWS, CAP * DEVICES), 0) == row_of
    wide = jnp.concatenate([values[PLANES * k : PLANES * (k + 1), :] for k in range(CAP)], axis=1)
    high = wide.astype(jnp.bfloat16).astype(jnp.float32)
    parts[0] = high
    parts[1] = wide - high
    for k in range(CAP):
        col = tags[:, k : k + 1] & (COLS - 1)
        place[k * DEVICES : (k + 1) * DEVICES, :] = jnp.where(
            iota((DEVICES, COLS), 1) == col, 1.0, 0.0
        ).astype(jnp.bfloat16)
    group = 4

    def step(g, carry):
        total = None
        for part in range(PARTS):
            left = []
            for q in range(group):
                row = parts[part, pl.ds(g * group + q, 1), :]
                left.append(jnp.where(on_row, row, 0.0).astype(jnp.bfloat16))
            got = jnp.dot(
                jnp.concatenate(left, axis=0), place[...], preferred_element_type=jnp.float32
            )
            total = got if total is None else total + got
        out[pl.ds(pl.multiple_of(g * group * ROWS, 8), group * ROWS), :] = total
        return carry

    lax.fori_loop(0, PLANES // group, step, 0)


def forcing(slots, moment):
    return pl.pallas_call(
        functools.partial(forcing_kernel, moment),
        out_shape=f32(PLANES * ROWS, COLS),
        in_specs=[VMEM],
        out_specs=VMEM,
        scratch_shapes=[
            pltpu.VMEM((PARTS, PLANES, CAP * DEVICES), jnp.float32),
            pltpu.VMEM((CAP * DEVICES, COLS), jnp.bfloat16),
        ],
        compiler_params=params(8),
        cost_estimate=pl.CostEstimate(flops=8000000000, bytes_accessed=4325376, transcendentals=0),
        name=f"forcing_{moment}",
    )(slots)


QUARTER = PLANES * ROWS


def tile_rows(quarter, plane, block):
    return pl.ds(pl.multiple_of(quarter * QUARTER + plane * ROWS + block * 8, 8), 8)


PITCH = ROWS + 16


def wide_rows(quarter, plane, block, shift=0):
    start = (quarter * PLANES + plane) * PITCH + 8
    if shift:
        return pl.ds(start + shift + block * 8, 8)
    return pl.ds(pl.multiple_of(start + block * 8, 8), 8)


def edge_tiles(tile):
    def sides(block, carry):
        tile(block, 0)
        tile(block, 3)
        return carry

    def ends(end, carry):
        tile(end * (ROWS // 8 - 1), 1)
        tile(end * (ROWS // 8 - 1), 2)
        return carry

    lax.fori_loop(0, ROWS // 8, sides, 0)
    lax.fori_loop(0, 2, ends, 0)


def inner_tiles(tile):
    def step(block, carry):
        tile(block, 1)
        tile(block, 2)
        return carry

    lax.fori_loop(1, ROWS // 8 - 1, step, 0)


def eliminate(value, coupling, depth, at):
    links = []
    for k in range(LEVELS - 1):
        links.append(jnp.where(k + 1 < depth, coupling[at(k)], 0.0))
    ratio = []
    partial = [[], []]
    for k in range(LEVELS):
        pivot = jnp.float32(1.0)
        if k > 0:
            pivot = pivot + links[k - 1]
        if k < LEVELS - 1:
            pivot = pivot + links[k]
        if k > 0:
            pivot = pivot - links[k - 1] * ratio[k - 1]
        inverse = 1.0 / pivot
        for tracer in range(2):
            right = value(tracer * LEVELS + k)
            if k > 0:
                right = right + links[k - 1] * partial[tracer][k - 1]
            partial[tracer].append(right * inverse)
        if k < LEVELS - 1:
            ratio.append(links[k] * inverse)
    for k in range(LEVELS - 2, -1, -1):
        for tracer in range(2):
            partial[tracer][k] = partial[tracer][k] + ratio[k] * partial[tracer][k + 1]
    return partial


def solve_tile(value, coupling, scale, depth_ref, solved, weighted, sides, block, quarter):
    columns = slice(quarter * 128, (quarter + 1) * 128)

    def at(plane):
        return (pl.ds(pl.multiple_of(plane * ROWS + block * 8, 8), 8), columns)

    depth = depth_ref[pl.ds(pl.multiple_of(block * 8, 8), 8), columns]
    result = eliminate(value, coupling, depth, at)
    lane = iota((8, 128), 1)
    column = jnp.zeros((8, 128), jnp.float32)
    for k in range(LEVELS):
        weight = jnp.where(k < depth, scale[at(k)], 0.0)
        for tracer in range(2):
            plane = tracer * LEVELS + k
            found = result[tracer][k]
            heavy = weight * found
            solved[tile_rows(quarter, plane, block), :] = found
            weighted[wide_rows(quarter, plane, block), :] = heavy
            if quarter == 0:
                moved = heavy if plane == 0 else pltpu.roll(heavy, plane, 1)
                column = jnp.where(lane == plane, moved, column)
            if quarter == 3:
                column = jnp.where(lane == plane, pltpu.roll(heavy, plane + 1, 1), column)
    if quarter == 0:
        sides[pl.ds(pl.multiple_of(block * 8, 8), 8), :] = column
    if quarter == 3:
        sides[pl.ds(pl.multiple_of(ROWS + block * 8, 8), 8), :] = column


def send_edges(meta, weighted, sides, payload, first_row, last_row):
    sub = meta[13]
    payload[0] = jnp.transpose(sides[...])[:PLANES, :]
    for b in range(4):
        top = weighted[pl.ds(b * PLANES * PITCH + 8, PLANES, stride=PITCH), :]
        bottom = weighted[pl.ds(b * PLANES * PITCH + ROWS + 7, PLANES, stride=PITCH), :]
        payload[1 + b] = jnp.where(sub == N_SUB - 1, bottom, top)
        first_row[b] = top
        last_row[b] = bottom


BIG = (f32(4 * QUARTER, 128), f32(4 * PLANES * PITCH, 128))
EDGES = (f32(5, PLANES, 128), f32(4, PLANES, 128), f32(4, PLANES, 128))


def first_tile(adjoint, force, coupling, scale, depth, solved, weighted, sides):
    def tile(block, quarter):
        columns = slice(quarter * 128, (quarter + 1) * 128)

        def value(plane):
            at = (pl.ds(pl.multiple_of(plane * ROWS + block * 8, 8), 8), columns)
            return adjoint[at] + force[at]

        solve_tile(value, coupling, scale, depth, solved, weighted, sides, block, quarter)

    return tile


def first_edges_kernel(meta, adjoint, force, coupling, scale, depth, solved, weighted, payload,
                       first_row, last_row, sides):
    edge_tiles(first_tile(adjoint, force, coupling, scale, depth, solved, weighted, sides))
    send_edges(meta, weighted, sides, payload, first_row, last_row)


def first_inner_kernel(adjoint, force, coupling, scale, depth, _, __, solved, weighted):
    inner_tiles(first_tile(adjoint, force, coupling, scale, depth, solved, weighted, None))


SIDES = pltpu.VMEM((128, 128), jnp.float32)


def cost(flops):
    return pl.CostEstimate(flops=flops, bytes_accessed=10000000, transcendentals=0)


def first_edges(meta, *given):
    return pl.pallas_call(
        first_edges_kernel,
        out_shape=BIG + EDGES,
        in_specs=[SMEM] + [VMEM] * 5,
        out_specs=(VMEM,) * 5,
        scratch_shapes=[SIDES],
        compiler_params=params(8),
        cost_estimate=cost(30000000),
        name="first_edges",
    )(meta, *given)


def first_inner(solved, weighted, *given):
    return pl.pallas_call(
        first_inner_kernel,
        out_shape=BIG,
        in_specs=[VMEM] * 7,
        out_specs=(VMEM,) * 2,
        input_output_aliases={5: 0, 6: 1},
        compiler_params=params(4),
        cost_estimate=cost(20000000),
        name="first_inner",
    )(*given, solved, weighted)


def route_kernel(meta, gathered, first_row, last_row, send, here):
    sub = meta[13]
    lane = iota((PLANES, 128), 1)

    def half(edge, dest, wanted):
        place, other_edge, turned = meta[3 * edge], meta[3 * edge + 1], meta[3 * edge + 2]
        chunk = jnp.where(turned == 1, N_SUB - 1 - dest, dest)
        block = jnp.where(other_edge < 2, 1 + (chunk >> 1), 0)
        side = jnp.where(other_edge < 2, chunk & 1, other_edge - 2)
        found = gathered[place, block]
        return jnp.where(side == wanted, found, pltpu.roll(found, 64, 1))

    for dest in range(N_SUB):
        send[dest, 0] = jnp.where(lane < 64, half(2, dest, 0), half(3, dest, 1))
        send[dest, 1] = jnp.zeros((PLANES, 128), jnp.float32)
    for edge, dest in ((0, 0), (1, N_SUB - 1)):
        found = gathered[meta[3 * edge], 0]
        send[dest, 1] = jnp.where(
            meta[3 * edge + 1] == 2, found, pltpu.roll(found, 64, 1)
        )
    own = jnp.where(sub == N_SUB - 1, 1, 0)
    place_here = meta[3 * own]
    place_across = meta[3 * (1 - own)]
    for b in range(4):
        here[b] = gathered[place_here, 1 + b]
        across = gathered[place_across, 1 + b]
        first = first_row[b]
        last = last_row[b]
        for dest in range(N_SUB):
            if dest == 0:
                row = jnp.where(sub == N_SUB - 1, across, first)
            elif dest == N_SUB - 1:
                row = jnp.where(sub == 0, across, last)
            else:
                row = jnp.where(sub == dest - 1, last, first)
            send[dest, 2 + b] = row


def route(meta, gathered, first_row, last_row):
    return pl.pallas_call(
        route_kernel,
        out_shape=(f32(N_SUB, 6, PLANES, 128), f32(4, PLANES, 128)),
        in_specs=[SMEM] + [VMEM] * 3,
        out_specs=(VMEM,) * 2,
        compiler_params=params(8),
        cost_estimate=pl.CostEstimate(flops=1000000, bytes_accessed=1000000, transcendentals=0),
        name="route",
    )(meta, gathered, first_row, last_row)


def exchange(meta, depth, beside_z, beside_y, payload, first_row, last_row):
    def turn(k):
        return [
            (y * 8 + z * 2 + c, y * 8 + ((z + k) % 4) * 2 + c)
            for y in range(2)
            for z in range(4)
            for c in range(2)
        ]

    all_parts = payload[None]
    all_parts = jnp.concatenate(
        [all_parts] + [lax.ppermute(all_parts, "tile", turn(k)) for k in (1, 2, 3)], axis=0
    )
    all_parts, depth, *extra = lax.optimization_barrier((all_parts, depth, *beside_z()))
    all_parts = jnp.concatenate(
        [all_parts, lax.ppermute(all_parts, "tile", [(i, i ^ 8) for i in range(N_TILE)])], axis=0
    )
    extra = beside_y(depth, *extra)
    all_parts, *extra = lax.optimization_barrier((all_parts, *extra))
    all_parts = jnp.concatenate(
        [all_parts, lax.ppermute(all_parts, "tile", [(i, i ^ 1) for i in range(N_TILE)])], axis=0
    )
    send, here = route(meta, all_parts, first_row, last_row)
    got = lax.all_to_all(send, "sub", split_axis=0, concat_axis=0, tiled=True)
    return (got, here), extra


def place_halo(meta, got, here, weighted, strips):
    sub = meta[13]
    before = jnp.maximum(sub - 1, 0)
    after = jnp.minimum(sub + 1, N_SUB - 1)
    opposite = jnp.where(sub == 0, N_SUB - 1, 0)
    lane = iota((PLANES, 128), 1)

    def source(edge):
        other_edge, turned = meta[3 * edge + 1], meta[3 * edge + 2]
        same = jnp.where(turned == 1, N_SUB - 1 - sub, sub)
        return jnp.where(other_edge == 0, 0, jnp.where(other_edge == 1, N_SUB - 1, same))

    sides = jnp.where(lane < 64, got[source(2), 0], got[source(3), 0])
    to = iota((128, 128), 0)
    of = iota((128, 128), 1)
    turned = jnp.where(to < 64, meta[8], meta[11])
    wanted = jnp.where(turned == 1, (to & 64) + 63 - (to & 63), to)
    pick = jnp.where(of == wanted, 1.0, 0.0)
    strips[:, :PLANES] = lax.dot_general(
        pick, sides, (((1,), (1,)), ((), ())), precision=HIGHEST, preferred_element_type=jnp.float32
    )

    own = jnp.where(sub == N_SUB - 1, 1, 0)
    other_edge, turned = meta[3 * own + 1], meta[3 * own + 2]
    flip = jnp.where(of == jnp.where(turned == 1, 127 - to, to), 1.0, 0.0)
    row = []
    for b in range(4):
        joined = jnp.where(lane < 64, got[2 * b, 1], pltpu.roll(got[2 * b + 1, 1], 64, 1))
        joined = jnp.where(other_edge < 2, got[opposite, 2 + b], joined)
        row.append(jnp.where(other_edge == own, here[b], joined))
    for b in range(4):
        ordered = jnp.where(turned == 1, row[3 - b], row[b])
        strip = jnp.dot(ordered, flip, precision=HIGHEST, preferred_element_type=jnp.float32)
        at = b * PLANES * PITCH
        above_row = jnp.where(sub == 0, strip, got[before, 2 + b])
        below_row = jnp.where(sub == N_SUB - 1, strip, got[after, 2 + b])
        weighted[pl.ds(at + 7, PLANES, stride=PITCH), :] = above_row
        weighted[pl.ds(at + ROWS + 8, PLANES, stride=PITCH), :] = below_row


def stepped(solved, weighted, scale, depth_ref, strips, block, quarter):
    columns = slice(quarter * 128, (quarter + 1) * 128)
    lane = iota((8, 128), 1)
    here = pl.ds(pl.multiple_of(block * 8, 8), 8)
    depth = depth_ref[here, columns]
    if quarter == 0:
        west = strips[here, :]
    if quarter == 3:
        east = strips[pl.ds(pl.multiple_of(ROWS + block * 8, 8), 8), :]
    weights = {}

    def value(plane):
        level = plane % LEVELS
        if level not in weights:
            at = pl.ds(pl.multiple_of(level * ROWS + block * 8, 8), 8)
            weights[level] = jnp.where(level < depth, scale[at, columns], 0.0) * explicit_rate
        center = weighted[wide_rows(quarter, plane, block), :]
        total = weighted[wide_rows(quarter, plane, block, -1), :]
        total = total + weighted[wide_rows(quarter, plane, block, 1), :]
        if quarter == 0:
            edge = west if plane == 0 else pltpu.roll(west, 128 - plane, 1)
            total = total + jnp.where(lane == 0, edge, pltpu.roll(center, 1, 1))
        else:
            left = weighted[wide_rows(quarter - 1, plane, block), :]
            total = total + pltpu.roll(jnp.where(lane == 127, left, center), 1, 1)
        if quarter == 3:
            edge = pltpu.roll(east, 127 - plane, 1)
            total = total + jnp.where(lane == 127, edge, pltpu.roll(center, 127, 1))
        else:
            right = weighted[wide_rows(quarter + 1, plane, block), :]
            total = total + pltpu.roll(jnp.where(lane == 0, right, center), 127, 1)
        return solved[tile_rows(quarter, plane, block), :] + weights[level] * (
            total - 4.0 * center
        )

    return value


def second_tile(solved_in, weighted_in, force, coupling, scale, depth, solved, weighted, strips,
                sides):
    def tile(block, quarter):
        columns = slice(quarter * 128, (quarter + 1) * 128)
        late = stepped(solved_in, weighted_in, scale, depth, strips, block, quarter)

        def value(plane):
            at = (pl.ds(pl.multiple_of(plane * ROWS + block * 8, 8), 8), columns)
            return late(plane) + force[at]

        solve_tile(value, coupling, scale, depth, solved, weighted, sides, block, quarter)

    return tile


def second_inner_kernel(solved_in, weighted_in, force, coupling, scale, depth, solved, weighted):
    inner_tiles(
        second_tile(
            solved_in, weighted_in, force, coupling, scale, depth, solved, weighted, None, None
        )
    )


def second_edges_kernel(meta, got, here, solved_in, weighted_in, force, coupling, scale, depth, _,
                        __, solved, weighted, payload, first_row, last_row, weighted_late, sides,
                        strips):
    place_halo(meta, got, here, weighted_late, strips)
    edge_tiles(
        second_tile(
            solved_in, weighted_late, force, coupling, scale, depth, solved, weighted, strips, sides
        )
    )
    send_edges(meta, weighted, sides, payload, first_row, last_row)


def second_inner(*given):
    return pl.pallas_call(
        second_inner_kernel,
        out_shape=BIG,
        in_specs=[VMEM] * 6,
        out_specs=(VMEM,) * 2,
        compiler_params=params(4),
        cost_estimate=cost(30000000),
        name="second_inner",
    )(*given)


def second_edges(meta, halos, *given):
    return pl.pallas_call(
        second_edges_kernel,
        out_shape=BIG + EDGES + BIG[1:],
        in_specs=[SMEM] + [VMEM] * 10,
        out_specs=(VMEM,) * 6,
        input_output_aliases={9: 0, 10: 1, 4: 5},
        scratch_shapes=[SIDES] * 2,
        compiler_params=params(8),
        cost_estimate=cost(40000000),
        name="second_edges",
    )(meta, *halos, *given)


def last_tile(solved, weighted, scale, depth, strips, ready):
    def tile(block, quarter):
        columns = slice(quarter * 128, (quarter + 1) * 128)
        value = stepped(solved, weighted, scale, depth, strips, block, quarter)
        for level in range(LEVELS):
            for plane in (level, LEVELS + level):
                ready[plane, pl.ds(pl.multiple_of(block * 8, 8), 8), columns] = value(plane)

    return tile


INSIDE = (slice(8, ROWS - 8), slice(128, 384))
OUTSIDE = [
    (slice(0, ROWS), slice(0, 128)),
    (slice(0, ROWS), slice(384, 512)),
    (slice(0, 8), slice(128, 384)),
    (slice(ROWS - 8, ROWS), slice(128, 384)),
]


def last_inner_kernel(solved, weighted, scale, depth, out, ready, sems):
    inner_tiles(last_tile(solved, weighted, scale, depth, None, ready))
    rows, columns = INSIDE
    copy = pltpu.make_async_copy(
        ready.at[:, rows, columns], out.at[:, rows, columns], sems.at[0]
    )
    copy.start()
    copy.wait()


def last_edges_kernel(meta, got, here, solved, weighted_in, scale, depth, _, out, weighted, strips,
                      ready, sems):
    place_halo(meta, got, here, weighted, strips)
    tile = last_tile(solved, weighted, scale, depth, strips, ready)

    def copy(i):
        rows, columns = OUTSIDE[i]
        return pltpu.make_async_copy(
            ready.at[:, rows, columns], out.at[:, rows, columns], sems.at[i]
        )

    def column(quarter):
        def step(block, carry):
            tile(block, quarter)
            return carry

        lax.fori_loop(0, ROWS // 8, step, 0)

    column(0)
    copy(0).start()
    column(3)
    copy(1).start()
    for i, block in ((2, 0), (3, ROWS // 8 - 1)):
        tile(block, 1)
        tile(block, 2)
        copy(i).start()
    for i in range(4):
        copy(i).wait()


READY = [pltpu.VMEM((PLANES, ROWS, COLS), jnp.float32), pltpu.SemaphoreType.DMA((4,))]
ANY = pl.BlockSpec(memory_space=pl.ANY)


def last_inner(*given):
    return pl.pallas_call(
        last_inner_kernel,
        out_shape=f32(PLANES, ROWS, COLS),
        in_specs=[VMEM] * 4,
        out_specs=ANY,
        scratch_shapes=READY,
        compiler_params=params(6),
        cost_estimate=cost(20000000),
        name="last_inner",
    )(*given)


def last_edges(meta, halos, *given):
    return pl.pallas_call(
        last_edges_kernel,
        out_shape=(f32(PLANES, ROWS, COLS), BIG[1]),
        in_specs=[SMEM] + [VMEM] * 6 + [ANY],
        out_specs=(ANY, VMEM),
        input_output_aliases={7: 0, 4: 1},
        scratch_shapes=[SIDES] + READY,
        compiler_params=params(8),
        cost_estimate=cost(20000000),
        name="last_edges",
    )(meta, *halos, *given)[0]


def body(
    adjoint_final,
    diff_scale,
    vert_coupling,
    column_depth,
    seam_table,
    tile_owner,
    prof_face,
    prof_cell,
    prof_time,
    misfit,
):
    rows = prof_face.shape[0]
    slots, meta = pack(
        tile_owner,
        jnp.transpose(seam_table, (2, 1, 0)),
        prof_face.reshape(1, rows),
        prof_cell.reshape(1, rows),
        prof_time.reshape(1, rows),
        misfit.reshape(PLANES, rows),
    )
    slots = lax.all_to_all(slots, ("tile", "sub"), split_axis=0, concat_axis=0, tiled=True)
    adjoint = adjoint_final.reshape(PLANES * ROWS, COLS)
    scale = diff_scale.reshape(LEVELS * ROWS, COLS)
    coupling = vert_coupling.reshape((LEVELS - 1) * ROWS, COLS)
    late = forcing(slots, 1)
    given = (adjoint, late, coupling, scale, column_depth)
    solved, weighted, *edges = first_edges(meta, *given)

    def beside_z():
        return (forcing(slots, 0),)

    def beside_y(depth, early):
        whole = first_inner(solved, weighted, *given[:-1], depth)
        return *whole, early, *second_inner(*whole, early, coupling, scale, depth)

    halos, (solved, weighted, early, *begun) = exchange(
        meta, column_depth, beside_z, beside_y, *edges
    )
    solved, weighted, *edges, _ = second_edges(
        meta, halos, solved, weighted, early, coupling, scale, column_depth, *begun
    )
    halos, begun = exchange(
        meta,
        column_depth,
        lambda: (),
        lambda depth: (last_inner(solved, weighted, scale, depth),),
        *edges,
    )
    out = last_edges(meta, halos, solved, weighted, scale, column_depth, *begun)
    return out.reshape(adjoint_final.shape)


def solution(mesh):
    return jax.shard_map(
        body,
        mesh=mesh,
        in_specs=(
            P(None, None, ("tile", "sub"), None),
            P(None, ("tile", "sub"), None),
            P(None, ("tile", "sub"), None),
            P(("tile", "sub"), None),
            P(),
            P(),
            P(("tile", "sub")),
            P(("tile", "sub")),
            P(("tile", "sub")),
            P(None, None, ("tile", "sub")),
        ),
        out_specs=P(None, None, ("tile", "sub"), None),
        check_vma=False,
    )
```

```python
import functools

import jax
import jax.numpy as jnp
from jax import lax
from jax.experimental import pallas as pl
from jax.experimental.pallas import tpu as pltpu
from jax.sharding import PartitionSpec as P

CAP = 4
LEVELS = 16
PLANES = 2 * LEVELS
ROWS = 64
COLS = 512
CELLS = ROWS * COLS
N_TILE = 16
N_SUB = 8
DEVICES = N_TILE * N_SUB
FACES = 16
explicit_rate = 0.2
HIGHEST = lax.Precision.HIGHEST
VMEM = pl.BlockSpec(memory_space=pltpu.VMEM)
SMEM = pl.BlockSpec(memory_space=pltpu.SMEM)
META = 16
PARTS = 2


def iota(shape, axis):
    return lax.broadcasted_iota(jnp.int32, shape, axis)


def params(mib):
    return pltpu.CompilerParams(vmem_limit_bytes=mib * 1024 * 1024)


def f32(*shape):
    return jax.ShapeDtypeStruct(shape, jnp.float32)


def pack_kernel(owner_in, seam_in, face_in, cell_in, time_in, misfit_in, out, meta, owners, seams,
                face, cell, time, misfit, sems):
    copies = [
        pltpu.make_async_copy(source, target, sems.at[i])
        for i, (source, target) in enumerate(
            (
                (owner_in, owners),
                (seam_in, seams),
                (face_in, face),
                (cell_in, cell),
                (time_in, time),
                (misfit_in, misfit),
            )
        )
    ]
    for copy in copies:
        copy.start()
    for copy in copies:
        copy.wait()

    def owner(f):
        return owners[f]

    def seam(part, edge, f):
        return seams[part, edge, f]


    tile = lax.axis_index("tile")
    sub = lax.axis_index("sub")
    my_face = jnp.int32(0)
    for f in range(FACES):
        my_face = my_face + jnp.where(owner(f) == tile, f, 0)
    meta[12] = tile
    meta[13] = sub
    for edge in range(4):
        other = owner(seam(0, edge, my_face))
        away = (
            ((other & 1) ^ (tile & 1)) * 8
            + (((other >> 3) & 1) ^ ((tile >> 3) & 1)) * 4
            + ((((tile >> 1) & 3) + 4 - ((other >> 1) & 3)) & 3)
        )
        meta[3 * edge] = away
        meta[3 * edge + 1] = seam(1, edge, my_face)
        meta[3 * edge + 2] = seam(2, edge, my_face)

    rows = face.shape[1]
    faces = face[...]
    home = jnp.zeros_like(faces)
    for f in range(FACES):
        home = jnp.where(faces == f, owner(f), home)
    cells = cell[...]
    tile_row = cells >> 9
    target = home * N_SUB + (tile_row >> 6)
    code = (time[...] - 1) * CELLS + (tile_row & (ROWS - 1)) * COLS + (cells & (COLS - 1))
    first = iota((rows, rows), 0)
    second = iota((rows, rows), 1)
    target_row = jnp.broadcast_to(target.astype(jnp.float32), (rows, rows))
    target_col = jnp.sum(jnp.where(first == second, target_row, 0.0), axis=1, keepdims=True)
    rank = jnp.sum(
        jnp.where((target_col == target_row) & (first < second), 1.0, 0.0), axis=0, keepdims=True
    )
    rank = rank.astype(jnp.int32)
    values = misfit[...]
    tag = code.astype(jnp.float32) + 1.0
    dest = iota((DEVICES, rows), 0)
    total = jnp.zeros((DEVICES, 2 * DEVICES), jnp.float32)
    for k in range(CAP):
        hit = jnp.where((dest == target) & (rank == k), 1.0, 0.0)
        pieces = []
        if k > 0:
            pieces.append(jnp.zeros((PLANES * k, rows), jnp.float32))
        pieces.append(values)
        if k < CAP - 1:
            pieces.append(jnp.zeros((PLANES * (CAP - 1 - k), rows), jnp.float32))
        pieces.append(jnp.where(dest == k, tag, 0.0))
        stacked = jnp.concatenate(pieces, axis=0)
        total = total + lax.dot_general(
            hit, stacked, (((1,), (1,)), ((), ())), precision=HIGHEST,
            preferred_element_type=jnp.float32,
        )
    out[:, 0, :] = total[:, :DEVICES]
    out[:, 1, :] = total[:, DEVICES:] - 1.0


def pack(owner, seam, face, cell, time, misfit):
    line = pltpu.VMEM(face.shape, jnp.int32)
    return pl.pallas_call(
        pack_kernel,
        out_shape=(f32(DEVICES, 2, DEVICES), jax.ShapeDtypeStruct((META,), jnp.int32)),
        in_specs=[pl.BlockSpec(memory_space=pl.ANY)] * 6,
        out_specs=(VMEM, SMEM),
        scratch_shapes=[
            pltpu.SMEM(owner.shape, jnp.int32),
            pltpu.SMEM(seam.shape, jnp.int32),
            line,
            line,
            line,
            pltpu.VMEM(misfit.shape, jnp.float32),
            pltpu.SemaphoreType.DMA((6,)),
        ],
        compiler_params=pltpu.CompilerParams(vmem_limit_bytes=66000000),
        name="pack",
    )(owner, seam, face, cell, time, misfit)


def forcing_kernel(moment, slots, out, parts, place):
    values = jnp.transpose(slots[:, 0, :])
    tags = (slots[:, 1, :] + 0.5).astype(jnp.int32)
    tags = jnp.where(slots[:, 1, :] < 0.0, -1, tags)
    tags_t = jnp.transpose(tags.astype(jnp.float32)).astype(jnp.int32)
    tag_row = jnp.concatenate([tags_t[k : k + 1, :] for k in range(CAP)], axis=1)
    valid = (tag_row >= moment * CELLS) & (tag_row < (moment + 1) * CELLS)
    row_of = jnp.where(valid, (tag_row & (CELLS - 1)) >> 9, -1)
    on_row = iota((ROWS, CAP * DEVICES), 0) == row_of
    wide = jnp.concatenate([values[PLANES * k : PLANES * (k + 1), :] for k in range(CAP)], axis=1)
    high = wide.astype(jnp.bfloat16).astype(jnp.float32)
    parts[0] = high
    parts[1] = wide - high
    for k in range(CAP):
        col = tags[:, k : k + 1] & (COLS - 1)
        place[k * DEVICES : (k + 1) * DEVICES, :] = jnp.where(
            iota((DEVICES, COLS), 1) == col, 1.0, 0.0
        ).astype(jnp.bfloat16)
    group = 4

    def step(g, carry):
        total = None
        for part in range(PARTS):
            left = []
            for q in range(group):
                row = parts[part, pl.ds(g * group + q, 1), :]
                left.append(jnp.where(on_row, row, 0.0).astype(jnp.bfloat16))
            got = jnp.dot(
                jnp.concatenate(left, axis=0), place[...], preferred_element_type=jnp.float32
            )
            total = got if total is None else total + got
        out[pl.ds(pl.multiple_of(g * group * ROWS, 8), group * ROWS), :] = total
        return carry

    lax.fori_loop(0, PLANES // group, step, 0)


def forcing(slots, moment):
    return pl.pallas_call(
        functools.partial(forcing_kernel, moment),
        out_shape=f32(PLANES * ROWS, COLS),
        in_specs=[VMEM],
        out_specs=VMEM,
        scratch_shapes=[
            pltpu.VMEM((PARTS, PLANES, CAP * DEVICES), jnp.float32),
            pltpu.VMEM((CAP * DEVICES, COLS), jnp.bfloat16),
        ],
        compiler_params=params(8),
        cost_estimate=pl.CostEstimate(flops=8000000000, bytes_accessed=4325376, transcendentals=0),
        name=f"forcing_{moment}",
    )(slots)


QUARTER = PLANES * ROWS


def tile_rows(quarter, plane, block):
    return pl.ds(pl.multiple_of(quarter * QUARTER + plane * ROWS + block * 8, 8), 8)


PITCH = ROWS + 16


def wide_rows(quarter, plane, block, shift=0):
    start = (quarter * PLANES + plane) * PITCH + 8
    if shift:
        return pl.ds(start + shift + block * 8, 8)
    return pl.ds(pl.multiple_of(start + block * 8, 8), 8)


def side_tiles(tile):
    def step(block, carry):
        tile(block, 0)
        tile(block, 3)
        return carry

    lax.fori_loop(1, ROWS // 8 - 1, step, 0)


def end_tiles(tile):
    def step(end, carry):
        for quarter in range(4):
            tile(end * (ROWS // 8 - 1), quarter)
        return carry

    lax.fori_loop(0, 2, step, 0)


def inner_tiles(tile):
    def step(block, carry):
        tile(block, 1)
        tile(block, 2)
        return carry

    lax.fori_loop(1, ROWS // 8 - 1, step, 0)


def eliminate(value, coupling, depth, at):
    links = []
    for k in range(LEVELS - 1):
        links.append(jnp.where(k + 1 < depth, coupling[at(k)], 0.0))
    ratio = []
    partial = [[], []]
    for k in range(LEVELS):
        pivot = jnp.float32(1.0)
        if k > 0:
            pivot = pivot + links[k - 1]
        if k < LEVELS - 1:
            pivot = pivot + links[k]
        if k > 0:
            pivot = pivot - links[k - 1] * ratio[k - 1]
        inverse = 1.0 / pivot
        for tracer in range(2):
            right = value(tracer * LEVELS + k)
            if k > 0:
                right = right + links[k - 1] * partial[tracer][k - 1]
            partial[tracer].append(right * inverse)
        if k < LEVELS - 1:
            ratio.append(links[k] * inverse)
    for k in range(LEVELS - 2, -1, -1):
        for tracer in range(2):
            partial[tracer][k] = partial[tracer][k] + ratio[k] * partial[tracer][k + 1]
    return partial


def solve_tile(value, coupling, scale, depth_ref, solved, weighted, sides, block, quarter):
    columns = slice(quarter * 128, (quarter + 1) * 128)

    def at(plane):
        return (pl.ds(pl.multiple_of(plane * ROWS + block * 8, 8), 8), columns)

    depth = depth_ref[pl.ds(pl.multiple_of(block * 8, 8), 8), columns]
    result = eliminate(value, coupling, depth, at)
    lane = iota((8, 128), 1)
    column = jnp.zeros((8, 128), jnp.float32)
    for k in range(LEVELS):
        weight = jnp.where(k < depth, scale[at(k)], 0.0)
        for tracer in range(2):
            plane = tracer * LEVELS + k
            found = result[tracer][k]
            heavy = weight * found
            solved[tile_rows(quarter, plane, block), :] = found
            weighted[wide_rows(quarter, plane, block), :] = heavy
            if quarter == 0:
                moved = heavy if plane == 0 else pltpu.roll(heavy, plane, 1)
                column = jnp.where(lane == plane, moved, column)
            if quarter == 3:
                column = jnp.where(lane == plane, pltpu.roll(heavy, plane + 1, 1), column)
    if quarter == 0:
        sides[pl.ds(pl.multiple_of(block * 8, 8), 8), :] = column
    if quarter == 3:
        sides[pl.ds(pl.multiple_of(ROWS + block * 8, 8), 8), :] = column


def send_edges(meta, weighted, sides, payload, first_row, last_row):
    sub = meta[13]
    payload[0] = jnp.transpose(sides[...])[:PLANES, :]
    for b in range(4):
        top = weighted[pl.ds(b * PLANES * PITCH + 8, PLANES, stride=PITCH), :]
        bottom = weighted[pl.ds(b * PLANES * PITCH + ROWS + 7, PLANES, stride=PITCH), :]
        payload[1 + b] = jnp.where(sub == N_SUB - 1, bottom, top)
        first_row[b] = top
        last_row[b] = bottom


BIG = (f32(4 * QUARTER, 128), f32(4 * PLANES * PITCH, 128))
EDGES = (f32(5, PLANES, 128), f32(4, PLANES, 128), f32(4, PLANES, 128))


def first_tile(adjoint, force, coupling, scale, depth, solved, weighted, sides):
    def tile(block, quarter):
        columns = slice(quarter * 128, (quarter + 1) * 128)

        def value(plane):
            at = (pl.ds(pl.multiple_of(plane * ROWS + block * 8, 8), 8), columns)
            return adjoint[at] + force[at]

        solve_tile(value, coupling, scale, depth, solved, weighted, sides, block, quarter)

    return tile


def first_edges_kernel(meta, adjoint, force, coupling, scale, depth, solved, weighted, payload,
                       first_row, last_row, sides):
    tile = first_tile(adjoint, force, coupling, scale, depth, solved, weighted, sides)
    side_tiles(tile)
    end_tiles(tile)
    send_edges(meta, weighted, sides, payload, first_row, last_row)


def first_inner_kernel(adjoint, force, coupling, scale, depth, _, __, solved, weighted):
    inner_tiles(first_tile(adjoint, force, coupling, scale, depth, solved, weighted, None))


SIDES = pltpu.VMEM((128, 128), jnp.float32)


def cost(flops):
    return pl.CostEstimate(flops=flops, bytes_accessed=10000000, transcendentals=0)


def first_edges(meta, *given):
    return pl.pallas_call(
        first_edges_kernel,
        out_shape=BIG + EDGES,
        in_specs=[SMEM] + [VMEM] * 5,
        out_specs=(VMEM,) * 5,
        scratch_shapes=[SIDES],
        compiler_params=params(8),
        cost_estimate=cost(30000000),
        name="first_edges",
    )(meta, *given)


def first_inner(solved, weighted, *given):
    return pl.pallas_call(
        first_inner_kernel,
        out_shape=BIG,
        in_specs=[VMEM] * 7,
        out_specs=(VMEM,) * 2,
        input_output_aliases={5: 0, 6: 1},
        compiler_params=params(4),
        cost_estimate=cost(20000000),
        name="first_inner",
    )(*given, solved, weighted)


def route_kernel(meta, gathered, send, here, across):
    sub = meta[13]
    lane = iota((PLANES, 128), 1)

    def half(edge, dest, wanted):
        place, other_edge, turned = meta[3 * edge], meta[3 * edge + 1], meta[3 * edge + 2]
        chunk = jnp.where(turned == 1, N_SUB - 1 - dest, dest)
        block = jnp.where(other_edge < 2, 1 + (chunk >> 1), 0)
        side = jnp.where(other_edge < 2, chunk & 1, other_edge - 2)
        found = gathered[place, block]
        return jnp.where(side == wanted, found, pltpu.roll(found, 64, 1))

    for dest in range(N_SUB):
        send[dest, 0] = jnp.where(lane < 64, half(2, dest, 0), half(3, dest, 1))
        send[dest, 1] = jnp.zeros((PLANES, 128), jnp.float32)
    for edge, dest in ((0, 0), (1, N_SUB - 1)):
        found = gathered[meta[3 * edge], 0]
        send[dest, 1] = jnp.where(
            meta[3 * edge + 1] == 2, found, pltpu.roll(found, 64, 1)
        )
    own = jnp.where(sub == N_SUB - 1, 1, 0)
    place_here = meta[3 * own]
    place_across = meta[3 * (1 - own)]
    for b in range(4):
        here[b] = gathered[place_here, 1 + b]
        across[b] = gathered[place_across, 1 + b]


def route(meta, gathered):
    return pl.pallas_call(
        route_kernel,
        out_shape=(f32(N_SUB, 2, PLANES, 128), f32(4, PLANES, 128), f32(4, PLANES, 128)),
        in_specs=[SMEM, VMEM],
        out_specs=(VMEM,) * 3,
        compiler_params=params(8),
        cost_estimate=pl.CostEstimate(flops=1000000, bytes_accessed=1000000, transcendentals=0),
        name="route",
    )(meta, gathered)


def exchange(meta, depth, beside_z, beside_y, payload, first_row, last_row):
    def turn(k):
        return [
            (y * 8 + z * 2 + c, y * 8 + ((z + k) % 4) * 2 + c)
            for y in range(2)
            for z in range(4)
            for c in range(2)
        ]

    all_parts = payload[None]
    all_parts = jnp.concatenate(
        [all_parts] + [lax.ppermute(all_parts, "tile", turn(k)) for k in (1, 2, 3)], axis=0
    )
    all_parts, depth, first_row, last_row, *extra = lax.optimization_barrier(
        (all_parts, depth, first_row, last_row, *beside_z())
    )
    above = lax.ppermute(last_row, "sub", [(i, i + 1) for i in range(N_SUB - 1)])
    below = lax.ppermute(first_row, "sub", [(i + 1, i) for i in range(N_SUB - 1)])
    all_parts = jnp.concatenate(
        [all_parts, lax.ppermute(all_parts, "tile", [(i, i ^ 8) for i in range(N_TILE)])], axis=0
    )
    extra = beside_y(depth, *extra)
    all_parts, above, below, *extra = lax.optimization_barrier(
        (all_parts, above, below, *extra)
    )
    all_parts = jnp.concatenate(
        [all_parts, lax.ppermute(all_parts, "tile", [(i, i ^ 1) for i in range(N_TILE)])], axis=0
    )
    send, here, across = route(meta, all_parts)
    got = lax.all_to_all(send, "sub", split_axis=0, concat_axis=0, tiled=True)
    got, across = lax.optimization_barrier((got, across))
    across = lax.ppermute(across, "sub", [(0, N_SUB - 1), (N_SUB - 1, 0)])
    return got, (here, across, above, below), extra


def place_strips(meta, got, strips):
    sub = meta[13]
    lane = iota((PLANES, 128), 1)

    def source(edge):
        other_edge, turned = meta[3 * edge + 1], meta[3 * edge + 2]
        same = jnp.where(turned == 1, N_SUB - 1 - sub, sub)
        return jnp.where(other_edge == 0, 0, jnp.where(other_edge == 1, N_SUB - 1, same))

    sides = jnp.where(lane < 64, got[source(2), 0], got[source(3), 0])
    to = iota((128, 128), 0)
    of = iota((128, 128), 1)
    turned = jnp.where(to < 64, meta[8], meta[11])
    wanted = jnp.where(turned == 1, (to & 64) + 63 - (to & 63), to)
    pick = jnp.where(of == wanted, 1.0, 0.0)
    strips[:, :PLANES] = lax.dot_general(
        pick, sides, (((1,), (1,)), ((), ())), precision=HIGHEST, preferred_element_type=jnp.float32
    )


def place_ends(meta, got, here, across, above, below, weighted):
    sub = meta[13]
    lane = iota((PLANES, 128), 1)
    to = iota((128, 128), 0)
    of = iota((128, 128), 1)
    own = jnp.where(sub == N_SUB - 1, 1, 0)
    other_edge, turned = meta[3 * own + 1], meta[3 * own + 2]
    flip = jnp.where(of == jnp.where(turned == 1, 127 - to, to), 1.0, 0.0)
    row = []
    for b in range(4):
        joined = jnp.where(lane < 64, got[2 * b, 1], pltpu.roll(got[2 * b + 1, 1], 64, 1))
        joined = jnp.where(other_edge < 2, across[b], joined)
        row.append(jnp.where(other_edge == own, here[b], joined))
    for b in range(4):
        ordered = jnp.where(turned == 1, row[3 - b], row[b])
        strip = jnp.dot(ordered, flip, precision=HIGHEST, preferred_element_type=jnp.float32)
        at = b * PLANES * PITCH
        above_row = jnp.where(sub == 0, strip, above[b])
        below_row = jnp.where(sub == N_SUB - 1, strip, below[b])
        weighted[pl.ds(at + 7, PLANES, stride=PITCH), :] = above_row
        weighted[pl.ds(at + ROWS + 8, PLANES, stride=PITCH), :] = below_row


def stepped(solved, weighted, scale, depth_ref, strips, block, quarter):
    columns = slice(quarter * 128, (quarter + 1) * 128)
    lane = iota((8, 128), 1)
    here = pl.ds(pl.multiple_of(block * 8, 8), 8)
    depth = depth_ref[here, columns]
    if quarter == 0:
        west = strips[here, :]
    if quarter == 3:
        east = strips[pl.ds(pl.multiple_of(ROWS + block * 8, 8), 8), :]
    weights = {}

    def value(plane):
        level = plane % LEVELS
        if level not in weights:
            at = pl.ds(pl.multiple_of(level * ROWS + block * 8, 8), 8)
            weights[level] = jnp.where(level < depth, scale[at, columns], 0.0) * explicit_rate
        center = weighted[wide_rows(quarter, plane, block), :]
        total = weighted[wide_rows(quarter, plane, block, -1), :]
        total = total + weighted[wide_rows(quarter, plane, block, 1), :]
        if quarter == 0:
            edge = west if plane == 0 else pltpu.roll(west, 128 - plane, 1)
            total = total + jnp.where(lane == 0, edge, pltpu.roll(center, 1, 1))
        else:
            left = weighted[wide_rows(quarter - 1, plane, block), :]
            total = total + pltpu.roll(jnp.where(lane == 127, left, center), 1, 1)
        if quarter == 3:
            edge = pltpu.roll(east, 127 - plane, 1)
            total = total + jnp.where(lane == 127, edge, pltpu.roll(center, 127, 1))
        else:
            right = weighted[wide_rows(quarter + 1, plane, block), :]
            total = total + pltpu.roll(jnp.where(lane == 0, right, center), 127, 1)
        return solved[tile_rows(quarter, plane, block), :] + weights[level] * (
            total - 4.0 * center
        )

    return value


def second_tile(solved_in, weighted_in, force, coupling, scale, depth, solved, weighted, strips,
                sides):
    def tile(block, quarter):
        columns = slice(quarter * 128, (quarter + 1) * 128)
        late = stepped(solved_in, weighted_in, scale, depth, strips, block, quarter)

        def value(plane):
            at = (pl.ds(pl.multiple_of(plane * ROWS + block * 8, 8), 8), columns)
            return late(plane) + force[at]

        solve_tile(value, coupling, scale, depth, solved, weighted, sides, block, quarter)

    return tile


def second_inner_kernel(solved_in, weighted_in, force, coupling, scale, depth, solved, weighted):
    inner_tiles(
        second_tile(
            solved_in, weighted_in, force, coupling, scale, depth, solved, weighted, None, None
        )
    )


def second_sides_kernel(meta, got, solved_in, weighted_in, force, coupling, scale, depth, _, __,
                        solved, weighted, strips, sides):
    place_strips(meta, got, strips)
    side_tiles(
        second_tile(
            solved_in, weighted_in, force, coupling, scale, depth, solved, weighted, strips, sides
        )
    )


def second_ends_kernel(meta, got, here, across, above, below, strips, sides_in, solved_in,
                       weighted_in, force, coupling, scale, depth, _, __, solved, weighted, payload,
                       first_row, last_row, weighted_late, sides):
    place_ends(meta, got, here, across, above, below, weighted_late)
    end_tiles(
        second_tile(
            solved_in, weighted_late, force, coupling, scale, depth, solved, weighted, strips, sides
        )
    )
    send_edges(meta, weighted, sides, payload, first_row, last_row)


def second_inner(*given):
    return pl.pallas_call(
        second_inner_kernel,
        out_shape=BIG,
        in_specs=[VMEM] * 6,
        out_specs=(VMEM,) * 2,
        compiler_params=params(4),
        cost_estimate=cost(30000000),
        name="second_inner",
    )(*given)


SQUARE = f32(128, 128)


def second_sides(meta, got, *given):
    return pl.pallas_call(
        second_sides_kernel,
        out_shape=BIG + (SQUARE, SQUARE),
        in_specs=[SMEM] + [VMEM] * 9,
        out_specs=(VMEM,) * 4,
        input_output_aliases={8: 0, 9: 1},
        compiler_params=params(4),
        cost_estimate=cost(30000000),
        name="second_sides",
    )(meta, got, *given)


def second_ends(meta, got, ends, *given):
    return pl.pallas_call(
        second_ends_kernel,
        out_shape=BIG + EDGES + BIG[1:] + (SQUARE,),
        in_specs=[SMEM] + [VMEM] * 15,
        out_specs=(VMEM,) * 7,
        input_output_aliases={14: 0, 15: 1, 9: 5, 7: 6},
        compiler_params=params(4),
        cost_estimate=cost(30000000),
        name="second_ends",
    )(meta, got, *ends, *given)


def last_tile(solved, weighted, scale, depth, strips, ready):
    def tile(block, quarter):
        columns = slice(quarter * 128, (quarter + 1) * 128)
        value = stepped(solved, weighted, scale, depth, strips, block, quarter)
        for level in range(LEVELS):
            for plane in (level, LEVELS + level):
                ready[plane, pl.ds(pl.multiple_of(block * 8, 8), 8), columns] = value(plane)

    return tile


INSIDE = (slice(8, ROWS - 8), slice(128, 384))
BESIDE = ((slice(8, ROWS - 8), slice(0, 128)), (slice(8, ROWS - 8), slice(384, 512)))
ENDS = ((slice(0, 8), slice(0, COLS)), (slice(ROWS - 8, ROWS), slice(0, COLS)))


def copies_out(ready, out, pieces, sems):
    return [
        pltpu.make_async_copy(ready.at[:, rows, columns], out.at[:, rows, columns], sems.at[i])
        for i, (rows, columns) in enumerate(pieces)
    ]


def last_inner_kernel(solved, weighted, scale, depth, out, ready, sems):
    inner_tiles(last_tile(solved, weighted, scale, depth, None, ready))
    for copy in copies_out(ready, out, (INSIDE,), sems):
        copy.start()
        copy.wait()


def last_sides_kernel(meta, got, solved, weighted, scale, depth, _, out, strips, ready, sems):
    place_strips(meta, got, strips)
    tile = last_tile(solved, weighted, scale, depth, strips, ready)
    copies = copies_out(ready, out, BESIDE, sems)
    for quarter, copy in zip((0, 3), copies):
        def step(block, carry):
            tile(block, quarter)
            return carry

        lax.fori_loop(1, ROWS // 8 - 1, step, 0)
        copy.start()
    for copy in copies:
        copy.wait()


def last_ends_kernel(meta, got, here, across, above, below, strips, solved, weighted_in, scale,
                     depth, _, out, weighted, ready, sems):
    place_ends(meta, got, here, across, above, below, weighted)
    tile = last_tile(solved, weighted, scale, depth, strips, ready)
    copies = copies_out(ready, out, ENDS, sems)
    for block, copy in zip((0, ROWS // 8 - 1), copies):
        for quarter in range(4):
            tile(block, quarter)
        copy.start()
    for copy in copies:
        copy.wait()


READY = [pltpu.VMEM((PLANES, ROWS, COLS), jnp.float32), pltpu.SemaphoreType.DMA((4,))]
ANY = pl.BlockSpec(memory_space=pl.ANY)


def last_inner(*given):
    return pl.pallas_call(
        last_inner_kernel,
        out_shape=f32(PLANES, ROWS, COLS),
        in_specs=[VMEM] * 4,
        out_specs=ANY,
        scratch_shapes=READY,
        compiler_params=params(6),
        cost_estimate=cost(20000000),
        name="last_inner",
    )(*given)


def last_sides(meta, got, *given):
    return pl.pallas_call(
        last_sides_kernel,
        out_shape=(f32(PLANES, ROWS, COLS), SQUARE),
        in_specs=[SMEM] + [VMEM] * 5 + [ANY],
        out_specs=(ANY, VMEM),
        input_output_aliases={6: 0},
        scratch_shapes=READY,
        compiler_params=params(6),
        cost_estimate=cost(20000000),
        name="last_sides",
    )(meta, got, *given)


def last_ends(meta, got, ends, *given):
    return pl.pallas_call(
        last_ends_kernel,
        out_shape=(f32(PLANES, ROWS, COLS), BIG[1]),
        in_specs=[SMEM] + [VMEM] * 10 + [ANY],
        out_specs=(ANY, VMEM),
        input_output_aliases={11: 0, 8: 1},
        scratch_shapes=READY,
        compiler_params=params(6),
        cost_estimate=cost(20000000),
        name="last_ends",
    )(meta, got, *ends, *given)[0]


def body(
    adjoint_final,
    diff_scale,
    vert_coupling,
    column_depth,
    seam_table,
    tile_owner,
    prof_face,
    prof_cell,
    prof_time,
    misfit,
):
    rows = prof_face.shape[0]
    slots, meta = pack(
        tile_owner,
        jnp.transpose(seam_table, (2, 1, 0)),
        prof_face.reshape(1, rows),
        prof_cell.reshape(1, rows),
        prof_time.reshape(1, rows),
        misfit.reshape(PLANES, rows),
    )
    slots = lax.all_to_all(slots, ("tile", "sub"), split_axis=0, concat_axis=0, tiled=True)
    adjoint = adjoint_final.reshape(PLANES * ROWS, COLS)
    scale = diff_scale.reshape(LEVELS * ROWS, COLS)
    coupling = vert_coupling.reshape((LEVELS - 1) * ROWS, COLS)
    late = forcing(slots, 1)
    given = (adjoint, late, coupling, scale, column_depth)
    solved, weighted, *edges = first_edges(meta, *given)

    def beside_z():
        return (forcing(slots, 0),)

    def beside_y(depth, early):
        whole = first_inner(solved, weighted, *given[:-1], depth)
        return *whole, early, *second_inner(*whole, early, coupling, scale, depth)

    got, ends, (solved, weighted, early, *begun) = exchange(
        meta, column_depth, beside_z, beside_y, *edges
    )
    given = (solved, weighted, early, coupling, scale, column_depth)
    *begun, strips, sides = second_sides(meta, got, *given, *begun)
    solved, weighted, *edges, _, _ = second_ends(meta, got, ends, strips, sides, *given, *begun)
    got, ends, begun = exchange(
        meta,
        column_depth,
        lambda: (),
        lambda depth: (last_inner(solved, weighted, scale, depth),),
        *edges,
    )
    given = (solved, weighted, scale, column_depth)
    out, strips = last_sides(meta, got, *given, *begun)
    out = last_ends(meta, got, ends, strips, *given, out)
    return out.reshape(adjoint_final.shape)


def solution(mesh):
    return jax.shard_map(
        body,
        mesh=mesh,
        in_specs=(
            P(None, None, ("tile", "sub"), None),
            P(None, ("tile", "sub"), None),
            P(None, ("tile", "sub"), None),
            P(("tile", "sub"), None),
            P(),
            P(),
            P(("tile", "sub")),
            P(("tile", "sub")),
            P(("tile", "sub")),
            P(None, None, ("tile", "sub")),
        ),
        out_specs=P(None, None, ("tile", "sub"), None),
        check_vma=False,
    )
```

```python
import functools

import jax
import jax.numpy as jnp
from jax import lax
from jax.experimental import pallas as pl
from jax.experimental.pallas import tpu as pltpu
from jax.sharding import PartitionSpec as P

CAP = 4
LEVELS = 16
PLANES = 2 * LEVELS
ROWS = 64
COLS = 512
CELLS = ROWS * COLS
N_TILE = 16
N_SUB = 8
DEVICES = N_TILE * N_SUB
FACES = 16
explicit_rate = 0.2
HIGHEST = lax.Precision.HIGHEST
VMEM = pl.BlockSpec(memory_space=pltpu.VMEM)
SMEM = pl.BlockSpec(memory_space=pltpu.SMEM)
META = 16
PARTS = 2


def iota(shape, axis):
    return lax.broadcasted_iota(jnp.int32, shape, axis)


def params(mib):
    return pltpu.CompilerParams(vmem_limit_bytes=mib * 1024 * 1024)


def f32(*shape):
    return jax.ShapeDtypeStruct(shape, jnp.float32)


def pack_kernel(owner_in, seam_in, face_in, cell_in, time_in, misfit_in, out, meta, owners, seams,
                face, cell, time, misfit, sems):
    copies = [
        pltpu.make_async_copy(source, target, sems.at[i])
        for i, (source, target) in enumerate(
            (
                (owner_in, owners),
                (seam_in, seams),
                (face_in, face),
                (cell_in, cell),
                (time_in, time),
                (misfit_in, misfit),
            )
        )
    ]
    for copy in copies:
        copy.start()
    for copy in copies:
        copy.wait()

    def owner(f):
        return owners[f]

    def seam(part, edge, f):
        return seams[part, edge, f]


    tile = lax.axis_index("tile")
    sub = lax.axis_index("sub")
    my_face = jnp.int32(0)
    for f in range(FACES):
        my_face = my_face + jnp.where(owner(f) == tile, f, 0)
    meta[12] = tile
    meta[13] = sub
    for edge in range(4):
        other = owner(seam(0, edge, my_face))
        away = (
            ((other & 1) ^ (tile & 1)) * 8
            + (((other >> 3) & 1) ^ ((tile >> 3) & 1)) * 4
            + ((((tile >> 1) & 3) + 4 - ((other >> 1) & 3)) & 3)
        )
        meta[3 * edge] = away
        meta[3 * edge + 1] = seam(1, edge, my_face)
        meta[3 * edge + 2] = seam(2, edge, my_face)

    rows = face.shape[1]
    faces = face[...]
    home = jnp.zeros_like(faces)
    for f in range(FACES):
        home = jnp.where(faces == f, owner(f), home)
    cells = cell[...]
    tile_row = cells >> 9
    target = home * N_SUB + (tile_row >> 6)
    code = (time[...] - 1) * CELLS + (tile_row & (ROWS - 1)) * COLS + (cells & (COLS - 1))
    first = iota((rows, rows), 0)
    second = iota((rows, rows), 1)
    target_row = jnp.broadcast_to(target.astype(jnp.float32), (rows, rows))
    target_col = jnp.sum(jnp.where(first == second, target_row, 0.0), axis=1, keepdims=True)
    rank = jnp.sum(
        jnp.where((target_col == target_row) & (first < second), 1.0, 0.0), axis=0, keepdims=True
    )
    rank = rank.astype(jnp.int32)
    values = misfit[...]
    tag = code.astype(jnp.float32) + 1.0
    dest = iota((DEVICES, rows), 0)
    total = jnp.zeros((DEVICES, 2 * DEVICES), jnp.float32)
    for k in range(CAP):
        hit = jnp.where((dest == target) & (rank == k), 1.0, 0.0)
        pieces = []
        if k > 0:
            pieces.append(jnp.zeros((PLANES * k, rows), jnp.float32))
        pieces.append(values)
        if k < CAP - 1:
            pieces.append(jnp.zeros((PLANES * (CAP - 1 - k), rows), jnp.float32))
        pieces.append(jnp.where(dest == k, tag, 0.0))
        stacked = jnp.concatenate(pieces, axis=0)
        total = total + lax.dot_general(
            hit, stacked, (((1,), (1,)), ((), ())), precision=HIGHEST,
            preferred_element_type=jnp.float32,
        )
    out[:, 0, :] = total[:, :DEVICES]
    out[:, 1, :] = total[:, DEVICES:] - 1.0


def pack(owner, seam, face, cell, time, misfit):
    line = pltpu.VMEM(face.shape, jnp.int32)
    return pl.pallas_call(
        pack_kernel,
        out_shape=(f32(DEVICES, 2, DEVICES), jax.ShapeDtypeStruct((META,), jnp.int32)),
        in_specs=[pl.BlockSpec(memory_space=pl.ANY)] * 6,
        out_specs=(VMEM, SMEM),
        scratch_shapes=[
            pltpu.SMEM(owner.shape, jnp.int32),
            pltpu.SMEM(seam.shape, jnp.int32),
            line,
            line,
            line,
            pltpu.VMEM(misfit.shape, jnp.float32),
            pltpu.SemaphoreType.DMA((6,)),
        ],
        compiler_params=pltpu.CompilerParams(vmem_limit_bytes=66000000),
        name="pack",
    )(owner, seam, face, cell, time, misfit)


def forcing_kernel(moment, slots, out, parts, place):
    values = jnp.transpose(slots[:, 0, :])
    tags = (slots[:, 1, :] + 0.5).astype(jnp.int32)
    tags = jnp.where(slots[:, 1, :] < 0.0, -1, tags)
    tags_t = jnp.transpose(tags.astype(jnp.float32)).astype(jnp.int32)
    tag_row = jnp.concatenate([tags_t[k : k + 1, :] for k in range(CAP)], axis=1)
    valid = (tag_row >= moment * CELLS) & (tag_row < (moment + 1) * CELLS)
    row_of = jnp.where(valid, (tag_row & (CELLS - 1)) >> 9, -1)
    on_row = iota((ROWS, CAP * DEVICES), 0) == row_of
    wide = jnp.concatenate([values[PLANES * k : PLANES * (k + 1), :] for k in range(CAP)], axis=1)
    high = wide.astype(jnp.bfloat16).astype(jnp.float32)
    parts[0] = high
    parts[1] = wide - high
    for k in range(CAP):
        col = tags[:, k : k + 1] & (COLS - 1)
        place[k * DEVICES : (k + 1) * DEVICES, :] = jnp.where(
            iota((DEVICES, COLS), 1) == col, 1.0, 0.0
        ).astype(jnp.bfloat16)
    group = 16

    def step(g, carry):
        total = None
        for part in range(PARTS):
            left = []
            for q in range(group):
                row = parts[part, pl.ds(g * group + q, 1), :]
                left.append(jnp.where(on_row, row, 0.0).astype(jnp.bfloat16))
            got = jnp.dot(
                jnp.concatenate(left, axis=0), place[...], preferred_element_type=jnp.float32
            )
            total = got if total is None else total + got
        out[pl.ds(pl.multiple_of(g * group * ROWS, 8), group * ROWS), :] = total
        return carry

    lax.fori_loop(0, PLANES // group, step, 0)


def forcing(slots, moment):
    return pl.pallas_call(
        functools.partial(forcing_kernel, moment),
        out_shape=f32(PLANES * ROWS, COLS),
        in_specs=[VMEM],
        out_specs=VMEM,
        scratch_shapes=[
            pltpu.VMEM((PARTS, PLANES, CAP * DEVICES), jnp.float32),
            pltpu.VMEM((CAP * DEVICES, COLS), jnp.bfloat16),
        ],
        compiler_params=params(16),
        cost_estimate=pl.CostEstimate(flops=8000000000, bytes_accessed=4325376, transcendentals=0),
        name=f"forcing_{moment}",
    )(slots)


QUARTER = PLANES * ROWS


def tile_rows(quarter, plane, block):
    return pl.ds(pl.multiple_of(quarter * QUARTER + plane * ROWS + block * 8, 8), 8)


PITCH = ROWS + 16


def wide_rows(quarter, plane, block, shift=0):
    start = (quarter * PLANES + plane) * PITCH + 8
    if shift:
        return pl.ds(start + shift + block * 8, 8)
    return pl.ds(pl.multiple_of(start + block * 8, 8), 8)


def edge_tiles(tile):
    def sides(block, carry):
        tile(block, 0)
        tile(block, 3)
        return carry

    def ends(end, carry):
        tile(end * (ROWS // 8 - 1), 1)
        tile(end * (ROWS // 8 - 1), 2)
        return carry

    lax.fori_loop(0, ROWS // 8, sides, 0, unroll=4)
    lax.fori_loop(0, 2, ends, 0)


def inner_tiles(tile):
    def step(block, carry):
        tile(block, 1)
        tile(block, 2)
        return carry

    lax.fori_loop(1, ROWS // 8 - 1, step, 0)


def eliminate(value, coupling, depth, at):
    links = []
    for k in range(LEVELS - 1):
        links.append(jnp.where(k + 1 < depth, coupling[at(k)], 0.0))
    ratio = []
    partial = [[], []]
    for k in range(LEVELS):
        pivot = jnp.float32(1.0)
        if k > 0:
            pivot = pivot + links[k - 1]
        if k < LEVELS - 1:
            pivot = pivot + links[k]
        if k > 0:
            pivot = pivot - links[k - 1] * ratio[k - 1]
        inverse = 1.0 / pivot
        for tracer in range(2):
            right = value(tracer * LEVELS + k)
            if k > 0:
                right = right + links[k - 1] * partial[tracer][k - 1]
            partial[tracer].append(right * inverse)
        if k < LEVELS - 1:
            ratio.append(links[k] * inverse)
    for k in range(LEVELS - 2, -1, -1):
        for tracer in range(2):
            partial[tracer][k] = partial[tracer][k] + ratio[k] * partial[tracer][k + 1]
    return partial


def solve_tile(value, coupling, scale, depth_ref, solved, weighted, sides, block, quarter):
    columns = slice(quarter * 128, (quarter + 1) * 128)

    def at(plane):
        return (pl.ds(pl.multiple_of(plane * ROWS + block * 8, 8), 8), columns)

    depth = depth_ref[pl.ds(pl.multiple_of(block * 8, 8), 8), columns]
    result = eliminate(value, coupling, depth, at)
    lane = iota((8, 128), 1)
    column = jnp.zeros((8, 128), jnp.float32)
    for k in range(LEVELS):
        weight = jnp.where(k < depth, scale[at(k)], 0.0)
        for tracer in range(2):
            plane = tracer * LEVELS + k
            found = result[tracer][k]
            heavy = weight * found
            solved[tile_rows(quarter, plane, block), :] = found
            weighted[wide_rows(quarter, plane, block), :] = heavy
            if quarter == 0:
                moved = heavy if plane == 0 else pltpu.roll(heavy, plane, 1)
                column = jnp.where(lane == plane, moved, column)
            if quarter == 3:
                column = jnp.where(lane == plane, pltpu.roll(heavy, plane + 1, 1), column)
    if quarter == 0:
        sides[pl.ds(pl.multiple_of(block * 8, 8), 8), :] = column
    if quarter == 3:
        sides[pl.ds(pl.multiple_of(ROWS + block * 8, 8), 8), :] = column


def send_edges(meta, weighted, sides, payload, first_row, last_row):
    sub = meta[13]
    payload[0] = jnp.transpose(sides[...])[:PLANES, :]
    for b in range(4):
        top = weighted[pl.ds(b * PLANES * PITCH + 8, PLANES, stride=PITCH), :]
        bottom = weighted[pl.ds(b * PLANES * PITCH + ROWS + 7, PLANES, stride=PITCH), :]
        payload[1 + b] = jnp.where(sub == N_SUB - 1, bottom, top)
        first_row[b] = top
        last_row[b] = bottom


BIG = (f32(4 * QUARTER, 128), f32(4 * PLANES * PITCH, 128))
EDGES = (f32(5, PLANES, 128), f32(4, PLANES, 128), f32(4, PLANES, 128))


def first_tile(adjoint, force, coupling, scale, depth, solved, weighted, sides):
    def tile(block, quarter):
        columns = slice(quarter * 128, (quarter + 1) * 128)

        def value(plane):
            at = (pl.ds(pl.multiple_of(plane * ROWS + block * 8, 8), 8), columns)
            return adjoint[at] + force[at]

        solve_tile(value, coupling, scale, depth, solved, weighted, sides, block, quarter)

    return tile


def first_edges_kernel(meta, adjoint, force, coupling, scale, depth, solved, weighted, payload,
                       first_row, last_row, sides):
    edge_tiles(first_tile(adjoint, force, coupling, scale, depth, solved, weighted, sides))
    send_edges(meta, weighted, sides, payload, first_row, last_row)


def first_inner_kernel(adjoint, force, coupling, scale, depth, _, __, solved, weighted):
    inner_tiles(first_tile(adjoint, force, coupling, scale, depth, solved, weighted, None))


SIDES = pltpu.VMEM((128, 128), jnp.float32)


def cost(flops):
    return pl.CostEstimate(flops=flops, bytes_accessed=10000000, transcendentals=0)


def first_edges(meta, *given):
    return pl.pallas_call(
        first_edges_kernel,
        out_shape=BIG + EDGES,
        in_specs=[SMEM] + [VMEM] * 5,
        out_specs=(VMEM,) * 5,
        scratch_shapes=[SIDES],
        compiler_params=params(8),
        cost_estimate=cost(30000000),
        name="first_edges",
    )(meta, *given)


def first_inner(solved, weighted, *given):
    return pl.pallas_call(
        first_inner_kernel,
        out_shape=BIG,
        in_specs=[VMEM] * 7,
        out_specs=(VMEM,) * 2,
        input_output_aliases={5: 0, 6: 1},
        compiler_params=params(4),
        cost_estimate=cost(20000000),
        name="first_inner",
    )(*given, solved, weighted)


SLOT_ROWS = PLANES + LEVELS


def route_kernel(meta, gathered, first_row, last_row, send, here):
    sub = meta[13]
    lane = iota((PLANES, 128), 1)

    def half(edge, dest, wanted):
        place, other_edge, turned = meta[3 * edge], meta[3 * edge + 1], meta[3 * edge + 2]
        chunk = jnp.where(turned == 1, N_SUB - 1 - dest, dest)
        block = jnp.where(other_edge < 2, 1 + (chunk >> 1), 0)
        side = jnp.where(other_edge < 2, chunk & 1, other_edge - 2)
        found = gathered[place, block]
        return jnp.where(side == wanted, found, pltpu.roll(found, 64, 1))

    for dest in range(N_SUB):
        send[dest, :PLANES, :] = jnp.where(lane < 64, half(2, dest, 0), half(3, dest, 1))
        send[dest, PLANES : PLANES + LEVELS, :] = jnp.zeros((LEVELS, 128), jnp.float32)
    for edge, dest in ((0, 0), (1, N_SUB - 1)):
        found = gathered[meta[3 * edge], 0]
        turned = pltpu.roll(found, 64, 1)
        low = jnp.where(meta[3 * edge + 1] == 2, found, turned)
        high = jnp.where(meta[3 * edge + 1] == 2, turned, found)
        send[dest, PLANES : PLANES + LEVELS, :] = jnp.where(
            lane[:LEVELS] < 64, low[:LEVELS], high[LEVELS:]
        )
    own = jnp.where(sub == N_SUB - 1, 1, 0)
    place_here = meta[3 * own]
    place_across = meta[3 * (1 - own)]
    for b in range(4):
        here[b] = gathered[place_here, 1 + b]
        across = gathered[place_across, 1 + b]
        first = first_row[b]
        last = last_row[b]
        for dest in range(N_SUB):
            if dest == 0:
                row = jnp.where(sub == N_SUB - 1, across, first)
            elif dest == N_SUB - 1:
                row = jnp.where(sub == 0, across, last)
            else:
                row = jnp.where(sub == dest - 1, last, first)
            send[dest, SLOT_ROWS + b * PLANES : SLOT_ROWS + (b + 1) * PLANES, :] = row


def route(meta, gathered, first_row, last_row):
    return pl.pallas_call(
        route_kernel,
        out_shape=(f32(N_SUB, SLOT_ROWS + 4 * PLANES, 128), f32(4, PLANES, 128)),
        in_specs=[SMEM] + [VMEM] * 3,
        out_specs=(VMEM,) * 2,
        compiler_params=params(8),
        cost_estimate=pl.CostEstimate(flops=1000000, bytes_accessed=1000000, transcendentals=0),
        name="route",
    )(meta, gathered, first_row, last_row)


def exchange(meta, depth, beside_z, beside_y, payload, first_row, last_row):
    def turn(k):
        return [
            (y * 8 + z * 2 + c, y * 8 + ((z + k) % 4) * 2 + c)
            for y in range(2)
            for z in range(4)
            for c in range(2)
        ]

    all_parts = payload[None]
    all_parts = jnp.concatenate(
        [all_parts] + [lax.ppermute(all_parts, "tile", turn(k)) for k in (1, 2, 3)], axis=0
    )
    all_parts, depth, *extra = lax.optimization_barrier((all_parts, depth, *beside_z()))
    all_parts = jnp.concatenate(
        [all_parts, lax.ppermute(all_parts, "tile", [(i, i ^ 8) for i in range(N_TILE)])], axis=0
    )
    extra = beside_y(depth, *extra)
    all_parts, *extra = lax.optimization_barrier((all_parts, *extra))
    all_parts = jnp.concatenate(
        [all_parts, lax.ppermute(all_parts, "tile", [(i, i ^ 1) for i in range(N_TILE)])], axis=0
    )
    send, here = route(meta, all_parts, first_row, last_row)
    got = lax.all_to_all(send, "sub", split_axis=0, concat_axis=0, tiled=True)
    return (got, here), extra


def place_halo(meta, got, here, weighted, strips):
    sub = meta[13]
    before = jnp.maximum(sub - 1, 0)
    after = jnp.minimum(sub + 1, N_SUB - 1)
    opposite = jnp.where(sub == 0, N_SUB - 1, 0)
    lane = iota((PLANES, 128), 1)

    def source(edge):
        other_edge, turned = meta[3 * edge + 1], meta[3 * edge + 2]
        same = jnp.where(turned == 1, N_SUB - 1 - sub, sub)
        return jnp.where(other_edge == 0, 0, jnp.where(other_edge == 1, N_SUB - 1, same))

    sides = jnp.where(lane < 64, got[source(2), :PLANES, :], got[source(3), :PLANES, :])
    to = iota((128, 128), 0)
    of = iota((128, 128), 1)
    turned = jnp.where(to < 64, meta[8], meta[11])
    wanted = jnp.where(turned == 1, (to & 64) + 63 - (to & 63), to)
    pick = jnp.where(of == wanted, 1.0, 0.0)
    strips[:, :PLANES] = lax.dot_general(
        pick, sides, (((1,), (1,)), ((), ())), precision=HIGHEST, preferred_element_type=jnp.float32
    )

    own = jnp.where(sub == N_SUB - 1, 1, 0)
    other_edge, turned = meta[3 * own + 1], meta[3 * own + 2]
    flip = jnp.where(of == jnp.where(turned == 1, 127 - to, to), 1.0, 0.0)
    row = []
    for b in range(4):
        part = slice(SLOT_ROWS + b * PLANES, SLOT_ROWS + (b + 1) * PLANES)
        even = got[2 * b, PLANES:SLOT_ROWS, :]
        odd = got[2 * b + 1, PLANES:SLOT_ROWS, :]
        joined = jnp.concatenate(
            [
                jnp.where(lane[:LEVELS] < 64, even, pltpu.roll(odd, 64, 1)),
                jnp.where(lane[:LEVELS] < 64, pltpu.roll(even, 64, 1), odd),
            ],
            axis=0,
        )
        joined = jnp.where(other_edge < 2, got[opposite, part, :], joined)
        row.append(jnp.where(other_edge == own, here[b], joined))
    for b in range(4):
        ordered = jnp.where(turned == 1, row[3 - b], row[b])
        strip = jnp.dot(ordered, flip, precision=HIGHEST, preferred_element_type=jnp.float32)
        at = b * PLANES * PITCH
        part = slice(SLOT_ROWS + b * PLANES, SLOT_ROWS + (b + 1) * PLANES)
        above_row = jnp.where(sub == 0, strip, got[before, part, :])
        below_row = jnp.where(sub == N_SUB - 1, strip, got[after, part, :])
        weighted[pl.ds(at + 7, PLANES, stride=PITCH), :] = above_row
        weighted[pl.ds(at + ROWS + 8, PLANES, stride=PITCH), :] = below_row


def stepped(solved, weighted, scale, depth_ref, strips, block, quarter):
    columns = slice(quarter * 128, (quarter + 1) * 128)
    lane = iota((8, 128), 1)
    here = pl.ds(pl.multiple_of(block * 8, 8), 8)
    depth = depth_ref[here, columns]
    if quarter == 0:
        west = strips[here, :]
    if quarter == 3:
        east = strips[pl.ds(pl.multiple_of(ROWS + block * 8, 8), 8), :]
    weights = {}

    def value(plane):
        level = plane % LEVELS
        if level not in weights:
            at = pl.ds(pl.multiple_of(level * ROWS + block * 8, 8), 8)
            weights[level] = jnp.where(level < depth, scale[at, columns], 0.0) * explicit_rate
        center = weighted[wide_rows(quarter, plane, block), :]
        total = weighted[wide_rows(quarter, plane, block, -1), :]
        total = total + weighted[wide_rows(quarter, plane, block, 1), :]
        if quarter == 0:
            edge = west if plane == 0 else pltpu.roll(west, 128 - plane, 1)
            total = total + jnp.where(lane == 0, edge, pltpu.roll(center, 1, 1))
        else:
            left = weighted[wide_rows(quarter - 1, plane, block), :]
            total = total + pltpu.roll(jnp.where(lane == 127, left, center), 1, 1)
        if quarter == 3:
            edge = pltpu.roll(east, 127 - plane, 1)
            total = total + jnp.where(lane == 127, edge, pltpu.roll(center, 127, 1))
        else:
            right = weighted[wide_rows(quarter + 1, plane, block), :]
            total = total + pltpu.roll(jnp.where(lane == 0, right, center), 127, 1)
        return solved[tile_rows(quarter, plane, block), :] + weights[level] * (
            total - 4.0 * center
        )

    return value


def second_tile(solved_in, weighted_in, force, coupling, scale, depth, solved, weighted, strips,
                sides):
    def tile(block, quarter):
        columns = slice(quarter * 128, (quarter + 1) * 128)
        late = stepped(solved_in, weighted_in, scale, depth, strips, block, quarter)

        def value(plane):
            at = (pl.ds(pl.multiple_of(plane * ROWS + block * 8, 8), 8), columns)
            return late(plane) + force[at]

        solve_tile(value, coupling, scale, depth, solved, weighted, sides, block, quarter)

    return tile


def second_inner_kernel(solved_in, weighted_in, force, coupling, scale, depth, solved, weighted):
    inner_tiles(
        second_tile(
            solved_in, weighted_in, force, coupling, scale, depth, solved, weighted, None, None
        )
    )


def second_edges_kernel(meta, got, here, solved_in, weighted_in, force, coupling, scale, depth, _,
                        __, solved, weighted, payload, first_row, last_row, weighted_late, sides,
                        strips):
    place_halo(meta, got, here, weighted_late, strips)
    edge_tiles(
        second_tile(
            solved_in, weighted_late, force, coupling, scale, depth, solved, weighted, strips, sides
        )
    )
    send_edges(meta, weighted, sides, payload, first_row, last_row)


def second_inner(*given):
    return pl.pallas_call(
        second_inner_kernel,
        out_shape=BIG,
        in_specs=[VMEM] * 6,
        out_specs=(VMEM,) * 2,
        compiler_params=params(4),
        cost_estimate=cost(30000000),
        name="second_inner",
    )(*given)


def second_edges(meta, halos, *given):
    return pl.pallas_call(
        second_edges_kernel,
        out_shape=BIG + EDGES + BIG[1:],
        in_specs=[SMEM] + [VMEM] * 10,
        out_specs=(VMEM,) * 6,
        input_output_aliases={9: 0, 10: 1, 4: 5},
        scratch_shapes=[SIDES] * 2,
        compiler_params=params(8),
        cost_estimate=cost(40000000),
        name="second_edges",
    )(meta, *halos, *given)


def last_tile(solved, weighted, scale, depth, strips, ready):
    def tile(block, quarter):
        columns = slice(quarter * 128, (quarter + 1) * 128)
        value = stepped(solved, weighted, scale, depth, strips, block, quarter)
        for level in range(LEVELS):
            for plane in (level, LEVELS + level):
                ready[plane, pl.ds(pl.multiple_of(block * 8, 8), 8), columns] = value(plane)

    return tile


INSIDE = (slice(8, ROWS - 8), slice(128, 384))
OUTSIDE = [
    (slice(0, ROWS), slice(0, 128)),
    (slice(0, ROWS), slice(384, 512)),
    (slice(0, 8), slice(128, 384)),
    (slice(ROWS - 8, ROWS), slice(128, 384)),
]


def last_inner_kernel(solved, weighted, scale, depth, out, ready, sems):
    inner_tiles(last_tile(solved, weighted, scale, depth, None, ready))
    rows, columns = INSIDE
    copy = pltpu.make_async_copy(
        ready.at[:, rows, columns], out.at[:, rows, columns], sems.at[0]
    )
    copy.start()
    copy.wait()


def last_edges_kernel(meta, got, here, solved, weighted_in, scale, depth, _, out, weighted, strips,
                      ready, sems):
    place_halo(meta, got, here, weighted, strips)
    tile = last_tile(solved, weighted, scale, depth, strips, ready)

    def copy(i):
        rows, columns = OUTSIDE[i]
        return pltpu.make_async_copy(
            ready.at[:, rows, columns], out.at[:, rows, columns], sems.at[i]
        )

    def column(quarter):
        def step(block, carry):
            tile(block, quarter)
            return carry

        lax.fori_loop(0, ROWS // 8, step, 0, unroll=4)

    column(0)
    copy(0).start()
    column(3)
    copy(1).start()
    for i, block in ((2, 0), (3, ROWS // 8 - 1)):
        tile(block, 1)
        tile(block, 2)
        copy(i).start()
    for i in range(4):
        copy(i).wait()


READY = [pltpu.VMEM((PLANES, ROWS, COLS), jnp.float32), pltpu.SemaphoreType.DMA((4,))]
ANY = pl.BlockSpec(memory_space=pl.ANY)


def last_inner(*given):
    return pl.pallas_call(
        last_inner_kernel,
        out_shape=f32(PLANES, ROWS, COLS),
        in_specs=[VMEM] * 4,
        out_specs=ANY,
        scratch_shapes=READY,
        compiler_params=params(6),
        cost_estimate=cost(20000000),
        name="last_inner",
    )(*given)


def last_edges(meta, halos, *given):
    return pl.pallas_call(
        last_edges_kernel,
        out_shape=(f32(PLANES, ROWS, COLS), BIG[1]),
        in_specs=[SMEM] + [VMEM] * 6 + [ANY],
        out_specs=(ANY, VMEM),
        input_output_aliases={7: 0, 4: 1},
        scratch_shapes=[SIDES] + READY,
        compiler_params=params(8),
        cost_estimate=cost(20000000),
        name="last_edges",
    )(meta, *halos, *given)[0]


def body(
    adjoint_final,
    diff_scale,
    vert_coupling,
    column_depth,
    seam_table,
    tile_owner,
    prof_face,
    prof_cell,
    prof_time,
    misfit,
):
    rows = prof_face.shape[0]
    slots, meta = pack(
        tile_owner,
        jnp.transpose(seam_table, (2, 1, 0)),
        prof_face.reshape(1, rows),
        prof_cell.reshape(1, rows),
        prof_time.reshape(1, rows),
        misfit.reshape(PLANES, rows),
    )
    slots = lax.all_to_all(slots, ("tile", "sub"), split_axis=0, concat_axis=0, tiled=True)
    adjoint = adjoint_final.reshape(PLANES * ROWS, COLS)
    scale = diff_scale.reshape(LEVELS * ROWS, COLS)
    coupling = vert_coupling.reshape((LEVELS - 1) * ROWS, COLS)
    late = forcing(slots, 1)
    given = (adjoint, late, coupling, scale, column_depth)
    solved, weighted, *edges = first_edges(meta, *given)

    def beside_z():
        return (forcing(slots, 0),)

    def beside_y(depth, early):
        whole = first_inner(solved, weighted, *given[:-1], depth)
        return *whole, early, *second_inner(*whole, early, coupling, scale, depth)

    halos, (solved, weighted, early, *begun) = exchange(
        meta, column_depth, beside_z, beside_y, *edges
    )
    solved, weighted, *edges, _ = second_edges(
        meta, halos, solved, weighted, early, coupling, scale, column_depth, *begun
    )
    halos, begun = exchange(
        meta,
        column_depth,
        lambda: (),
        lambda depth: (last_inner(solved, weighted, scale, depth),),
        *edges,
    )
    out = last_edges(meta, halos, solved, weighted, scale, column_depth, *begun)
    return out.reshape(adjoint_final.shape)


def solution(mesh):
    return jax.shard_map(
        body,
        mesh=mesh,
        in_specs=(
            P(None, None, ("tile", "sub"), None),
            P(None, ("tile", "sub"), None),
            P(None, ("tile", "sub"), None),
            P(("tile", "sub"), None),
            P(),
            P(),
            P(("tile", "sub")),
            P(("tile", "sub")),
            P(("tile", "sub")),
            P(None, None, ("tile", "sub")),
        ),
        out_specs=P(None, None, ("tile", "sub"), None),
        check_vma=False,
    )
```

```python
import functools

import jax
import jax.numpy as jnp
from jax import lax
from jax.experimental import pallas as pl
from jax.experimental.pallas import tpu as pltpu
from jax.sharding import PartitionSpec as P

CAP = 4
LEVELS = 16
PLANES = 2 * LEVELS
ROWS = 64
COLS = 512
CELLS = ROWS * COLS
N_TILE = 16
N_SUB = 8
DEVICES = N_TILE * N_SUB
FACES = 16
explicit_rate = 0.2
HIGHEST = lax.Precision.HIGHEST
VMEM = pl.BlockSpec(memory_space=pltpu.VMEM)
SMEM = pl.BlockSpec(memory_space=pltpu.SMEM)
META = 16
PARTS = 2


def iota(shape, axis):
    return lax.broadcasted_iota(jnp.int32, shape, axis)


def params(mib):
    return pltpu.CompilerParams(vmem_limit_bytes=mib * 1024 * 1024)


def f32(*shape):
    return jax.ShapeDtypeStruct(shape, jnp.float32)


def pack_kernel(owner_in, seam_in, face_in, cell_in, time_in, misfit_in, out, meta, owners, seams,
                face, cell, time, misfit, sems):
    copies = [
        pltpu.make_async_copy(source, target, sems.at[i])
        for i, (source, target) in enumerate(
            (
                (owner_in, owners),
                (seam_in, seams),
                (face_in, face),
                (cell_in, cell),
                (time_in, time),
                (misfit_in, misfit),
            )
        )
    ]
    for copy in copies:
        copy.start()
    for copy in copies:
        copy.wait()

    def owner(f):
        return owners[f]

    def seam(part, edge, f):
        return seams[part, edge, f]


    tile = lax.axis_index("tile")
    sub = lax.axis_index("sub")
    my_face = jnp.int32(0)
    for f in range(FACES):
        my_face = my_face + jnp.where(owner(f) == tile, f, 0)
    meta[12] = tile
    meta[13] = sub
    for edge in range(4):
        other = owner(seam(0, edge, my_face))
        steps = (((tile >> 1) & 3) + 4 - ((other >> 1) & 3)) & 3
        away = (
            ((other & 1) ^ (tile & 1)) * 8
            + (((other >> 3) & 1) ^ ((tile >> 3) & 1)) * 4
            + (steps ^ (steps >> 1))
        )
        meta[3 * edge] = away
        meta[3 * edge + 1] = seam(1, edge, my_face)
        meta[3 * edge + 2] = seam(2, edge, my_face)

    rows = face.shape[1]
    faces = face[...]
    home = jnp.zeros_like(faces)
    for f in range(FACES):
        home = jnp.where(faces == f, owner(f), home)
    cells = cell[...]
    tile_row = cells >> 9
    target = home * N_SUB + (tile_row >> 6)
    code = (time[...] - 1) * CELLS + (tile_row & (ROWS - 1)) * COLS + (cells & (COLS - 1))
    first = iota((rows, rows), 0)
    second = iota((rows, rows), 1)
    target_row = jnp.broadcast_to(target.astype(jnp.float32), (rows, rows))
    target_col = jnp.sum(jnp.where(first == second, target_row, 0.0), axis=1, keepdims=True)
    rank = jnp.sum(
        jnp.where((target_col == target_row) & (first < second), 1.0, 0.0), axis=0, keepdims=True
    )
    rank = rank.astype(jnp.int32)
    values = misfit[...]
    tag = code.astype(jnp.float32) + 1.0
    dest = iota((DEVICES, rows), 0)
    total = jnp.zeros((DEVICES, 2 * DEVICES), jnp.float32)
    for k in range(CAP):
        hit = jnp.where((dest == target) & (rank == k), 1.0, 0.0)
        pieces = []
        if k > 0:
            pieces.append(jnp.zeros((PLANES * k, rows), jnp.float32))
        pieces.append(values)
        if k < CAP - 1:
            pieces.append(jnp.zeros((PLANES * (CAP - 1 - k), rows), jnp.float32))
        pieces.append(jnp.where(dest == k, tag, 0.0))
        stacked = jnp.concatenate(pieces, axis=0)
        total = total + lax.dot_general(
            hit, stacked, (((1,), (1,)), ((), ())), precision=HIGHEST,
            preferred_element_type=jnp.float32,
        )
    out[:, 0, :] = total[:, :DEVICES]
    out[:, 1, :] = total[:, DEVICES:] - 1.0


def pack(owner, seam, face, cell, time, misfit):
    line = pltpu.VMEM(face.shape, jnp.int32)
    return pl.pallas_call(
        pack_kernel,
        out_shape=(f32(DEVICES, 2, DEVICES), jax.ShapeDtypeStruct((META,), jnp.int32)),
        in_specs=[pl.BlockSpec(memory_space=pl.ANY)] * 6,
        out_specs=(VMEM, SMEM),
        scratch_shapes=[
            pltpu.SMEM(owner.shape, jnp.int32),
            pltpu.SMEM(seam.shape, jnp.int32),
            line,
            line,
            line,
            pltpu.VMEM(misfit.shape, jnp.float32),
            pltpu.SemaphoreType.DMA((6,)),
        ],
        compiler_params=pltpu.CompilerParams(vmem_limit_bytes=66000000),
        name="pack",
    )(owner, seam, face, cell, time, misfit)


def forcing_kernel(moment, slots, out, parts, place):
    values = jnp.transpose(slots[:, 0, :])
    tags = (slots[:, 1, :] + 0.5).astype(jnp.int32)
    tags = jnp.where(slots[:, 1, :] < 0.0, -1, tags)
    tags_t = jnp.transpose(tags.astype(jnp.float32)).astype(jnp.int32)
    tag_row = jnp.concatenate([tags_t[k : k + 1, :] for k in range(CAP)], axis=1)
    valid = (tag_row >= moment * CELLS) & (tag_row < (moment + 1) * CELLS)
    row_of = jnp.where(valid, (tag_row & (CELLS - 1)) >> 9, -1)
    on_row = iota((ROWS, CAP * DEVICES), 0) == row_of
    wide = jnp.concatenate([values[PLANES * k : PLANES * (k + 1), :] for k in range(CAP)], axis=1)
    high = wide.astype(jnp.bfloat16).astype(jnp.float32)
    parts[0] = high
    parts[1] = wide - high
    for k in range(CAP):
        col = tags[:, k : k + 1] & (COLS - 1)
        place[k * DEVICES : (k + 1) * DEVICES, :] = jnp.where(
            iota((DEVICES, COLS), 1) == col, 1.0, 0.0
        ).astype(jnp.bfloat16)
    group = 16

    def step(g, carry):
        total = None
        for part in range(PARTS):
            left = []
            for q in range(group):
                row = parts[part, pl.ds(g * group + q, 1), :]
                left.append(jnp.where(on_row, row, 0.0).astype(jnp.bfloat16))
            got = jnp.dot(
                jnp.concatenate(left, axis=0), place[...], preferred_element_type=jnp.float32
            )
            total = got if total is None else total + got
        out[pl.ds(pl.multiple_of(g * group * ROWS, 8), group * ROWS), :] = total
        return carry

    lax.fori_loop(0, PLANES // group, step, 0)


def forcing(slots, moment):
    return pl.pallas_call(
        functools.partial(forcing_kernel, moment),
        out_shape=f32(PLANES * ROWS, COLS),
        in_specs=[VMEM],
        out_specs=VMEM,
        scratch_shapes=[
            pltpu.VMEM((PARTS, PLANES, CAP * DEVICES), jnp.float32),
            pltpu.VMEM((CAP * DEVICES, COLS), jnp.bfloat16),
        ],
        compiler_params=params(16),
        cost_estimate=pl.CostEstimate(flops=8000000000, bytes_accessed=4325376, transcendentals=0),
        name=f"forcing_{moment}",
    )(slots)


QUARTER = PLANES * ROWS


def tile_rows(quarter, plane, block):
    return pl.ds(pl.multiple_of(quarter * QUARTER + plane * ROWS + block * 8, 8), 8)


PITCH = ROWS + 16


def wide_rows(quarter, plane, block, shift=0):
    start = (quarter * PLANES + plane) * PITCH + 8
    if shift:
        return pl.ds(start + shift + block * 8, 8)
    return pl.ds(pl.multiple_of(start + block * 8, 8), 8)


def edge_tiles(tile):
    def sides(block, carry):
        tile(block, 0)
        tile(block, 3)
        return carry

    def ends(end, carry):
        tile(end * (ROWS // 8 - 1), 1)
        tile(end * (ROWS // 8 - 1), 2)
        return carry

    lax.fori_loop(0, ROWS // 8, sides, 0, unroll=4)
    lax.fori_loop(0, 2, ends, 0)


def inner_tiles(tile):
    def step(block, carry):
        tile(block, 1)
        tile(block, 2)
        return carry

    lax.fori_loop(1, ROWS // 8 - 1, step, 0)


def eliminate(value, coupling, depth, at):
    links = []
    for k in range(LEVELS - 1):
        links.append(jnp.where(k + 1 < depth, coupling[at(k)], 0.0))
    ratio = []
    partial = [[], []]
    for k in range(LEVELS):
        pivot = jnp.float32(1.0)
        if k > 0:
            pivot = pivot + links[k - 1]
        if k < LEVELS - 1:
            pivot = pivot + links[k]
        if k > 0:
            pivot = pivot - links[k - 1] * ratio[k - 1]
        inverse = 1.0 / pivot
        for tracer in range(2):
            right = value(tracer * LEVELS + k)
            if k > 0:
                right = right + links[k - 1] * partial[tracer][k - 1]
            partial[tracer].append(right * inverse)
        if k < LEVELS - 1:
            ratio.append(links[k] * inverse)
    for k in range(LEVELS - 2, -1, -1):
        for tracer in range(2):
            partial[tracer][k] = partial[tracer][k] + ratio[k] * partial[tracer][k + 1]
    return partial


def solve_tile(value, coupling, scale, depth_ref, solved, weighted, sides, block, quarter):
    columns = slice(quarter * 128, (quarter + 1) * 128)

    def at(plane):
        return (pl.ds(pl.multiple_of(plane * ROWS + block * 8, 8), 8), columns)

    depth = depth_ref[pl.ds(pl.multiple_of(block * 8, 8), 8), columns]
    result = eliminate(value, coupling, depth, at)
    lane = iota((8, 128), 1)
    column = jnp.zeros((8, 128), jnp.float32)
    for k in range(LEVELS):
        weight = jnp.where(k < depth, scale[at(k)], 0.0)
        for tracer in range(2):
            plane = tracer * LEVELS + k
            found = result[tracer][k]
            heavy = weight * found
            solved[tile_rows(quarter, plane, block), :] = found
            weighted[wide_rows(quarter, plane, block), :] = heavy
            if quarter == 0:
                moved = heavy if plane == 0 else pltpu.roll(heavy, plane, 1)
                column = jnp.where(lane == plane, moved, column)
            if quarter == 3:
                column = jnp.where(lane == plane, pltpu.roll(heavy, plane + 1, 1), column)
    if quarter == 0:
        sides[pl.ds(pl.multiple_of(block * 8, 8), 8), :] = column
    if quarter == 3:
        sides[pl.ds(pl.multiple_of(ROWS + block * 8, 8), 8), :] = column


def send_edges(meta, weighted, sides, payload, first_row, last_row):
    sub = meta[13]
    payload[0] = jnp.transpose(sides[...])[:PLANES, :]
    for b in range(4):
        top = weighted[pl.ds(b * PLANES * PITCH + 8, PLANES, stride=PITCH), :]
        bottom = weighted[pl.ds(b * PLANES * PITCH + ROWS + 7, PLANES, stride=PITCH), :]
        payload[1 + b] = jnp.where(sub == N_SUB - 1, bottom, top)
        first_row[b] = top
        last_row[b] = bottom


BIG = (f32(4 * QUARTER, 128), f32(4 * PLANES * PITCH, 128))
EDGES = (f32(5, PLANES, 128), f32(4, PLANES, 128), f32(4, PLANES, 128))


def first_tile(adjoint, force, coupling, scale, depth, solved, weighted, sides):
    def tile(block, quarter):
        columns = slice(quarter * 128, (quarter + 1) * 128)

        def value(plane):
            at = (pl.ds(pl.multiple_of(plane * ROWS + block * 8, 8), 8), columns)
            return adjoint[at] + force[at]

        solve_tile(value, coupling, scale, depth, solved, weighted, sides, block, quarter)

    return tile


def first_edges_kernel(meta, adjoint, force, coupling, scale, depth, solved, weighted, payload,
                       first_row, last_row, sides):
    edge_tiles(first_tile(adjoint, force, coupling, scale, depth, solved, weighted, sides))
    send_edges(meta, weighted, sides, payload, first_row, last_row)


def first_inner_kernel(adjoint, force, coupling, scale, depth, _, __, solved, weighted):
    inner_tiles(first_tile(adjoint, force, coupling, scale, depth, solved, weighted, None))


SIDES = pltpu.VMEM((128, 128), jnp.float32)


def cost(flops):
    return pl.CostEstimate(flops=flops, bytes_accessed=10000000, transcendentals=0)


def first_edges(meta, *given):
    return pl.pallas_call(
        first_edges_kernel,
        out_shape=BIG + EDGES,
        in_specs=[SMEM] + [VMEM] * 5,
        out_specs=(VMEM,) * 5,
        scratch_shapes=[SIDES],
        compiler_params=params(8),
        cost_estimate=cost(30000000),
        name="first_edges",
    )(meta, *given)


def first_inner(solved, weighted, *given):
    return pl.pallas_call(
        first_inner_kernel,
        out_shape=BIG,
        in_specs=[VMEM] * 7,
        out_specs=(VMEM,) * 2,
        input_output_aliases={5: 0, 6: 1},
        compiler_params=params(4),
        cost_estimate=cost(20000000),
        name="first_inner",
    )(*given, solved, weighted)


SLOT_ROWS = PLANES + LEVELS


def route_kernel(meta, gathered, first_row, last_row, send, here):
    sub = meta[13]
    lane = iota((PLANES, 128), 1)

    def half(edge, dest, wanted):
        place, other_edge, turned = meta[3 * edge], meta[3 * edge + 1], meta[3 * edge + 2]
        chunk = jnp.where(turned == 1, N_SUB - 1 - dest, dest)
        block = jnp.where(other_edge < 2, 1 + (chunk >> 1), 0)
        side = jnp.where(other_edge < 2, chunk & 1, other_edge - 2)
        found = gathered[place, block]
        return jnp.where(side == wanted, found, pltpu.roll(found, 64, 1))

    for dest in range(N_SUB):
        send[dest, :PLANES, :] = jnp.where(lane < 64, half(2, dest, 0), half(3, dest, 1))
        send[dest, PLANES : PLANES + LEVELS, :] = jnp.zeros((LEVELS, 128), jnp.float32)
    for edge, dest in ((0, 0), (1, N_SUB - 1)):
        found = gathered[meta[3 * edge], 0]
        turned = pltpu.roll(found, 64, 1)
        low = jnp.where(meta[3 * edge + 1] == 2, found, turned)
        high = jnp.where(meta[3 * edge + 1] == 2, turned, found)
        send[dest, PLANES : PLANES + LEVELS, :] = jnp.where(
            lane[:LEVELS] < 64, low[:LEVELS], high[LEVELS:]
        )
    own = jnp.where(sub == N_SUB - 1, 1, 0)
    place_here = meta[3 * own]
    place_across = meta[3 * (1 - own)]
    for b in range(4):
        here[b] = gathered[place_here, 1 + b]
        across = gathered[place_across, 1 + b]
        first = first_row[b]
        last = last_row[b]
        for dest in range(N_SUB):
            if dest == 0:
                row = jnp.where(sub == N_SUB - 1, across, first)
            elif dest == N_SUB - 1:
                row = jnp.where(sub == 0, across, last)
            else:
                row = jnp.where(sub == dest - 1, last, first)
            send[dest, SLOT_ROWS + b * PLANES : SLOT_ROWS + (b + 1) * PLANES, :] = row


def route(meta, gathered, first_row, last_row):
    return pl.pallas_call(
        route_kernel,
        out_shape=(f32(N_SUB, SLOT_ROWS + 4 * PLANES, 128), f32(4, PLANES, 128)),
        in_specs=[SMEM] + [VMEM] * 3,
        out_specs=(VMEM,) * 2,
        compiler_params=params(8),
        cost_estimate=pl.CostEstimate(flops=1000000, bytes_accessed=1000000, transcendentals=0),
        name="route",
    )(meta, gathered, first_row, last_row)


def exchange(meta, depth, beside_z, beside_y, payload, first_row, last_row):
    def turn(k):
        return [
            (y * 8 + z * 2 + c, y * 8 + ((z + k) % 4) * 2 + c)
            for y in range(2)
            for z in range(4)
            for c in range(2)
        ]

    all_parts = payload[None]
    all_parts = jnp.concatenate(
        [all_parts] + [lax.ppermute(all_parts, "tile", turn(k)) for k in (1, 3, 2)], axis=0
    )
    all_parts, depth, *extra = lax.optimization_barrier((all_parts, depth, *beside_z()))
    all_parts = jnp.concatenate(
        [all_parts, lax.ppermute(all_parts, "tile", [(i, i ^ 8) for i in range(N_TILE)])], axis=0
    )
    extra = beside_y(depth, *extra)
    all_parts, *extra = lax.optimization_barrier((all_parts, *extra))
    all_parts = jnp.concatenate(
        [all_parts, lax.ppermute(all_parts, "tile", [(i, i ^ 1) for i in range(N_TILE)])], axis=0
    )
    send, here = route(meta, all_parts, first_row, last_row)
    got = lax.all_to_all(send, "sub", split_axis=0, concat_axis=0, tiled=True)
    return (got, here), extra


def place_halo(meta, got, here, weighted, strips):
    sub = meta[13]
    before = jnp.maximum(sub - 1, 0)
    after = jnp.minimum(sub + 1, N_SUB - 1)
    opposite = jnp.where(sub == 0, N_SUB - 1, 0)
    lane = iota((PLANES, 128), 1)

    def source(edge):
        other_edge, turned = meta[3 * edge + 1], meta[3 * edge + 2]
        same = jnp.where(turned == 1, N_SUB - 1 - sub, sub)
        return jnp.where(other_edge == 0, 0, jnp.where(other_edge == 1, N_SUB - 1, same))

    sides = jnp.where(lane < 64, got[source(2), :PLANES, :], got[source(3), :PLANES, :])
    to = iota((128, 128), 0)
    of = iota((128, 128), 1)
    turned = jnp.where(to < 64, meta[8], meta[11])
    wanted = jnp.where(turned == 1, (to & 64) + 63 - (to & 63), to)
    pick = jnp.where(of == wanted, 1.0, 0.0)
    strips[:, :PLANES] = lax.dot_general(
        pick, sides, (((1,), (1,)), ((), ())), precision=HIGHEST, preferred_element_type=jnp.float32
    )

    own = jnp.where(sub == N_SUB - 1, 1, 0)
    other_edge, turned = meta[3 * own + 1], meta[3 * own + 2]
    flip = jnp.where(of == jnp.where(turned == 1, 127 - to, to), 1.0, 0.0)
    row = []
    for b in range(4):
        part = slice(SLOT_ROWS + b * PLANES, SLOT_ROWS + (b + 1) * PLANES)
        even = got[2 * b, PLANES:SLOT_ROWS, :]
        odd = got[2 * b + 1, PLANES:SLOT_ROWS, :]
        joined = jnp.concatenate(
            [
                jnp.where(lane[:LEVELS] < 64, even, pltpu.roll(odd, 64, 1)),
                jnp.where(lane[:LEVELS] < 64, pltpu.roll(even, 64, 1), odd),
            ],
            axis=0,
        )
        joined = jnp.where(other_edge < 2, got[opposite, part, :], joined)
        row.append(jnp.where(other_edge == own, here[b], joined))
    for b in range(4):
        ordered = jnp.where(turned == 1, row[3 - b], row[b])
        strip = jnp.dot(ordered, flip, precision=HIGHEST, preferred_element_type=jnp.float32)
        at = b * PLANES * PITCH
        part = slice(SLOT_ROWS + b * PLANES, SLOT_ROWS + (b + 1) * PLANES)
        above_row = jnp.where(sub == 0, strip, got[before, part, :])
        below_row = jnp.where(sub == N_SUB - 1, strip, got[after, part, :])
        weighted[pl.ds(at + 7, PLANES, stride=PITCH), :] = above_row
        weighted[pl.ds(at + ROWS + 8, PLANES, stride=PITCH), :] = below_row


def stepped(solved, weighted, scale, depth_ref, strips, block, quarter):
    columns = slice(quarter * 128, (quarter + 1) * 128)
    lane = iota((8, 128), 1)
    here = pl.ds(pl.multiple_of(block * 8, 8), 8)
    depth = depth_ref[here, columns]
    if quarter == 0:
        west = strips[here, :]
    if quarter == 3:
        east = strips[pl.ds(pl.multiple_of(ROWS + block * 8, 8), 8), :]
    weights = {}

    def value(plane):
        level = plane % LEVELS
        if level not in weights:
            at = pl.ds(pl.multiple_of(level * ROWS + block * 8, 8), 8)
            weights[level] = jnp.where(level < depth, scale[at, columns], 0.0) * explicit_rate
        center = weighted[wide_rows(quarter, plane, block), :]
        total = weighted[wide_rows(quarter, plane, block, -1), :]
        total = total + weighted[wide_rows(quarter, plane, block, 1), :]
        if quarter == 0:
            edge = west if plane == 0 else pltpu.roll(west, 128 - plane, 1)
            total = total + jnp.where(lane == 0, edge, pltpu.roll(center, 1, 1))
        else:
            left = weighted[wide_rows(quarter - 1, plane, block), :]
            total = total + pltpu.roll(jnp.where(lane == 127, left, center), 1, 1)
        if quarter == 3:
            edge = pltpu.roll(east, 127 - plane, 1)
            total = total + jnp.where(lane == 127, edge, pltpu.roll(center, 127, 1))
        else:
            right = weighted[wide_rows(quarter + 1, plane, block), :]
            total = total + pltpu.roll(jnp.where(lane == 0, right, center), 127, 1)
        return solved[tile_rows(quarter, plane, block), :] + weights[level] * (
            total - 4.0 * center
        )

    return value


def second_tile(solved_in, weighted_in, force, coupling, scale, depth, solved, weighted, strips,
                sides):
    def tile(block, quarter):
        columns = slice(quarter * 128, (quarter + 1) * 128)
        late = stepped(solved_in, weighted_in, scale, depth, strips, block, quarter)

        def value(plane):
            at = (pl.ds(pl.multiple_of(plane * ROWS + block * 8, 8), 8), columns)
            return late(plane) + force[at]

        solve_tile(value, coupling, scale, depth, solved, weighted, sides, block, quarter)

    return tile


def second_inner_kernel(solved_in, weighted_in, force, coupling, scale, depth, solved, weighted):
    inner_tiles(
        second_tile(
            solved_in, weighted_in, force, coupling, scale, depth, solved, weighted, None, None
        )
    )


def second_edges_kernel(meta, got, here, solved_in, weighted_in, force, coupling, scale, depth, _,
                        __, solved, weighted, payload, first_row, last_row, weighted_late, sides,
                        strips, late):
    place_halo(meta, got, here, weighted_late, strips)

    def right_side(block, quarter):
        columns = slice(quarter * 128, (quarter + 1) * 128)
        value = stepped(solved_in, weighted_late, scale, depth, strips, block, quarter)
        for level in range(LEVELS):
            for plane in (level, LEVELS + level):
                at = (pl.ds(pl.multiple_of(plane * ROWS + block * 8, 8), 8), columns)
                late[at] = value(plane) + force[at]

    def solve(block, quarter):
        columns = slice(quarter * 128, (quarter + 1) * 128)

        def value(plane):
            return late[pl.ds(pl.multiple_of(plane * ROWS + block * 8, 8), 8), columns]

        solve_tile(value, coupling, scale, depth, solved, weighted, sides, block, quarter)

    edge_tiles(right_side)
    edge_tiles(solve)
    send_edges(meta, weighted, sides, payload, first_row, last_row)


def second_inner(*given):
    return pl.pallas_call(
        second_inner_kernel,
        out_shape=BIG,
        in_specs=[VMEM] * 6,
        out_specs=(VMEM,) * 2,
        compiler_params=params(4),
        cost_estimate=cost(30000000),
        name="second_inner",
    )(*given)


def second_edges(meta, halos, *given):
    return pl.pallas_call(
        second_edges_kernel,
        out_shape=BIG + EDGES + BIG[1:],
        in_specs=[SMEM] + [VMEM] * 10,
        out_specs=(VMEM,) * 6,
        input_output_aliases={9: 0, 10: 1, 4: 5},
        scratch_shapes=[SIDES] * 2 + [pltpu.VMEM((PLANES * ROWS, COLS), jnp.float32)],
        compiler_params=params(12),
        cost_estimate=cost(40000000),
        name="second_edges",
    )(meta, *halos, *given)


def last_tile(solved, weighted, scale, depth, strips, ready):
    def tile(block, quarter):
        columns = slice(quarter * 128, (quarter + 1) * 128)
        value = stepped(solved, weighted, scale, depth, strips, block, quarter)
        for level in range(LEVELS):
            for plane in (level, LEVELS + level):
                ready[plane, pl.ds(pl.multiple_of(block * 8, 8), 8), columns] = value(plane)

    return tile


INSIDE = (slice(8, ROWS - 8), slice(128, 384))
OUTSIDE = [
    (slice(0, ROWS), slice(0, 128)),
    (slice(0, ROWS), slice(384, 512)),
    (slice(0, 8), slice(128, 384)),
    (slice(ROWS - 8, ROWS), slice(128, 384)),
]


def last_inner_kernel(solved, weighted, scale, depth, out, ready, sems):
    inner_tiles(last_tile(solved, weighted, scale, depth, None, ready))
    rows, columns = INSIDE
    copy = pltpu.make_async_copy(
        ready.at[:, rows, columns], out.at[:, rows, columns], sems.at[0]
    )
    copy.start()
    copy.wait()


def last_edges_kernel(meta, got, here, solved, weighted_in, scale, depth, _, out, weighted, strips,
                      ready, sems):
    place_halo(meta, got, here, weighted, strips)
    tile = last_tile(solved, weighted, scale, depth, strips, ready)

    def copy(i):
        rows, columns = OUTSIDE[i]
        return pltpu.make_async_copy(
            ready.at[:, rows, columns], out.at[:, rows, columns], sems.at[i]
        )

    def column(quarter):
        def step(block, carry):
            tile(block, quarter)
            return carry

        lax.fori_loop(0, ROWS // 8, step, 0, unroll=4)

    column(0)
    copy(0).start()
    column(3)
    copy(1).start()
    for i, block in ((2, 0), (3, ROWS // 8 - 1)):
        tile(block, 1)
        tile(block, 2)
        copy(i).start()
    for i in range(4):
        copy(i).wait()


READY = [pltpu.VMEM((PLANES, ROWS, COLS), jnp.float32), pltpu.SemaphoreType.DMA((4,))]
ANY = pl.BlockSpec(memory_space=pl.ANY)


def last_inner(*given):
    return pl.pallas_call(
        last_inner_kernel,
        out_shape=f32(PLANES, ROWS, COLS),
        in_specs=[VMEM] * 4,
        out_specs=ANY,
        scratch_shapes=READY,
        compiler_params=params(6),
        cost_estimate=cost(20000000),
        name="last_inner",
    )(*given)


def last_edges(meta, halos, *given):
    return pl.pallas_call(
        last_edges_kernel,
        out_shape=(f32(PLANES, ROWS, COLS), BIG[1]),
        in_specs=[SMEM] + [VMEM] * 6 + [ANY],
        out_specs=(ANY, VMEM),
        input_output_aliases={7: 0, 4: 1},
        scratch_shapes=[SIDES] + READY,
        compiler_params=params(8),
        cost_estimate=cost(20000000),
        name="last_edges",
    )(meta, *halos, *given)[0]


def body(
    adjoint_final,
    diff_scale,
    vert_coupling,
    column_depth,
    seam_table,
    tile_owner,
    prof_face,
    prof_cell,
    prof_time,
    misfit,
):
    rows = prof_face.shape[0]
    slots, meta = pack(
        tile_owner,
        jnp.transpose(seam_table, (2, 1, 0)),
        prof_face.reshape(1, rows),
        prof_cell.reshape(1, rows),
        prof_time.reshape(1, rows),
        misfit.reshape(PLANES, rows),
    )
    slots = lax.all_to_all(slots, ("tile", "sub"), split_axis=0, concat_axis=0, tiled=True)
    adjoint = adjoint_final.reshape(PLANES * ROWS, COLS)
    scale = diff_scale.reshape(LEVELS * ROWS, COLS)
    coupling = vert_coupling.reshape((LEVELS - 1) * ROWS, COLS)
    late = forcing(slots, 1)
    given = (adjoint, late, coupling, scale, column_depth)
    solved, weighted, *edges = first_edges(meta, *given)

    def beside_z():
        return (forcing(slots, 0),)

    def beside_y(depth, early):
        whole = first_inner(solved, weighted, *given[:-1], depth)
        return *whole, early, *second_inner(*whole, early, coupling, scale, depth)

    halos, (solved, weighted, early, *begun) = exchange(
        meta, column_depth, beside_z, beside_y, *edges
    )
    solved, weighted, *edges, _ = second_edges(
        meta, halos, solved, weighted, early, coupling, scale, column_depth, *begun
    )
    halos, begun = exchange(
        meta,
        column_depth,
        lambda: (),
        lambda depth: (last_inner(solved, weighted, scale, depth),),
        *edges,
    )
    out = last_edges(meta, halos, solved, weighted, scale, column_depth, *begun)
    return out.reshape(adjoint_final.shape)


def solution(mesh):
    return jax.shard_map(
        body,
        mesh=mesh,
        in_specs=(
            P(None, None, ("tile", "sub"), None),
            P(None, ("tile", "sub"), None),
            P(None, ("tile", "sub"), None),
            P(("tile", "sub"), None),
            P(),
            P(),
            P(("tile", "sub")),
            P(("tile", "sub")),
            P(("tile", "sub")),
            P(None, None, ("tile", "sub")),
        ),
        out_specs=P(None, None, ("tile", "sub"), None),
        check_vma=False,
    )
```

```python
import functools

import jax
import jax.numpy as jnp
from jax import lax
from jax.experimental import pallas as pl
from jax.experimental.pallas import tpu as pltpu
from jax.sharding import PartitionSpec as P

CAP = 4
LEVELS = 16
PLANES = 2 * LEVELS
ROWS = 64
COLS = 512
CELLS = ROWS * COLS
N_TILE = 16
N_SUB = 8
DEVICES = N_TILE * N_SUB
FACES = 16
explicit_rate = 0.2
HIGHEST = lax.Precision.HIGHEST
VMEM = pl.BlockSpec(memory_space=pltpu.VMEM)
SMEM = pl.BlockSpec(memory_space=pltpu.SMEM)
META = 16
PARTS = 2


def iota(shape, axis):
    return lax.broadcasted_iota(jnp.int32, shape, axis)


def params(mib):
    return pltpu.CompilerParams(vmem_limit_bytes=mib * 1024 * 1024)


def f32(*shape):
    return jax.ShapeDtypeStruct(shape, jnp.float32)


def pack_kernel(owner_in, seam_in, face_in, cell_in, time_in, misfit_in, out, meta, owners, seams,
                face, cell, time, misfit, sems):
    copies = [
        pltpu.make_async_copy(source, target, sems.at[i])
        for i, (source, target) in enumerate(
            (
                (owner_in, owners),
                (seam_in, seams),
                (face_in, face),
                (cell_in, cell),
                (time_in, time),
                (misfit_in, misfit),
            )
        )
    ]
    for copy in copies:
        copy.start()
    for copy in copies:
        copy.wait()

    def owner(f):
        return owners[f]

    def seam(part, edge, f):
        return seams[part, edge, f]


    tile = lax.axis_index("tile")
    sub = lax.axis_index("sub")
    my_face = jnp.int32(0)
    for f in range(FACES):
        my_face = my_face + jnp.where(owner(f) == tile, f, 0)
    meta[12] = tile
    meta[13] = sub
    for edge in range(4):
        other = owner(seam(0, edge, my_face))
        steps = (((tile >> 1) & 3) + 4 - ((other >> 1) & 3)) & 3
        away = (
            ((other & 1) ^ (tile & 1)) * 8
            + (((other >> 3) & 1) ^ ((tile >> 3) & 1)) * 4
            + (steps ^ (steps >> 1))
        )
        meta[3 * edge] = away
        meta[3 * edge + 1] = seam(1, edge, my_face)
        meta[3 * edge + 2] = seam(2, edge, my_face)

    rows = face.shape[1]
    faces = face[...]
    home = jnp.zeros_like(faces)
    for f in range(FACES):
        home = jnp.where(faces == f, owner(f), home)
    cells = cell[...]
    tile_row = cells >> 9
    target = home * N_SUB + (tile_row >> 6)
    code = (time[...] - 1) * CELLS + (tile_row & (ROWS - 1)) * COLS + (cells & (COLS - 1))
    first = iota((rows, rows), 0)
    second = iota((rows, rows), 1)
    target_row = jnp.broadcast_to(target.astype(jnp.float32), (rows, rows))
    target_col = jnp.sum(jnp.where(first == second, target_row, 0.0), axis=1, keepdims=True)
    rank = jnp.sum(
        jnp.where((target_col == target_row) & (first < second), 1.0, 0.0), axis=0, keepdims=True
    )
    rank = rank.astype(jnp.int32)
    values = misfit[...]
    tag = code.astype(jnp.float32) + 1.0
    dest = iota((DEVICES, rows), 0)
    total = jnp.zeros((DEVICES, 2 * DEVICES), jnp.float32)
    for k in range(CAP):
        hit = jnp.where((dest == target) & (rank == k), 1.0, 0.0)
        pieces = []
        if k > 0:
            pieces.append(jnp.zeros((PLANES * k, rows), jnp.float32))
        pieces.append(values)
        if k < CAP - 1:
            pieces.append(jnp.zeros((PLANES * (CAP - 1 - k), rows), jnp.float32))
        pieces.append(jnp.where(dest == k, tag, 0.0))
        stacked = jnp.concatenate(pieces, axis=0)
        total = total + lax.dot_general(
            hit, stacked, (((1,), (1,)), ((), ())), precision=HIGHEST,
            preferred_element_type=jnp.float32,
        )
    out[:, 0, :] = total[:, :DEVICES]
    out[:, 1, :] = total[:, DEVICES:] - 1.0


def pack(owner, seam, face, cell, time, misfit):
    line = pltpu.VMEM(face.shape, jnp.int32)
    return pl.pallas_call(
        pack_kernel,
        out_shape=(f32(DEVICES, 2, DEVICES), jax.ShapeDtypeStruct((META,), jnp.int32)),
        in_specs=[pl.BlockSpec(memory_space=pl.ANY)] * 6,
        out_specs=(VMEM, SMEM),
        scratch_shapes=[
            pltpu.SMEM(owner.shape, jnp.int32),
            pltpu.SMEM(seam.shape, jnp.int32),
            line,
            line,
            line,
            pltpu.VMEM(misfit.shape, jnp.float32),
            pltpu.SemaphoreType.DMA((6,)),
        ],
        compiler_params=pltpu.CompilerParams(vmem_limit_bytes=66000000),
        name="pack",
    )(owner, seam, face, cell, time, misfit)


def forcing_kernel(moment, slots, out, parts, place):
    values = jnp.transpose(slots[:, 0, :])
    tags = (slots[:, 1, :] + 0.5).astype(jnp.int32)
    tags = jnp.where(slots[:, 1, :] < 0.0, -1, tags)
    tags_t = jnp.transpose(tags.astype(jnp.float32)).astype(jnp.int32)
    tag_row = jnp.concatenate([tags_t[k : k + 1, :] for k in range(CAP)], axis=1)
    valid = (tag_row >= moment * CELLS) & (tag_row < (moment + 1) * CELLS)
    row_of = jnp.where(valid, (tag_row & (CELLS - 1)) >> 9, -1)
    on_row = iota((ROWS, CAP * DEVICES), 0) == row_of
    wide = jnp.concatenate([values[PLANES * k : PLANES * (k + 1), :] for k in range(CAP)], axis=1)
    high = wide.astype(jnp.bfloat16).astype(jnp.float32)
    parts[0] = high
    parts[1] = wide - high
    for k in range(CAP):
        col = tags[:, k : k + 1] & (COLS - 1)
        place[k * DEVICES : (k + 1) * DEVICES, :] = jnp.where(
            iota((DEVICES, COLS), 1) == col, 1.0, 0.0
        ).astype(jnp.bfloat16)
    group = 16

    def step(g, carry):
        total = None
        for part in range(PARTS):
            left = []
            for q in range(group):
                row = parts[part, pl.ds(g * group + q, 1), :]
                left.append(jnp.where(on_row, row, 0.0).astype(jnp.bfloat16))
            got = jnp.dot(
                jnp.concatenate(left, axis=0), place[...], preferred_element_type=jnp.float32
            )
            total = got if total is None else total + got
        out[pl.ds(pl.multiple_of(g * group * ROWS, 8), group * ROWS), :] = total
        return carry

    lax.fori_loop(0, PLANES // group, step, 0)


def forcing(slots, moment):
    return pl.pallas_call(
        functools.partial(forcing_kernel, moment),
        out_shape=f32(PLANES * ROWS, COLS),
        in_specs=[VMEM],
        out_specs=VMEM,
        scratch_shapes=[
            pltpu.VMEM((PARTS, PLANES, CAP * DEVICES), jnp.float32),
            pltpu.VMEM((CAP * DEVICES, COLS), jnp.bfloat16),
        ],
        compiler_params=params(16),
        cost_estimate=pl.CostEstimate(flops=8000000000, bytes_accessed=4325376, transcendentals=0),
        name=f"forcing_{moment}",
    )(slots)


QUARTER = PLANES * ROWS


def tile_rows(quarter, plane, block):
    return pl.ds(pl.multiple_of(quarter * QUARTER + plane * ROWS + block * 8, 8), 8)


PITCH = ROWS + 16


def wide_rows(quarter, plane, block, shift=0):
    start = (quarter * PLANES + plane) * PITCH + 8
    if shift:
        return pl.ds(start + shift + block * 8, 8)
    return pl.ds(pl.multiple_of(start + block * 8, 8), 8)


def edge_tiles(tile):
    def sides(block, carry):
        tile(block, 0)
        tile(block, 3)
        return carry

    def ends(end, carry):
        tile(end * (ROWS // 8 - 1), 1)
        tile(end * (ROWS // 8 - 1), 2)
        return carry

    lax.fori_loop(0, ROWS // 8, sides, 0, unroll=4)
    lax.fori_loop(0, 2, ends, 0, unroll=2)


def inner_tiles(tile):
    def step(block, carry):
        tile(block, 1)
        tile(block, 2)
        return carry

    lax.fori_loop(1, ROWS // 8 - 1, step, 0)


def eliminate(value, coupling, depth, at):
    links = []
    for k in range(LEVELS - 1):
        links.append(jnp.where(k + 1 < depth, coupling[at(k)], 0.0))
    ratio = []
    partial = [[], []]
    for k in range(LEVELS):
        pivot = jnp.float32(1.0)
        if k > 0:
            pivot = pivot + links[k - 1]
        if k < LEVELS - 1:
            pivot = pivot + links[k]
        if k > 0:
            pivot = pivot - links[k - 1] * ratio[k - 1]
        inverse = 1.0 / pivot
        for tracer in range(2):
            right = value(tracer * LEVELS + k)
            if k > 0:
                right = right + links[k - 1] * partial[tracer][k - 1]
            partial[tracer].append(right * inverse)
        if k < LEVELS - 1:
            ratio.append(links[k] * inverse)
    for k in range(LEVELS - 2, -1, -1):
        for tracer in range(2):
            partial[tracer][k] = partial[tracer][k] + ratio[k] * partial[tracer][k + 1]
    return partial


def solve_tile(value, coupling, scale, depth_ref, solved, weighted, sides, block, quarter):
    columns = slice(quarter * 128, (quarter + 1) * 128)

    def at(plane):
        return (pl.ds(pl.multiple_of(plane * ROWS + block * 8, 8), 8), columns)

    depth = depth_ref[pl.ds(pl.multiple_of(block * 8, 8), 8), columns]
    result = eliminate(value, coupling, depth, at)
    lane = iota((8, 128), 1)
    column = jnp.zeros((8, 128), jnp.float32)
    for k in range(LEVELS):
        weight = jnp.where(k < depth, scale[at(k)], 0.0)
        for tracer in range(2):
            plane = tracer * LEVELS + k
            found = result[tracer][k]
            heavy = weight * found
            solved[tile_rows(quarter, plane, block), :] = found
            weighted[wide_rows(quarter, plane, block), :] = heavy
            if quarter == 0:
                moved = heavy if plane == 0 else pltpu.roll(heavy, plane, 1)
                column = jnp.where(lane == plane, moved, column)
            if quarter == 3:
                column = jnp.where(lane == plane, pltpu.roll(heavy, plane + 1, 1), column)
    if quarter == 0:
        sides[pl.ds(pl.multiple_of(block * 8, 8), 8), :] = column
    if quarter == 3:
        sides[pl.ds(pl.multiple_of(ROWS + block * 8, 8), 8), :] = column


def send_edges(meta, weighted, sides, payload, first_row, last_row):
    sub = meta[13]
    payload[0] = jnp.transpose(sides[...])[:PLANES, :]
    for b in range(4):
        top = weighted[pl.ds(b * PLANES * PITCH + 8, PLANES, stride=PITCH), :]
        bottom = weighted[pl.ds(b * PLANES * PITCH + ROWS + 7, PLANES, stride=PITCH), :]
        payload[1 + b] = jnp.where(sub == N_SUB - 1, bottom, top)
        first_row[b] = top
        last_row[b] = bottom


BIG = (f32(4 * QUARTER, 128), f32(4 * PLANES * PITCH, 128))
EDGES = (f32(5, PLANES, 128), f32(4, PLANES, 128), f32(4, PLANES, 128))


def first_tile(adjoint, force, coupling, scale, depth, solved, weighted, sides):
    def tile(block, quarter):
        columns = slice(quarter * 128, (quarter + 1) * 128)

        def value(plane):
            at = (pl.ds(pl.multiple_of(plane * ROWS + block * 8, 8), 8), columns)
            return adjoint[at] + force[at]

        solve_tile(value, coupling, scale, depth, solved, weighted, sides, block, quarter)

    return tile


def first_edges_kernel(meta, adjoint, force, coupling, scale, depth, solved, weighted, payload,
                       first_row, last_row, sides):
    edge_tiles(first_tile(adjoint, force, coupling, scale, depth, solved, weighted, sides))
    send_edges(meta, weighted, sides, payload, first_row, last_row)


def first_inner_kernel(adjoint, force, coupling, scale, depth, _, __, solved, weighted):
    inner_tiles(first_tile(adjoint, force, coupling, scale, depth, solved, weighted, None))


SIDES = pltpu.VMEM((128, 128), jnp.float32)


def cost(flops):
    return pl.CostEstimate(flops=flops, bytes_accessed=10000000, transcendentals=0)


def first_edges(meta, *given):
    return pl.pallas_call(
        first_edges_kernel,
        out_shape=BIG + EDGES,
        in_specs=[SMEM] + [VMEM] * 5,
        out_specs=(VMEM,) * 5,
        scratch_shapes=[SIDES],
        compiler_params=params(8),
        cost_estimate=cost(30000000),
        name="first_edges",
    )(meta, *given)


def first_inner(solved, weighted, *given):
    return pl.pallas_call(
        first_inner_kernel,
        out_shape=BIG,
        in_specs=[VMEM] * 7,
        out_specs=(VMEM,) * 2,
        input_output_aliases={5: 0, 6: 1},
        compiler_params=params(4),
        cost_estimate=cost(20000000),
        name="first_inner",
    )(*given, solved, weighted)


SLOT_ROWS = PLANES + LEVELS


def route_kernel(meta, gathered, first_row, last_row, send, here):
    sub = meta[13]
    lane = iota((PLANES, 128), 1)

    def half(edge, dest, wanted):
        place, other_edge, turned = meta[3 * edge], meta[3 * edge + 1], meta[3 * edge + 2]
        chunk = jnp.where(turned == 1, N_SUB - 1 - dest, dest)
        block = jnp.where(other_edge < 2, 1 + (chunk >> 1), 0)
        side = jnp.where(other_edge < 2, chunk & 1, other_edge - 2)
        found = gathered[place, block]
        return jnp.where(side == wanted, found, pltpu.roll(found, 64, 1))

    for dest in range(N_SUB):
        send[dest, :PLANES, :] = jnp.where(lane < 64, half(2, dest, 0), half(3, dest, 1))
        send[dest, PLANES : PLANES + LEVELS, :] = jnp.zeros((LEVELS, 128), jnp.float32)
    for edge, dest in ((0, 0), (1, N_SUB - 1)):
        found = gathered[meta[3 * edge], 0]
        turned = pltpu.roll(found, 64, 1)
        low = jnp.where(meta[3 * edge + 1] == 2, found, turned)
        high = jnp.where(meta[3 * edge + 1] == 2, turned, found)
        send[dest, PLANES : PLANES + LEVELS, :] = jnp.where(
            lane[:LEVELS] < 64, low[:LEVELS], high[LEVELS:]
        )
    own = jnp.where(sub == N_SUB - 1, 1, 0)
    place_here = meta[3 * own]
    place_across = meta[3 * (1 - own)]
    for b in range(4):
        here[b] = gathered[place_here, 1 + b]
        across = gathered[place_across, 1 + b]
        first = first_row[b]
        last = last_row[b]
        for dest in range(N_SUB):
            if dest == 0:
                row = jnp.where(sub == N_SUB - 1, across, first)
            elif dest == N_SUB - 1:
                row = jnp.where(sub == 0, across, last)
            else:
                row = jnp.where(sub == dest - 1, last, first)
            send[dest, SLOT_ROWS + b * PLANES : SLOT_ROWS + (b + 1) * PLANES, :] = row


def route(meta, gathered, first_row, last_row):
    return pl.pallas_call(
        route_kernel,
        out_shape=(f32(N_SUB, SLOT_ROWS + 4 * PLANES, 128), f32(4, PLANES, 128)),
        in_specs=[SMEM] + [VMEM] * 3,
        out_specs=(VMEM,) * 2,
        compiler_params=params(8),
        cost_estimate=pl.CostEstimate(flops=1000000, bytes_accessed=1000000, transcendentals=0),
        name="route",
    )(meta, gathered, first_row, last_row)


def exchange(meta, depth, beside_z, beside_y, payload, first_row, last_row):
    def turn(k):
        return [
            (y * 8 + z * 2 + c, y * 8 + ((z + k) % 4) * 2 + c)
            for y in range(2)
            for z in range(4)
            for c in range(2)
        ]

    all_parts = payload[None]
    all_parts = jnp.concatenate(
        [all_parts] + [lax.ppermute(all_parts, "tile", turn(k)) for k in (1, 3, 2)], axis=0
    )
    all_parts, depth, *extra = lax.optimization_barrier((all_parts, depth, *beside_z()))
    all_parts = jnp.concatenate(
        [all_parts, lax.ppermute(all_parts, "tile", [(i, i ^ 8) for i in range(N_TILE)])], axis=0
    )
    extra = beside_y(depth, *extra)
    all_parts, *extra = lax.optimization_barrier((all_parts, *extra))
    all_parts = jnp.concatenate(
        [all_parts, lax.ppermute(all_parts, "tile", [(i, i ^ 1) for i in range(N_TILE)])], axis=0
    )
    send, here = route(meta, all_parts, first_row, last_row)
    got = lax.all_to_all(send, "sub", split_axis=0, concat_axis=0, tiled=True)
    return (got, here), extra


def place_halo(meta, got, here, weighted, strips):
    sub = meta[13]
    before = jnp.maximum(sub - 1, 0)
    after = jnp.minimum(sub + 1, N_SUB - 1)
    opposite = jnp.where(sub == 0, N_SUB - 1, 0)
    lane = iota((PLANES, 128), 1)

    def source(edge):
        other_edge, turned = meta[3 * edge + 1], meta[3 * edge + 2]
        same = jnp.where(turned == 1, N_SUB - 1 - sub, sub)
        return jnp.where(other_edge == 0, 0, jnp.where(other_edge == 1, N_SUB - 1, same))

    sides = jnp.where(lane < 64, got[source(2), :PLANES, :], got[source(3), :PLANES, :])
    to = iota((128, 128), 0)
    of = iota((128, 128), 1)
    turned = jnp.where(to < 64, meta[8], meta[11])
    wanted = jnp.where(turned == 1, (to & 64) + 63 - (to & 63), to)
    pick = jnp.where(of == wanted, 1.0, 0.0)
    strips[:, :PLANES] = lax.dot_general(
        pick, sides, (((1,), (1,)), ((), ())), precision=HIGHEST, preferred_element_type=jnp.float32
    )

    own = jnp.where(sub == N_SUB - 1, 1, 0)
    other_edge, turned = meta[3 * own + 1], meta[3 * own + 2]
    flip = jnp.where(of == jnp.where(turned == 1, 127 - to, to), 1.0, 0.0)
    row = []
    for b in range(4):
        part = slice(SLOT_ROWS + b * PLANES, SLOT_ROWS + (b + 1) * PLANES)
        even = got[2 * b, PLANES:SLOT_ROWS, :]
        odd = got[2 * b + 1, PLANES:SLOT_ROWS, :]
        joined = jnp.concatenate(
            [
                jnp.where(lane[:LEVELS] < 64, even, pltpu.roll(odd, 64, 1)),
                jnp.where(lane[:LEVELS] < 64, pltpu.roll(even, 64, 1), odd),
            ],
            axis=0,
        )
        joined = jnp.where(other_edge < 2, got[opposite, part, :], joined)
        row.append(jnp.where(other_edge == own, here[b], joined))
    ordered = [jnp.where(turned == 1, row[3 - b], row[b]) for b in range(4)]
    strips_in_order = jnp.dot(
        jnp.concatenate(ordered, axis=0),
        flip,
        precision=HIGHEST,
        preferred_element_type=jnp.float32,
    )
    for b in range(4):
        strip = strips_in_order[b * PLANES : (b + 1) * PLANES]
        at = b * PLANES * PITCH
        part = slice(SLOT_ROWS + b * PLANES, SLOT_ROWS + (b + 1) * PLANES)
        above_row = jnp.where(sub == 0, strip, got[before, part, :])
        below_row = jnp.where(sub == N_SUB - 1, strip, got[after, part, :])
        weighted[pl.ds(at + 7, PLANES, stride=PITCH), :] = above_row
        weighted[pl.ds(at + ROWS + 8, PLANES, stride=PITCH), :] = below_row


def stepped(solved, weighted, scale, depth_ref, strips, block, quarter):
    columns = slice(quarter * 128, (quarter + 1) * 128)
    lane = iota((8, 128), 1)
    here = pl.ds(pl.multiple_of(block * 8, 8), 8)
    depth = depth_ref[here, columns]
    if quarter == 0:
        west = strips[here, :]
    if quarter == 3:
        east = strips[pl.ds(pl.multiple_of(ROWS + block * 8, 8), 8), :]
    weights = {}

    def value(plane):
        level = plane % LEVELS
        if level not in weights:
            at = pl.ds(pl.multiple_of(level * ROWS + block * 8, 8), 8)
            weights[level] = jnp.where(level < depth, scale[at, columns], 0.0) * explicit_rate
        center = weighted[wide_rows(quarter, plane, block), :]
        total = weighted[wide_rows(quarter, plane, block, -1), :]
        total = total + weighted[wide_rows(quarter, plane, block, 1), :]
        if quarter == 0:
            edge = west if plane == 0 else pltpu.roll(west, 128 - plane, 1)
            total = total + jnp.where(lane == 0, edge, pltpu.roll(center, 1, 1))
        else:
            left = weighted[wide_rows(quarter - 1, plane, block), :]
            total = total + pltpu.roll(jnp.where(lane == 127, left, center), 1, 1)
        if quarter == 3:
            edge = pltpu.roll(east, 127 - plane, 1)
            total = total + jnp.where(lane == 127, edge, pltpu.roll(center, 127, 1))
        else:
            right = weighted[wide_rows(quarter + 1, plane, block), :]
            total = total + pltpu.roll(jnp.where(lane == 0, right, center), 127, 1)
        return solved[tile_rows(quarter, plane, block), :] + weights[level] * (
            total - 4.0 * center
        )

    return value


def second_tile(solved_in, weighted_in, force, coupling, scale, depth, solved, weighted, strips,
                sides):
    def tile(block, quarter):
        columns = slice(quarter * 128, (quarter + 1) * 128)
        late = stepped(solved_in, weighted_in, scale, depth, strips, block, quarter)

        def value(plane):
            at = (pl.ds(pl.multiple_of(plane * ROWS + block * 8, 8), 8), columns)
            return late(plane) + force[at]

        solve_tile(value, coupling, scale, depth, solved, weighted, sides, block, quarter)

    return tile


def second_inner_kernel(solved_in, weighted_in, force, coupling, scale, depth, solved, weighted):
    inner_tiles(
        second_tile(
            solved_in, weighted_in, force, coupling, scale, depth, solved, weighted, None, None
        )
    )


def second_edges_kernel(meta, got, here, solved_in, weighted_in, force, coupling, scale, depth, _,
                        __, solved, weighted, payload, first_row, last_row, weighted_late, sides,
                        strips, late):
    place_halo(meta, got, here, weighted_late, strips)

    def right_side(block, quarter):
        columns = slice(quarter * 128, (quarter + 1) * 128)
        value = stepped(solved_in, weighted_late, scale, depth, strips, block, quarter)
        for level in range(LEVELS):
            for plane in (level, LEVELS + level):
                at = (pl.ds(pl.multiple_of(plane * ROWS + block * 8, 8), 8), columns)
                late[at] = value(plane) + force[at]

    def solve(block, quarter):
        columns = slice(quarter * 128, (quarter + 1) * 128)

        def value(plane):
            return late[pl.ds(pl.multiple_of(plane * ROWS + block * 8, 8), 8), columns]

        solve_tile(value, coupling, scale, depth, solved, weighted, sides, block, quarter)

    edge_tiles(right_side)
    edge_tiles(solve)
    send_edges(meta, weighted, sides, payload, first_row, last_row)


def second_inner(*given):
    return pl.pallas_call(
        second_inner_kernel,
        out_shape=BIG,
        in_specs=[VMEM] * 6,
        out_specs=(VMEM,) * 2,
        compiler_params=params(4),
        cost_estimate=cost(30000000),
        name="second_inner",
    )(*given)


def second_edges(meta, halos, *given):
    return pl.pallas_call(
        second_edges_kernel,
        out_shape=BIG + EDGES + BIG[1:],
        in_specs=[SMEM] + [VMEM] * 10,
        out_specs=(VMEM,) * 6,
        input_output_aliases={9: 0, 10: 1, 4: 5},
        scratch_shapes=[SIDES] * 2 + [pltpu.VMEM((PLANES * ROWS, COLS), jnp.float32)],
        compiler_params=params(12),
        cost_estimate=cost(40000000),
        name="second_edges",
    )(meta, *halos, *given)


def last_tile(solved, weighted, scale, depth, strips, ready):
    def tile(block, quarter):
        columns = slice(quarter * 128, (quarter + 1) * 128)
        value = stepped(solved, weighted, scale, depth, strips, block, quarter)
        for level in range(LEVELS):
            for plane in (level, LEVELS + level):
                ready[plane, pl.ds(pl.multiple_of(block * 8, 8), 8), columns] = value(plane)

    return tile


INSIDE = (slice(8, ROWS - 8), slice(128, 384))
OUTSIDE = [
    (slice(0, ROWS), slice(0, 128)),
    (slice(0, ROWS), slice(384, 512)),
    (slice(0, 8), slice(128, 384)),
    (slice(ROWS - 8, ROWS), slice(128, 384)),
]


def last_inner_kernel(solved, weighted, scale, depth, out, ready, sems):
    inner_tiles(last_tile(solved, weighted, scale, depth, None, ready))
    rows, columns = INSIDE
    copy = pltpu.make_async_copy(
        ready.at[:, rows, columns], out.at[:, rows, columns], sems.at[0]
    )
    copy.start()
    copy.wait()


def last_edges_kernel(meta, got, here, solved, weighted_in, scale, depth, _, out, weighted, strips,
                      ready, sems):
    place_halo(meta, got, here, weighted, strips)
    tile = last_tile(solved, weighted, scale, depth, strips, ready)

    def copy(i):
        rows, columns = OUTSIDE[i]
        return pltpu.make_async_copy(
            ready.at[:, rows, columns], out.at[:, rows, columns], sems.at[i]
        )

    def column(quarter):
        def step(block, carry):
            tile(block, quarter)
            return carry

        lax.fori_loop(0, ROWS // 8, step, 0, unroll=4)

    column(0)
    copy(0).start()
    column(3)
    copy(1).start()
    for i, block in ((2, 0), (3, ROWS // 8 - 1)):
        tile(block, 1)
        tile(block, 2)
        copy(i).start()
    for i in range(4):
        copy(i).wait()


READY = [pltpu.VMEM((PLANES, ROWS, COLS), jnp.float32), pltpu.SemaphoreType.DMA((4,))]
ANY = pl.BlockSpec(memory_space=pl.ANY)


def last_inner(*given):
    return pl.pallas_call(
        last_inner_kernel,
        out_shape=f32(PLANES, ROWS, COLS),
        in_specs=[VMEM] * 4,
        out_specs=ANY,
        scratch_shapes=READY,
        compiler_params=params(6),
        cost_estimate=cost(20000000),
        name="last_inner",
    )(*given)


def last_edges(meta, halos, *given):
    return pl.pallas_call(
        last_edges_kernel,
        out_shape=(f32(PLANES, ROWS, COLS), BIG[1]),
        in_specs=[SMEM] + [VMEM] * 6 + [ANY],
        out_specs=(ANY, VMEM),
        input_output_aliases={7: 0, 4: 1},
        scratch_shapes=[SIDES] + READY,
        compiler_params=params(8),
        cost_estimate=cost(20000000),
        name="last_edges",
    )(meta, *halos, *given)[0]


def body(
    adjoint_final,
    diff_scale,
    vert_coupling,
    column_depth,
    seam_table,
    tile_owner,
    prof_face,
    prof_cell,
    prof_time,
    misfit,
):
    rows = prof_face.shape[0]
    slots, meta = pack(
        tile_owner,
        jnp.transpose(seam_table, (2, 1, 0)),
        prof_face.reshape(1, rows),
        prof_cell.reshape(1, rows),
        prof_time.reshape(1, rows),
        misfit.reshape(PLANES, rows),
    )
    slots = lax.all_to_all(slots, ("tile", "sub"), split_axis=0, concat_axis=0, tiled=True)
    adjoint = adjoint_final.reshape(PLANES * ROWS, COLS)
    scale = diff_scale.reshape(LEVELS * ROWS, COLS)
    coupling = vert_coupling.reshape((LEVELS - 1) * ROWS, COLS)
    late = forcing(slots, 1)
    given = (adjoint, late, coupling, scale, column_depth)
    solved, weighted, *edges = first_edges(meta, *given)

    def beside_z():
        return (forcing(slots, 0),)

    def beside_y(depth, early):
        whole = first_inner(solved, weighted, *given[:-1], depth)
        return *whole, early, *second_inner(*whole, early, coupling, scale, depth)

    halos, (solved, weighted, early, *begun) = exchange(
        meta, column_depth, beside_z, beside_y, *edges
    )
    solved, weighted, *edges, _ = second_edges(
        meta, halos, solved, weighted, early, coupling, scale, column_depth, *begun
    )
    halos, begun = exchange(
        meta,
        column_depth,
        lambda: (),
        lambda depth: (last_inner(solved, weighted, scale, depth),),
        *edges,
    )
    out = last_edges(meta, halos, solved, weighted, scale, column_depth, *begun)
    return out.reshape(adjoint_final.shape)


def solution(mesh):
    return jax.shard_map(
        body,
        mesh=mesh,
        in_specs=(
            P(None, None, ("tile", "sub"), None),
            P(None, ("tile", "sub"), None),
            P(None, ("tile", "sub"), None),
            P(("tile", "sub"), None),
            P(),
            P(),
            P(("tile", "sub")),
            P(("tile", "sub")),
            P(("tile", "sub")),
            P(None, None, ("tile", "sub")),
        ),
        out_specs=P(None, None, ("tile", "sub"), None),
        check_vma=False,
    )
```

```python
import functools

import jax
import jax.numpy as jnp
from jax import lax
from jax.experimental import pallas as pl
from jax.experimental.pallas import tpu as pltpu
from jax.sharding import PartitionSpec as P

CAP = 4
LEVELS = 16
PLANES = 2 * LEVELS
ROWS = 64
COLS = 512
CELLS = ROWS * COLS
N_TILE = 16
N_SUB = 8
DEVICES = N_TILE * N_SUB
FACES = 16
explicit_rate = 0.2
HIGHEST = lax.Precision.HIGHEST
VMEM = pl.BlockSpec(memory_space=pltpu.VMEM)
SMEM = pl.BlockSpec(memory_space=pltpu.SMEM)
META = 16
PARTS = 2


def iota(shape, axis):
    return lax.broadcasted_iota(jnp.int32, shape, axis)


def params(mib):
    return pltpu.CompilerParams(vmem_limit_bytes=mib * 1024 * 1024)


def f32(*shape):
    return jax.ShapeDtypeStruct(shape, jnp.float32)


def pack_kernel(owner_in, seam_in, face_in, cell_in, time_in, misfit_in, out, meta, owners, seams,
                face, cell, time, misfit, sems):
    copies = [
        pltpu.make_async_copy(source, target, sems.at[i])
        for i, (source, target) in enumerate(
            (
                (owner_in, owners),
                (seam_in, seams),
                (face_in, face),
                (cell_in, cell),
                (time_in, time),
                (misfit_in, misfit),
            )
        )
    ]
    for copy in copies:
        copy.start()
    for copy in copies:
        copy.wait()

    def owner(f):
        return owners[f]

    def seam(part, edge, f):
        return seams[part, edge, f]


    tile = lax.axis_index("tile")
    sub = lax.axis_index("sub")
    my_face = jnp.int32(0)
    for f in range(FACES):
        my_face = my_face + jnp.where(owner(f) == tile, f, 0)
    meta[12] = tile
    meta[13] = sub
    for edge in range(4):
        other = owner(seam(0, edge, my_face))
        steps = (((tile >> 1) & 3) + 4 - ((other >> 1) & 3)) & 3
        away = (
            ((other & 1) ^ (tile & 1)) * 8
            + (((other >> 3) & 1) ^ ((tile >> 3) & 1)) * 4
            + (steps ^ (steps >> 1))
        )
        meta[3 * edge] = away
        meta[3 * edge + 1] = seam(1, edge, my_face)
        meta[3 * edge + 2] = seam(2, edge, my_face)

    rows = face.shape[1]
    faces = face[...]
    home = jnp.zeros_like(faces)
    for f in range(FACES):
        home = jnp.where(faces == f, owner(f), home)
    cells = cell[...]
    tile_row = cells >> 9
    target = home * N_SUB + (tile_row >> 6)
    code = (time[...] - 1) * CELLS + (tile_row & (ROWS - 1)) * COLS + (cells & (COLS - 1))
    first = iota((rows, rows), 0)
    second = iota((rows, rows), 1)
    target_row = jnp.broadcast_to(target.astype(jnp.float32), (rows, rows))
    target_col = jnp.sum(jnp.where(first == second, target_row, 0.0), axis=1, keepdims=True)
    rank = jnp.sum(
        jnp.where((target_col == target_row) & (first < second), 1.0, 0.0), axis=0, keepdims=True
    )
    rank = rank.astype(jnp.int32)
    values = misfit[...]
    tag = code.astype(jnp.float32) + 1.0
    dest = iota((DEVICES, rows), 0)
    total = jnp.zeros((DEVICES, 2 * DEVICES), jnp.float32)
    for k in range(CAP):
        hit = jnp.where((dest == target) & (rank == k), 1.0, 0.0)
        pieces = []
        if k > 0:
            pieces.append(jnp.zeros((PLANES * k, rows), jnp.float32))
        pieces.append(values)
        if k < CAP - 1:
            pieces.append(jnp.zeros((PLANES * (CAP - 1 - k), rows), jnp.float32))
        pieces.append(jnp.where(dest == k, tag, 0.0))
        stacked = jnp.concatenate(pieces, axis=0)
        total = total + lax.dot_general(
            hit, stacked, (((1,), (1,)), ((), ())), precision=HIGHEST,
            preferred_element_type=jnp.float32,
        )
    out[:, 0, :] = total[:, :DEVICES]
    out[:, 1, :] = total[:, DEVICES:] - 1.0


def pack(owner, seam, face, cell, time, misfit):
    line = pltpu.VMEM(face.shape, jnp.int32)
    return pl.pallas_call(
        pack_kernel,
        out_shape=(f32(DEVICES, 2, DEVICES), jax.ShapeDtypeStruct((META,), jnp.int32)),
        in_specs=[pl.BlockSpec(memory_space=pl.ANY)] * 6,
        out_specs=(VMEM, SMEM),
        scratch_shapes=[
            pltpu.SMEM(owner.shape, jnp.int32),
            pltpu.SMEM(seam.shape, jnp.int32),
            line,
            line,
            line,
            pltpu.VMEM(misfit.shape, jnp.float32),
            pltpu.SemaphoreType.DMA((6,)),
        ],
        compiler_params=pltpu.CompilerParams(vmem_limit_bytes=66000000),
        name="pack",
    )(owner, seam, face, cell, time, misfit)


def forcing_kernel(moment, slots, out, parts, place):
    values = jnp.transpose(slots[:, 0, :])
    tags = (slots[:, 1, :] + 0.5).astype(jnp.int32)
    tags = jnp.where(slots[:, 1, :] < 0.0, -1, tags)
    tags_t = jnp.transpose(tags.astype(jnp.float32)).astype(jnp.int32)
    tag_row = jnp.concatenate([tags_t[k : k + 1, :] for k in range(CAP)], axis=1)
    valid = (tag_row >= moment * CELLS) & (tag_row < (moment + 1) * CELLS)
    row_of = jnp.where(valid, (tag_row & (CELLS - 1)) >> 9, -1)
    on_row = iota((ROWS, CAP * DEVICES), 0) == row_of
    wide = jnp.concatenate([values[PLANES * k : PLANES * (k + 1), :] for k in range(CAP)], axis=1)
    high = wide.astype(jnp.bfloat16).astype(jnp.float32)
    parts[0] = high
    parts[1] = wide - high
    for k in range(CAP):
        col = tags[:, k : k + 1] & (COLS - 1)
        place[k * DEVICES : (k + 1) * DEVICES, :] = jnp.where(
            iota((DEVICES, COLS), 1) == col, 1.0, 0.0
        ).astype(jnp.bfloat16)
    group = 16

    def step(g, carry):
        total = None
        for part in range(PARTS):
            left = []
            for q in range(group):
                row = parts[part, pl.ds(g * group + q, 1), :]
                left.append(jnp.where(on_row, row, 0.0).astype(jnp.bfloat16))
            got = jnp.dot(
                jnp.concatenate(left, axis=0), place[...], preferred_element_type=jnp.float32
            )
            total = got if total is None else total + got
        out[pl.ds(pl.multiple_of(g * group * ROWS, 8), group * ROWS), :] = total
        return carry

    lax.fori_loop(0, PLANES // group, step, 0)


def forcing(slots, moment):
    return pl.pallas_call(
        functools.partial(forcing_kernel, moment),
        out_shape=f32(PLANES * ROWS, COLS),
        in_specs=[VMEM],
        out_specs=VMEM,
        scratch_shapes=[
            pltpu.VMEM((PARTS, PLANES, CAP * DEVICES), jnp.float32),
            pltpu.VMEM((CAP * DEVICES, COLS), jnp.bfloat16),
        ],
        compiler_params=params(16),
        cost_estimate=pl.CostEstimate(flops=8000000000, bytes_accessed=4325376, transcendentals=0),
        name=f"forcing_{moment}",
    )(slots)


QUARTER = PLANES * ROWS


def tile_rows(quarter, plane, block):
    return pl.ds(pl.multiple_of(quarter * QUARTER + plane * ROWS + block * 8, 8), 8)


PITCH = ROWS + 16


def wide_rows(quarter, plane, block, shift=0):
    start = (quarter * PLANES + plane) * PITCH + 8
    if shift:
        return pl.ds(start + shift + block * 8, 8)
    return pl.ds(pl.multiple_of(start + block * 8, 8), 8)


def edge_tiles(tile):
    def sides(block, carry):
        tile(block, 0)
        tile(block, 3)
        return carry

    def ends(end, carry):
        tile(end * (ROWS // 8 - 1), 1)
        tile(end * (ROWS // 8 - 1), 2)
        return carry

    lax.fori_loop(0, ROWS // 8, sides, 0, unroll=4)
    lax.fori_loop(0, 2, ends, 0, unroll=2)


def inner_tiles(tile):
    def step(block, carry):
        tile(block, 1)
        tile(block, 2)
        return carry

    lax.fori_loop(1, ROWS // 8 - 1, step, 0)


def eliminate(value, coupling, depth, at):
    links = []
    for k in range(LEVELS - 1):
        links.append(jnp.where(k + 1 < depth, coupling[at(k)], 0.0))
    ratio = []
    partial = [[], []]
    for k in range(LEVELS):
        pivot = jnp.float32(1.0)
        if k > 0:
            pivot = pivot + links[k - 1]
        if k < LEVELS - 1:
            pivot = pivot + links[k]
        if k > 0:
            pivot = pivot - links[k - 1] * ratio[k - 1]
        inverse = 1.0 / pivot
        for tracer in range(2):
            right = value(tracer * LEVELS + k)
            if k > 0:
                right = right + links[k - 1] * partial[tracer][k - 1]
            partial[tracer].append(right * inverse)
        if k < LEVELS - 1:
            ratio.append(links[k] * inverse)
    for k in range(LEVELS - 2, -1, -1):
        for tracer in range(2):
            partial[tracer][k] = partial[tracer][k] + ratio[k] * partial[tracer][k + 1]
    return partial


def solve_tile(value, coupling, scale, depth_ref, solved, weighted, sides, block, quarter):
    columns = slice(quarter * 128, (quarter + 1) * 128)

    def at(plane):
        return (pl.ds(pl.multiple_of(plane * ROWS + block * 8, 8), 8), columns)

    depth = depth_ref[pl.ds(pl.multiple_of(block * 8, 8), 8), columns]
    result = eliminate(value, coupling, depth, at)
    lane = iota((8, 128), 1)
    column = jnp.zeros((8, 128), jnp.float32)
    for k in range(LEVELS):
        weight = jnp.where(k < depth, scale[at(k)], 0.0)
        for tracer in range(2):
            plane = tracer * LEVELS + k
            found = result[tracer][k]
            heavy = weight * found
            solved[tile_rows(quarter, plane, block), :] = found
            weighted[wide_rows(quarter, plane, block), :] = heavy
            if quarter == 0:
                moved = heavy if plane == 0 else pltpu.roll(heavy, plane, 1)
                column = jnp.where(lane == plane, moved, column)
            if quarter == 3:
                column = jnp.where(lane == plane, pltpu.roll(heavy, plane + 1, 1), column)
    if quarter == 0:
        sides[pl.ds(pl.multiple_of(block * 8, 8), 8), :] = column
    if quarter == 3:
        sides[pl.ds(pl.multiple_of(ROWS + block * 8, 8), 8), :] = column


def send_edges(meta, weighted, sides, payload, first_row, last_row):
    sub = meta[13]
    payload[0] = jnp.transpose(sides[...])[:PLANES, :]
    for b in range(4):
        top = weighted[pl.ds(b * PLANES * PITCH + 8, PLANES, stride=PITCH), :]
        bottom = weighted[pl.ds(b * PLANES * PITCH + ROWS + 7, PLANES, stride=PITCH), :]
        payload[1 + b] = jnp.where(sub == N_SUB - 1, bottom, top)
        first_row[b] = top
        last_row[b] = bottom


BIG = (f32(4 * QUARTER, 128), f32(4 * PLANES * PITCH, 128))
EDGES = (f32(5, PLANES, 128), f32(4, PLANES, 128), f32(4, PLANES, 128))


def first_tile(adjoint, force, coupling, scale, depth, solved, weighted, sides):
    def tile(block, quarter):
        columns = slice(quarter * 128, (quarter + 1) * 128)

        def value(plane):
            at = (pl.ds(pl.multiple_of(plane * ROWS + block * 8, 8), 8), columns)
            return adjoint[at] + force[at]

        solve_tile(value, coupling, scale, depth, solved, weighted, sides, block, quarter)

    return tile


def first_edges_kernel(meta, adjoint, force, coupling, scale, depth, solved, weighted, payload,
                       first_row, last_row, sides):
    edge_tiles(first_tile(adjoint, force, coupling, scale, depth, solved, weighted, sides))
    send_edges(meta, weighted, sides, payload, first_row, last_row)


def first_inner_kernel(adjoint, force, coupling, scale, depth, _, __, solved, weighted):
    inner_tiles(first_tile(adjoint, force, coupling, scale, depth, solved, weighted, None))


SIDES = pltpu.VMEM((128, 128), jnp.float32)


def cost(flops):
    return pl.CostEstimate(flops=flops, bytes_accessed=10000000, transcendentals=0)


def first_edges(meta, *given):
    return pl.pallas_call(
        first_edges_kernel,
        out_shape=BIG + EDGES,
        in_specs=[SMEM] + [VMEM] * 5,
        out_specs=(VMEM,) * 5,
        scratch_shapes=[SIDES],
        compiler_params=params(8),
        cost_estimate=cost(30000000),
        name="first_edges",
    )(meta, *given)


def first_inner(solved, weighted, *given):
    return pl.pallas_call(
        first_inner_kernel,
        out_shape=BIG,
        in_specs=[VMEM] * 7,
        out_specs=(VMEM,) * 2,
        input_output_aliases={5: 0, 6: 1},
        compiler_params=params(4),
        cost_estimate=cost(20000000),
        name="first_inner",
    )(*given, solved, weighted)


SLOT_ROWS = PLANES + LEVELS


def route_kernel(meta, gathered, first_row, last_row, send, here):
    sub = meta[13]
    lane = iota((PLANES, 128), 1)

    def half(edge, dest, wanted):
        place, other_edge, turned = meta[3 * edge], meta[3 * edge + 1], meta[3 * edge + 2]
        chunk = jnp.where(turned == 1, N_SUB - 1 - dest, dest)
        block = jnp.where(other_edge < 2, 1 + (chunk >> 1), 0)
        side = jnp.where(other_edge < 2, chunk & 1, other_edge - 2)
        found = gathered[place, block]
        return jnp.where(side == wanted, found, pltpu.roll(found, 64, 1))

    for dest in range(N_SUB):
        send[dest, :PLANES, :] = jnp.where(lane < 64, half(2, dest, 0), half(3, dest, 1))
        send[dest, PLANES : PLANES + LEVELS, :] = jnp.zeros((LEVELS, 128), jnp.float32)
    for edge, dest in ((0, 0), (1, N_SUB - 1)):
        found = gathered[meta[3 * edge], 0]
        turned = pltpu.roll(found, 64, 1)
        low = jnp.where(meta[3 * edge + 1] == 2, found, turned)
        high = jnp.where(meta[3 * edge + 1] == 2, turned, found)
        send[dest, PLANES : PLANES + LEVELS, :] = jnp.where(
            lane[:LEVELS] < 64, low[:LEVELS], high[LEVELS:]
        )
    own = jnp.where(sub == N_SUB - 1, 1, 0)
    place_here = meta[3 * own]
    place_across = meta[3 * (1 - own)]
    for b in range(4):
        here[b] = gathered[place_here, 1 + b]
        across = gathered[place_across, 1 + b]
        first = first_row[b]
        last = last_row[b]
        for dest in range(N_SUB):
            if dest == 0:
                row = jnp.where(sub == N_SUB - 1, across, first)
            elif dest == N_SUB - 1:
                row = jnp.where(sub == 0, across, last)
            else:
                row = jnp.where(sub == dest - 1, last, first)
            send[dest, SLOT_ROWS + b * PLANES : SLOT_ROWS + (b + 1) * PLANES, :] = row


def route(meta, gathered, first_row, last_row):
    return pl.pallas_call(
        route_kernel,
        out_shape=(f32(N_SUB, SLOT_ROWS + 4 * PLANES, 128), f32(4, PLANES, 128)),
        in_specs=[SMEM] + [VMEM] * 3,
        out_specs=(VMEM,) * 2,
        compiler_params=params(8),
        cost_estimate=pl.CostEstimate(flops=1000000, bytes_accessed=1000000, transcendentals=0),
        name="route",
    )(meta, gathered, first_row, last_row)


def exchange(meta, held, beside_z, beside_y, payload, first_row, last_row):
    def turn(k):
        return [
            (y * 8 + z * 2 + c, y * 8 + ((z + k) % 4) * 2 + c)
            for y in range(2)
            for z in range(4)
            for c in range(2)
        ]

    all_parts = payload[None]
    all_parts = jnp.concatenate(
        [all_parts] + [lax.ppermute(all_parts, "tile", turn(k)) for k in (1, 3, 2)], axis=0
    )
    all_parts, held, extra = lax.optimization_barrier((all_parts, held, beside_z()))
    all_parts = jnp.concatenate(
        [all_parts, lax.ppermute(all_parts, "tile", [(i, i ^ 8) for i in range(N_TILE)])], axis=0
    )
    extra = beside_y(*held, *extra)
    all_parts, *extra = lax.optimization_barrier((all_parts, *extra))
    all_parts = jnp.concatenate(
        [all_parts, lax.ppermute(all_parts, "tile", [(i, i ^ 1) for i in range(N_TILE)])], axis=0
    )
    send, here = route(meta, all_parts, first_row, last_row)
    got = lax.all_to_all(send, "sub", split_axis=0, concat_axis=0, tiled=True)
    return (got, here), extra


def place_halo(meta, got, here, weighted, strips):
    sub = meta[13]
    before = jnp.maximum(sub - 1, 0)
    after = jnp.minimum(sub + 1, N_SUB - 1)
    opposite = jnp.where(sub == 0, N_SUB - 1, 0)
    lane = iota((PLANES, 128), 1)

    def source(edge):
        other_edge, turned = meta[3 * edge + 1], meta[3 * edge + 2]
        same = jnp.where(turned == 1, N_SUB - 1 - sub, sub)
        return jnp.where(other_edge == 0, 0, jnp.where(other_edge == 1, N_SUB - 1, same))

    sides = jnp.where(lane < 64, got[source(2), :PLANES, :], got[source(3), :PLANES, :])
    to = iota((128, 128), 0)
    of = iota((128, 128), 1)
    turned = jnp.where(to < 64, meta[8], meta[11])
    wanted = jnp.where(turned == 1, (to & 64) + 63 - (to & 63), to)
    pick = jnp.where(of == wanted, 1.0, 0.0)
    strips[:, :PLANES] = lax.dot_general(
        pick, sides, (((1,), (1,)), ((), ())), precision=HIGHEST, preferred_element_type=jnp.float32
    )

    own = jnp.where(sub == N_SUB - 1, 1, 0)
    other_edge, turned = meta[3 * own + 1], meta[3 * own + 2]
    flip = jnp.where(of == jnp.where(turned == 1, 127 - to, to), 1.0, 0.0)
    row = []
    for b in range(4):
        part = slice(SLOT_ROWS + b * PLANES, SLOT_ROWS + (b + 1) * PLANES)
        even = got[2 * b, PLANES:SLOT_ROWS, :]
        odd = got[2 * b + 1, PLANES:SLOT_ROWS, :]
        joined = jnp.concatenate(
            [
                jnp.where(lane[:LEVELS] < 64, even, pltpu.roll(odd, 64, 1)),
                jnp.where(lane[:LEVELS] < 64, pltpu.roll(even, 64, 1), odd),
            ],
            axis=0,
        )
        joined = jnp.where(other_edge < 2, got[opposite, part, :], joined)
        row.append(jnp.where(other_edge == own, here[b], joined))
    ordered = [jnp.where(turned == 1, row[3 - b], row[b]) for b in range(4)]
    strips_in_order = jnp.dot(
        jnp.concatenate(ordered, axis=0),
        flip,
        precision=HIGHEST,
        preferred_element_type=jnp.float32,
    )
    for b in range(4):
        strip = strips_in_order[b * PLANES : (b + 1) * PLANES]
        at = b * PLANES * PITCH
        part = slice(SLOT_ROWS + b * PLANES, SLOT_ROWS + (b + 1) * PLANES)
        above_row = jnp.where(sub == 0, strip, got[before, part, :])
        below_row = jnp.where(sub == N_SUB - 1, strip, got[after, part, :])
        weighted[pl.ds(at + 7, PLANES, stride=PITCH), :] = above_row
        weighted[pl.ds(at + ROWS + 8, PLANES, stride=PITCH), :] = below_row


def stepped(solved, weighted, scale, depth_ref, strips, block, quarter):
    columns = slice(quarter * 128, (quarter + 1) * 128)
    lane = iota((8, 128), 1)
    here = pl.ds(pl.multiple_of(block * 8, 8), 8)
    depth = depth_ref[here, columns]
    if quarter == 0:
        west = strips[here, :]
    if quarter == 3:
        east = strips[pl.ds(pl.multiple_of(ROWS + block * 8, 8), 8), :]
    weights = {}

    def value(plane):
        level = plane % LEVELS
        if level not in weights:
            at = pl.ds(pl.multiple_of(level * ROWS + block * 8, 8), 8)
            weights[level] = jnp.where(level < depth, scale[at, columns], 0.0) * explicit_rate
        center = weighted[wide_rows(quarter, plane, block), :]
        total = weighted[wide_rows(quarter, plane, block, -1), :]
        total = total + weighted[wide_rows(quarter, plane, block, 1), :]
        if quarter == 0:
            edge = west if plane == 0 else pltpu.roll(west, 128 - plane, 1)
            total = total + jnp.where(lane == 0, edge, pltpu.roll(center, 1, 1))
        else:
            left = weighted[wide_rows(quarter - 1, plane, block), :]
            total = total + pltpu.roll(jnp.where(lane == 127, left, center), 1, 1)
        if quarter == 3:
            edge = pltpu.roll(east, 127 - plane, 1)
            total = total + jnp.where(lane == 127, edge, pltpu.roll(center, 127, 1))
        else:
            right = weighted[wide_rows(quarter + 1, plane, block), :]
            total = total + pltpu.roll(jnp.where(lane == 0, right, center), 127, 1)
        return solved[tile_rows(quarter, plane, block), :] + weights[level] * (
            total - 4.0 * center
        )

    return value


def second_tile(solved_in, weighted_in, force, coupling, scale, depth, solved, weighted, strips,
                sides):
    def tile(block, quarter):
        columns = slice(quarter * 128, (quarter + 1) * 128)
        late = stepped(solved_in, weighted_in, scale, depth, strips, block, quarter)

        def value(plane):
            at = (pl.ds(pl.multiple_of(plane * ROWS + block * 8, 8), 8), columns)
            return late(plane) + force[at]

        solve_tile(value, coupling, scale, depth, solved, weighted, sides, block, quarter)

    return tile


def second_inner_kernel(solved_in, weighted_in, force, coupling, scale, depth, solved, weighted):
    inner_tiles(
        second_tile(
            solved_in, weighted_in, force, coupling, scale, depth, solved, weighted, None, None
        )
    )


def second_edges_kernel(meta, got, here, solved_in, weighted_in, force, coupling, scale, depth, _,
                        __, solved, weighted, payload, first_row, last_row, weighted_late, sides,
                        strips, late):
    place_halo(meta, got, here, weighted_late, strips)

    def right_side(block, quarter):
        columns = slice(quarter * 128, (quarter + 1) * 128)
        value = stepped(solved_in, weighted_late, scale, depth, strips, block, quarter)
        for level in range(LEVELS):
            for plane in (level, LEVELS + level):
                at = (pl.ds(pl.multiple_of(plane * ROWS + block * 8, 8), 8), columns)
                late[at] = value(plane) + force[at]

    def solve(block, quarter):
        columns = slice(quarter * 128, (quarter + 1) * 128)

        def value(plane):
            return late[pl.ds(pl.multiple_of(plane * ROWS + block * 8, 8), 8), columns]

        solve_tile(value, coupling, scale, depth, solved, weighted, sides, block, quarter)

    edge_tiles(right_side)
    edge_tiles(solve)
    send_edges(meta, weighted, sides, payload, first_row, last_row)


def second_inner(*given):
    return pl.pallas_call(
        second_inner_kernel,
        out_shape=BIG,
        in_specs=[VMEM] * 6,
        out_specs=(VMEM,) * 2,
        compiler_params=params(4),
        cost_estimate=cost(30000000),
        name="second_inner",
    )(*given)


def second_edges(meta, halos, *given):
    return pl.pallas_call(
        second_edges_kernel,
        out_shape=BIG + EDGES + BIG[1:],
        in_specs=[SMEM] + [VMEM] * 10,
        out_specs=(VMEM,) * 6,
        input_output_aliases={9: 0, 10: 1, 4: 5},
        scratch_shapes=[SIDES] * 2 + [pltpu.VMEM((PLANES * ROWS, COLS), jnp.float32)],
        compiler_params=params(12),
        cost_estimate=cost(40000000),
        name="second_edges",
    )(meta, *halos, *given)


def last_tile(solved, weighted, scale, depth, strips, ready):
    def tile(block, quarter):
        columns = slice(quarter * 128, (quarter + 1) * 128)
        value = stepped(solved, weighted, scale, depth, strips, block, quarter)
        for level in range(LEVELS):
            for plane in (level, LEVELS + level):
                ready[plane, pl.ds(pl.multiple_of(block * 8, 8), 8), columns] = value(plane)

    return tile


INSIDE = (slice(8, ROWS - 8), slice(128, 384))
OUTSIDE = [
    (slice(0, ROWS), slice(0, 128)),
    (slice(0, ROWS), slice(384, 512)),
    (slice(0, 8), slice(128, 384)),
    (slice(ROWS - 8, ROWS), slice(128, 384)),
]


def last_inner_kernel(solved, weighted, scale, depth, out, ready, sems):
    inner_tiles(last_tile(solved, weighted, scale, depth, None, ready))
    rows, columns = INSIDE
    copy = pltpu.make_async_copy(
        ready.at[:, rows, columns], out.at[:, rows, columns], sems.at[0]
    )
    copy.start()
    copy.wait()


def last_edges_kernel(meta, got, here, solved, weighted_in, scale, depth, _, out, weighted, strips,
                      ready, sems):
    place_halo(meta, got, here, weighted, strips)
    tile = last_tile(solved, weighted, scale, depth, strips, ready)

    def copy(i):
        rows, columns = OUTSIDE[i]
        return pltpu.make_async_copy(
            ready.at[:, rows, columns], out.at[:, rows, columns], sems.at[i]
        )

    def column(quarter):
        def step(block, carry):
            tile(block, quarter)
            return carry

        lax.fori_loop(0, ROWS // 8, step, 0, unroll=4)

    column(0)
    copy(0).start()
    column(3)
    copy(1).start()
    for i, block in ((2, 0), (3, ROWS // 8 - 1)):
        tile(block, 1)
        tile(block, 2)
        copy(i).start()
    for i in range(4):
        copy(i).wait()


READY = [pltpu.VMEM((PLANES, ROWS, COLS), jnp.float32), pltpu.SemaphoreType.DMA((4,))]
ANY = pl.BlockSpec(memory_space=pl.ANY)


def last_inner(*given):
    return pl.pallas_call(
        last_inner_kernel,
        out_shape=f32(PLANES, ROWS, COLS),
        in_specs=[VMEM] * 4,
        out_specs=ANY,
        scratch_shapes=READY,
        compiler_params=params(6),
        cost_estimate=cost(20000000),
        name="last_inner",
    )(*given)


def last_edges(meta, halos, *given):
    return pl.pallas_call(
        last_edges_kernel,
        out_shape=(f32(PLANES, ROWS, COLS), BIG[1]),
        in_specs=[SMEM] + [VMEM] * 6 + [ANY],
        out_specs=(ANY, VMEM),
        input_output_aliases={7: 0, 4: 1},
        scratch_shapes=[SIDES] + READY,
        compiler_params=params(8),
        cost_estimate=cost(20000000),
        name="last_edges",
    )(meta, *halos, *given)[0]


def body(
    adjoint_final,
    diff_scale,
    vert_coupling,
    column_depth,
    seam_table,
    tile_owner,
    prof_face,
    prof_cell,
    prof_time,
    misfit,
):
    rows = prof_face.shape[0]
    slots, meta = pack(
        tile_owner,
        jnp.transpose(seam_table, (2, 1, 0)),
        prof_face.reshape(1, rows),
        prof_cell.reshape(1, rows),
        prof_time.reshape(1, rows),
        misfit.reshape(PLANES, rows),
    )
    slots = lax.all_to_all(slots, ("tile", "sub"), split_axis=0, concat_axis=0, tiled=True)
    adjoint = adjoint_final.reshape(PLANES * ROWS, COLS)
    scale = diff_scale.reshape(LEVELS * ROWS, COLS)
    coupling = vert_coupling.reshape((LEVELS - 1) * ROWS, COLS)
    late = forcing(slots, 1)
    given = (adjoint, late, coupling, scale, column_depth)
    solved, weighted, *edges = first_edges(meta, *given)

    def beside_z():
        return first_inner(solved, weighted, *given)

    def beside_y(slots, *whole):
        early = forcing(slots, 0)
        return *whole, early, *second_inner(*whole, early, coupling, scale, column_depth)

    halos, (solved, weighted, early, *begun) = exchange(
        meta, (slots,), beside_z, beside_y, *edges
    )
    solved, weighted, *edges, _ = second_edges(
        meta, halos, solved, weighted, early, coupling, scale, column_depth, *begun
    )
    halos, begun = exchange(
        meta,
        (column_depth,),
        lambda: (),
        lambda depth: (last_inner(solved, weighted, scale, depth),),
        *edges,
    )
    out = last_edges(meta, halos, solved, weighted, scale, column_depth, *begun)
    return out.reshape(adjoint_final.shape)


def solution(mesh):
    return jax.shard_map(
        body,
        mesh=mesh,
        in_specs=(
            P(None, None, ("tile", "sub"), None),
            P(None, ("tile", "sub"), None),
            P(None, ("tile", "sub"), None),
            P(("tile", "sub"), None),
            P(),
            P(),
            P(("tile", "sub")),
            P(("tile", "sub")),
            P(("tile", "sub")),
            P(None, None, ("tile", "sub")),
        ),
        out_specs=P(None, None, ("tile", "sub"), None),
        check_vma=False,
    )
```

```python
import functools

import jax
import jax.numpy as jnp
from jax import lax
from jax.experimental import pallas as pl
from jax.experimental.pallas import tpu as pltpu
from jax.sharding import PartitionSpec as P

CAP = 4
LEVELS = 16
PLANES = 2 * LEVELS
ROWS = 64
COLS = 512
CELLS = ROWS * COLS
N_TILE = 16
N_SUB = 8
DEVICES = N_TILE * N_SUB
FACES = 16
explicit_rate = 0.2
HIGHEST = lax.Precision.HIGHEST
VMEM = pl.BlockSpec(memory_space=pltpu.VMEM)
SMEM = pl.BlockSpec(memory_space=pltpu.SMEM)
META = 16
PARTS = 2


def iota(shape, axis):
    return lax.broadcasted_iota(jnp.int32, shape, axis)


def params(mib):
    return pltpu.CompilerParams(vmem_limit_bytes=mib * 1024 * 1024)


def f32(*shape):
    return jax.ShapeDtypeStruct(shape, jnp.float32)


def pack_kernel(owner_in, seam_in, face_in, cell_in, time_in, misfit_in, out, meta, owners, seams,
                face, cell, time, misfit, sems):
    copies = [
        pltpu.make_async_copy(source, target, sems.at[i])
        for i, (source, target) in enumerate(
            (
                (owner_in, owners),
                (seam_in, seams),
                (face_in, face),
                (cell_in, cell),
                (time_in, time),
                (misfit_in, misfit),
            )
        )
    ]
    for copy in copies:
        copy.start()
    for copy in copies:
        copy.wait()

    def owner(f):
        return owners[f]

    def seam(part, edge, f):
        return seams[part, edge, f]


    tile = lax.axis_index("tile")
    sub = lax.axis_index("sub")
    my_face = jnp.int32(0)
    for f in range(FACES):
        my_face = my_face + jnp.where(owner(f) == tile, f, 0)
    meta[12] = tile
    meta[13] = sub
    for edge in range(4):
        other = owner(seam(0, edge, my_face))
        steps = (((tile >> 1) & 3) + 4 - ((other >> 1) & 3)) & 3
        away = (
            ((other & 1) ^ (tile & 1)) * 8
            + (((other >> 3) & 1) ^ ((tile >> 3) & 1)) * 4
            + (steps ^ (steps >> 1))
        )
        meta[3 * edge] = away
        meta[3 * edge + 1] = seam(1, edge, my_face)
        meta[3 * edge + 2] = seam(2, edge, my_face)

    rows = face.shape[1]
    faces = face[...]
    home = jnp.zeros_like(faces)
    for f in range(FACES):
        home = jnp.where(faces == f, owner(f), home)
    cells = cell[...]
    tile_row = cells >> 9
    target = home * N_SUB + (tile_row >> 6)
    code = (time[...] - 1) * CELLS + (tile_row & (ROWS - 1)) * COLS + (cells & (COLS - 1))
    first = iota((rows, rows), 0)
    second = iota((rows, rows), 1)
    target_row = jnp.broadcast_to(target.astype(jnp.float32), (rows, rows))
    target_col = jnp.sum(jnp.where(first == second, target_row, 0.0), axis=1, keepdims=True)
    rank = jnp.sum(
        jnp.where((target_col == target_row) & (first < second), 1.0, 0.0), axis=0, keepdims=True
    )
    rank = rank.astype(jnp.int32)
    values = misfit[...]
    tag = code.astype(jnp.float32) + 1.0
    dest = iota((DEVICES, rows), 0)
    total = jnp.zeros((DEVICES, 2 * DEVICES), jnp.float32)
    for k in range(CAP):
        hit = jnp.where((dest == target) & (rank == k), 1.0, 0.0)
        pieces = []
        if k > 0:
            pieces.append(jnp.zeros((PLANES * k, rows), jnp.float32))
        pieces.append(values)
        if k < CAP - 1:
            pieces.append(jnp.zeros((PLANES * (CAP - 1 - k), rows), jnp.float32))
        pieces.append(jnp.where(dest == k, tag, 0.0))
        stacked = jnp.concatenate(pieces, axis=0)
        hit = hit.astype(jnp.bfloat16)
        for _ in range(3):
            piece = stacked.astype(jnp.bfloat16)
            stacked = stacked - piece.astype(jnp.float32)
            total = total + lax.dot_general(
                hit, piece, (((1,), (1,)), ((), ())), preferred_element_type=jnp.float32
            )
    out[:, 0, :] = total[:, :DEVICES]
    out[:, 1, :] = total[:, DEVICES:] - 1.0


def pack(owner, seam, face, cell, time, misfit):
    line = pltpu.VMEM(face.shape, jnp.int32)
    return pl.pallas_call(
        pack_kernel,
        out_shape=(f32(DEVICES, 2, DEVICES), jax.ShapeDtypeStruct((META,), jnp.int32)),
        in_specs=[pl.BlockSpec(memory_space=pl.ANY)] * 6,
        out_specs=(VMEM, SMEM),
        scratch_shapes=[
            pltpu.SMEM(owner.shape, jnp.int32),
            pltpu.SMEM(seam.shape, jnp.int32),
            line,
            line,
            line,
            pltpu.VMEM(misfit.shape, jnp.float32),
            pltpu.SemaphoreType.DMA((6,)),
        ],
        compiler_params=pltpu.CompilerParams(vmem_limit_bytes=66000000),
        name="pack",
    )(owner, seam, face, cell, time, misfit)


def forcing_kernel(moment, slots, out, parts, place):
    values = jnp.transpose(slots[:, 0, :])
    tags = (slots[:, 1, :] + 0.5).astype(jnp.int32)
    tags = jnp.where(slots[:, 1, :] < 0.0, -1, tags)
    tags_t = jnp.transpose(tags.astype(jnp.float32)).astype(jnp.int32)
    tag_row = jnp.concatenate([tags_t[k : k + 1, :] for k in range(CAP)], axis=1)
    valid = (tag_row >= moment * CELLS) & (tag_row < (moment + 1) * CELLS)
    row_of = jnp.where(valid, (tag_row & (CELLS - 1)) >> 9, -1)
    on_row = iota((ROWS, CAP * DEVICES), 0) == row_of
    wide = jnp.concatenate([values[PLANES * k : PLANES * (k + 1), :] for k in range(CAP)], axis=1)
    high = wide.astype(jnp.bfloat16).astype(jnp.float32)
    parts[0] = high
    parts[1] = wide - high
    for k in range(CAP):
        col = tags[:, k : k + 1] & (COLS - 1)
        place[k * DEVICES : (k + 1) * DEVICES, :] = jnp.where(
            iota((DEVICES, COLS), 1) == col, 1.0, 0.0
        ).astype(jnp.bfloat16)
    group = 32

    def step(g, carry):
        total = None
        for part in range(PARTS):
            left = []
            for q in range(group):
                row = parts[part, pl.ds(g * group + q, 1), :]
                left.append(jnp.where(on_row, row, 0.0).astype(jnp.bfloat16))
            got = jnp.dot(
                jnp.concatenate(left, axis=0), place[...], preferred_element_type=jnp.float32
            )
            total = got if total is None else total + got
        out[pl.ds(pl.multiple_of(g * group * ROWS, 8), group * ROWS), :] = total
        return carry

    lax.fori_loop(0, PLANES // group, step, 0)


def forcing(slots, moment):
    return pl.pallas_call(
        functools.partial(forcing_kernel, moment),
        out_shape=f32(PLANES * ROWS, COLS),
        in_specs=[VMEM],
        out_specs=VMEM,
        scratch_shapes=[
            pltpu.VMEM((PARTS, PLANES, CAP * DEVICES), jnp.float32),
            pltpu.VMEM((CAP * DEVICES, COLS), jnp.bfloat16),
        ],
        compiler_params=params(16),
        cost_estimate=pl.CostEstimate(flops=8000000000, bytes_accessed=4325376, transcendentals=0),
        name=f"forcing_{moment}",
    )(slots)


QUARTER = PLANES * ROWS


def tile_rows(quarter, plane, block):
    return pl.ds(pl.multiple_of(quarter * QUARTER + plane * ROWS + block * 8, 8), 8)


PITCH = ROWS + 16


def wide_rows(quarter, plane, block, shift=0):
    start = (quarter * PLANES + plane) * PITCH + 8
    if shift:
        return pl.ds(start + shift + block * 8, 8)
    return pl.ds(pl.multiple_of(start + block * 8, 8), 8)


def edge_tiles(tile):
    def sides(block, carry):
        tile(block, 0)
        tile(block, 3)
        return carry

    def ends(end, carry):
        tile(end * (ROWS // 8 - 1), 1)
        tile(end * (ROWS // 8 - 1), 2)
        return carry

    lax.fori_loop(0, ROWS // 8, sides, 0, unroll=4)
    lax.fori_loop(0, 2, ends, 0, unroll=2)


def inner_tiles(tile):
    def step(block, carry):
        tile(block, 1)
        tile(block, 2)
        return carry

    lax.fori_loop(1, ROWS // 8 - 1, step, 0)


def eliminate(value, coupling, depth, at):
    links = []
    for k in range(LEVELS - 1):
        links.append(jnp.where(k + 1 < depth, coupling[at(k)], 0.0))
    ratio = []
    partial = [[], []]
    for k in range(LEVELS):
        pivot = jnp.float32(1.0)
        if k > 0:
            pivot = pivot + links[k - 1]
        if k < LEVELS - 1:
            pivot = pivot + links[k]
        if k > 0:
            pivot = pivot - links[k - 1] * ratio[k - 1]
        inverse = 1.0 / pivot
        for tracer in range(2):
            right = value(tracer * LEVELS + k)
            if k > 0:
                right = right + links[k - 1] * partial[tracer][k - 1]
            partial[tracer].append(right * inverse)
        if k < LEVELS - 1:
            ratio.append(links[k] * inverse)
    for k in range(LEVELS - 2, -1, -1):
        for tracer in range(2):
            partial[tracer][k] = partial[tracer][k] + ratio[k] * partial[tracer][k + 1]
    return partial


def solve_tile(value, coupling, scale, depth_ref, solved, weighted, sides, block, quarter):
    columns = slice(quarter * 128, (quarter + 1) * 128)

    def at(plane):
        return (pl.ds(pl.multiple_of(plane * ROWS + block * 8, 8), 8), columns)

    depth = depth_ref[pl.ds(pl.multiple_of(block * 8, 8), 8), columns]
    result = eliminate(value, coupling, depth, at)
    lane = iota((8, 128), 1)
    column = jnp.zeros((8, 128), jnp.float32)
    for k in range(LEVELS):
        weight = jnp.where(k < depth, scale[at(k)], 0.0)
        for tracer in range(2):
            plane = tracer * LEVELS + k
            found = result[tracer][k]
            heavy = weight * found
            solved[tile_rows(quarter, plane, block), :] = found
            weighted[wide_rows(quarter, plane, block), :] = heavy
            if quarter == 0:
                moved = heavy if plane == 0 else pltpu.roll(heavy, plane, 1)
                column = jnp.where(lane == plane, moved, column)
            if quarter == 3:
                column = jnp.where(lane == plane, pltpu.roll(heavy, plane + 1, 1), column)
    if quarter == 0:
        sides[pl.ds(pl.multiple_of(block * 8, 8), 8), :] = column
    if quarter == 3:
        sides[pl.ds(pl.multiple_of(ROWS + block * 8, 8), 8), :] = column


def send_edges(meta, weighted, sides, payload, first_row, last_row):
    sub = meta[13]
    payload[0] = jnp.transpose(sides[...])[:PLANES, :]
    for b in range(4):
        top = weighted[pl.ds(b * PLANES * PITCH + 8, PLANES, stride=PITCH), :]
        bottom = weighted[pl.ds(b * PLANES * PITCH + ROWS + 7, PLANES, stride=PITCH), :]
        payload[1 + b] = jnp.where(sub == N_SUB - 1, bottom, top)
        first_row[b] = top
        last_row[b] = bottom


BIG = (f32(4 * QUARTER, 128), f32(4 * PLANES * PITCH, 128))
EDGES = (f32(5, PLANES, 128), f32(4, PLANES, 128), f32(4, PLANES, 128))


def first_tile(adjoint, force, coupling, scale, depth, solved, weighted, sides):
    def tile(block, quarter):
        columns = slice(quarter * 128, (quarter + 1) * 128)

        def value(plane):
            at = (pl.ds(pl.multiple_of(plane * ROWS + block * 8, 8), 8), columns)
            return adjoint[at] + force[at]

        solve_tile(value, coupling, scale, depth, solved, weighted, sides, block, quarter)

    return tile


def first_edges_kernel(meta, adjoint, force, coupling, scale, depth, solved, weighted, payload,
                       first_row, last_row, sides):
    edge_tiles(first_tile(adjoint, force, coupling, scale, depth, solved, weighted, sides))
    send_edges(meta, weighted, sides, payload, first_row, last_row)


def first_inner_kernel(adjoint, force, coupling, scale, depth, _, __, solved, weighted):
    inner_tiles(first_tile(adjoint, force, coupling, scale, depth, solved, weighted, None))


SIDES = pltpu.VMEM((128, 128), jnp.float32)


def cost(flops):
    return pl.CostEstimate(flops=flops, bytes_accessed=10000000, transcendentals=0)


def first_edges(meta, *given):
    return pl.pallas_call(
        first_edges_kernel,
        out_shape=BIG + EDGES,
        in_specs=[SMEM] + [VMEM] * 5,
        out_specs=(VMEM,) * 5,
        scratch_shapes=[SIDES],
        compiler_params=params(8),
        cost_estimate=cost(30000000),
        name="first_edges",
    )(meta, *given)


def first_inner(solved, weighted, *given):
    return pl.pallas_call(
        first_inner_kernel,
        out_shape=BIG,
        in_specs=[VMEM] * 7,
        out_specs=(VMEM,) * 2,
        input_output_aliases={5: 0, 6: 1},
        compiler_params=params(4),
        cost_estimate=cost(20000000),
        name="first_inner",
    )(*given, solved, weighted)


SLOT_ROWS = PLANES + LEVELS


def route_kernel(meta, gathered, first_row, last_row, send, here):
    sub = meta[13]
    lane = iota((PLANES, 128), 1)

    def half(edge, dest, wanted):
        place, other_edge, turned = meta[3 * edge], meta[3 * edge + 1], meta[3 * edge + 2]
        chunk = jnp.where(turned == 1, N_SUB - 1 - dest, dest)
        block = jnp.where(other_edge < 2, 1 + (chunk >> 1), 0)
        side = jnp.where(other_edge < 2, chunk & 1, other_edge - 2)
        found = gathered[place, block]
        return jnp.where(side == wanted, found, pltpu.roll(found, 64, 1))

    for dest in range(N_SUB):
        send[dest, :PLANES, :] = jnp.where(lane < 64, half(2, dest, 0), half(3, dest, 1))
        send[dest, PLANES : PLANES + LEVELS, :] = jnp.zeros((LEVELS, 128), jnp.float32)
    for edge, dest in ((0, 0), (1, N_SUB - 1)):
        found = gathered[meta[3 * edge], 0]
        turned = pltpu.roll(found, 64, 1)
        low = jnp.where(meta[3 * edge + 1] == 2, found, turned)
        high = jnp.where(meta[3 * edge + 1] == 2, turned, found)
        send[dest, PLANES : PLANES + LEVELS, :] = jnp.where(
            lane[:LEVELS] < 64, low[:LEVELS], high[LEVELS:]
        )
    own = jnp.where(sub == N_SUB - 1, 1, 0)
    place_here = meta[3 * own]
    place_across = meta[3 * (1 - own)]
    for b in range(4):
        here[b] = gathered[place_here, 1 + b]
        across = gathered[place_across, 1 + b]
        first = first_row[b]
        last = last_row[b]
        for dest in range(N_SUB):
            if dest == 0:
                row = jnp.where(sub == N_SUB - 1, across, first)
            elif dest == N_SUB - 1:
                row = jnp.where(sub == 0, across, last)
            else:
                row = jnp.where(sub == dest - 1, last, first)
            send[dest, SLOT_ROWS + b * PLANES : SLOT_ROWS + (b + 1) * PLANES, :] = row


def route(meta, gathered, first_row, last_row):
    return pl.pallas_call(
        route_kernel,
        out_shape=(f32(N_SUB, SLOT_ROWS + 4 * PLANES, 128), f32(4, PLANES, 128)),
        in_specs=[SMEM] + [VMEM] * 3,
        out_specs=(VMEM,) * 2,
        compiler_params=params(8),
        cost_estimate=pl.CostEstimate(flops=1000000, bytes_accessed=1000000, transcendentals=0),
        name="route",
    )(meta, gathered, first_row, last_row)


def exchange(meta, depth, beside_z, beside_y, payload, first_row, last_row):
    def turn(k):
        return [
            (y * 8 + z * 2 + c, y * 8 + ((z + k) % 4) * 2 + c)
            for y in range(2)
            for z in range(4)
            for c in range(2)
        ]

    all_parts = payload[None]
    all_parts = jnp.concatenate(
        [all_parts] + [lax.ppermute(all_parts, "tile", turn(k)) for k in (1, 3, 2)], axis=0
    )
    all_parts, depth, *extra = lax.optimization_barrier((all_parts, depth, *beside_z()))
    all_parts = jnp.concatenate(
        [all_parts, lax.ppermute(all_parts, "tile", [(i, i ^ 8) for i in range(N_TILE)])], axis=0
    )
    extra = beside_y(depth, *extra)
    all_parts, *extra = lax.optimization_barrier((all_parts, *extra))
    all_parts = jnp.concatenate(
        [all_parts, lax.ppermute(all_parts, "tile", [(i, i ^ 1) for i in range(N_TILE)])], axis=0
    )
    send, here = route(meta, all_parts, first_row, last_row)
    got = lax.all_to_all(send, "sub", split_axis=0, concat_axis=0, tiled=True)
    return (got, here), extra


def place_halo(meta, got, here, weighted, strips):
    sub = meta[13]
    before = jnp.maximum(sub - 1, 0)
    after = jnp.minimum(sub + 1, N_SUB - 1)
    opposite = jnp.where(sub == 0, N_SUB - 1, 0)
    lane = iota((PLANES, 128), 1)

    def source(edge):
        other_edge, turned = meta[3 * edge + 1], meta[3 * edge + 2]
        same = jnp.where(turned == 1, N_SUB - 1 - sub, sub)
        return jnp.where(other_edge == 0, 0, jnp.where(other_edge == 1, N_SUB - 1, same))

    sides = jnp.where(lane < 64, got[source(2), :PLANES, :], got[source(3), :PLANES, :])
    to = iota((128, 128), 0)
    of = iota((128, 128), 1)
    turned = jnp.where(to < 64, meta[8], meta[11])
    wanted = jnp.where(turned == 1, (to & 64) + 63 - (to & 63), to)
    pick = jnp.where(of == wanted, 1.0, 0.0)
    strips[:, :PLANES] = lax.dot_general(
        pick, sides, (((1,), (1,)), ((), ())), precision=HIGHEST, preferred_element_type=jnp.float32
    )

    own = jnp.where(sub == N_SUB - 1, 1, 0)
    other_edge, turned = meta[3 * own + 1], meta[3 * own + 2]
    flip = jnp.where(of == jnp.where(turned == 1, 127 - to, to), 1.0, 0.0)
    row = []
    for b in range(4):
        part = slice(SLOT_ROWS + b * PLANES, SLOT_ROWS + (b + 1) * PLANES)
        even = got[2 * b, PLANES:SLOT_ROWS, :]
        odd = got[2 * b + 1, PLANES:SLOT_ROWS, :]
        joined = jnp.concatenate(
            [
                jnp.where(lane[:LEVELS] < 64, even, pltpu.roll(odd, 64, 1)),
                jnp.where(lane[:LEVELS] < 64, pltpu.roll(even, 64, 1), odd),
            ],
            axis=0,
        )
        joined = jnp.where(other_edge < 2, got[opposite, part, :], joined)
        row.append(jnp.where(other_edge == own, here[b], joined))
    ordered = [jnp.where(turned == 1, row[3 - b], row[b]) for b in range(4)]
    strips_in_order = jnp.dot(
        jnp.concatenate(ordered, axis=0),
        flip,
        precision=HIGHEST,
        preferred_element_type=jnp.float32,
    )
    for b in range(4):
        strip = strips_in_order[b * PLANES : (b + 1) * PLANES]
        at = b * PLANES * PITCH
        part = slice(SLOT_ROWS + b * PLANES, SLOT_ROWS + (b + 1) * PLANES)
        above_row = jnp.where(sub == 0, strip, got[before, part, :])
        below_row = jnp.where(sub == N_SUB - 1, strip, got[after, part, :])
        weighted[pl.ds(at + 7, PLANES, stride=PITCH), :] = above_row
        weighted[pl.ds(at + ROWS + 8, PLANES, stride=PITCH), :] = below_row


def stepped(solved, weighted, scale, depth_ref, strips, block, quarter):
    columns = slice(quarter * 128, (quarter + 1) * 128)
    lane = iota((8, 128), 1)
    here = pl.ds(pl.multiple_of(block * 8, 8), 8)
    depth = depth_ref[here, columns]
    if quarter == 0:
        west = strips[here, :]
    if quarter == 3:
        east = strips[pl.ds(pl.multiple_of(ROWS + block * 8, 8), 8), :]
    weights = {}

    def value(plane):
        level = plane % LEVELS
        if level not in weights:
            at = pl.ds(pl.multiple_of(level * ROWS + block * 8, 8), 8)
            weights[level] = jnp.where(level < depth, scale[at, columns], 0.0) * explicit_rate
        center = weighted[wide_rows(quarter, plane, block), :]
        total = weighted[wide_rows(quarter, plane, block, -1), :]
        total = total + weighted[wide_rows(quarter, plane, block, 1), :]
        if quarter == 0:
            edge = west if plane == 0 else pltpu.roll(west, 128 - plane, 1)
            total = total + jnp.where(lane == 0, edge, pltpu.roll(center, 1, 1))
        else:
            left = weighted[wide_rows(quarter - 1, plane, block), :]
            total = total + pltpu.roll(jnp.where(lane == 127, left, center), 1, 1)
        if quarter == 3:
            edge = pltpu.roll(east, 127 - plane, 1)
            total = total + jnp.where(lane == 127, edge, pltpu.roll(center, 127, 1))
        else:
            right = weighted[wide_rows(quarter + 1, plane, block), :]
            total = total + pltpu.roll(jnp.where(lane == 0, right, center), 127, 1)
        return solved[tile_rows(quarter, plane, block), :] + weights[level] * (
            total - 4.0 * center
        )

    return value


def second_tile(solved_in, weighted_in, force, coupling, scale, depth, solved, weighted, strips,
                sides):
    def tile(block, quarter):
        columns = slice(quarter * 128, (quarter + 1) * 128)
        late = stepped(solved_in, weighted_in, scale, depth, strips, block, quarter)

        def value(plane):
            at = (pl.ds(pl.multiple_of(plane * ROWS + block * 8, 8), 8), columns)
            return late(plane) + force[at]

        solve_tile(value, coupling, scale, depth, solved, weighted, sides, block, quarter)

    return tile


def second_inner_kernel(solved_in, weighted_in, force, coupling, scale, depth, solved, weighted):
    inner_tiles(
        second_tile(
            solved_in, weighted_in, force, coupling, scale, depth, solved, weighted, None, None
        )
    )


def second_edges_kernel(meta, got, here, solved_in, weighted_in, force, coupling, scale, depth, _,
                        __, solved, weighted, payload, first_row, last_row, weighted_late, sides,
                        strips, late):
    place_halo(meta, got, here, weighted_late, strips)

    def right_side(block, quarter):
        columns = slice(quarter * 128, (quarter + 1) * 128)
        value = stepped(solved_in, weighted_late, scale, depth, strips, block, quarter)
        for level in range(LEVELS):
            for plane in (level, LEVELS + level):
                at = (pl.ds(pl.multiple_of(plane * ROWS + block * 8, 8), 8), columns)
                late[at] = value(plane) + force[at]

    def solve(block, quarter):
        columns = slice(quarter * 128, (quarter + 1) * 128)

        def value(plane):
            return late[pl.ds(pl.multiple_of(plane * ROWS + block * 8, 8), 8), columns]

        solve_tile(value, coupling, scale, depth, solved, weighted, sides, block, quarter)

    edge_tiles(right_side)
    edge_tiles(solve)
    send_edges(meta, weighted, sides, payload, first_row, last_row)


def second_inner(*given):
    return pl.pallas_call(
        second_inner_kernel,
        out_shape=BIG,
        in_specs=[VMEM] * 6,
        out_specs=(VMEM,) * 2,
        compiler_params=params(4),
        cost_estimate=cost(30000000),
        name="second_inner",
    )(*given)


def second_edges(meta, halos, *given):
    return pl.pallas_call(
        second_edges_kernel,
        out_shape=BIG + EDGES + BIG[1:],
        in_specs=[SMEM] + [VMEM] * 10,
        out_specs=(VMEM,) * 6,
        input_output_aliases={9: 0, 10: 1, 4: 5},
        scratch_shapes=[SIDES] * 2 + [pltpu.VMEM((PLANES * ROWS, COLS), jnp.float32)],
        compiler_params=params(12),
        cost_estimate=cost(40000000),
        name="second_edges",
    )(meta, *halos, *given)


def last_tile(solved, weighted, scale, depth, strips, ready):
    def tile(block, quarter):
        columns = slice(quarter * 128, (quarter + 1) * 128)
        value = stepped(solved, weighted, scale, depth, strips, block, quarter)
        for level in range(LEVELS):
            for plane in (level, LEVELS + level):
                ready[plane, pl.ds(pl.multiple_of(block * 8, 8), 8), columns] = value(plane)

    return tile


INSIDE = (slice(8, ROWS - 8), slice(128, 384))
OUTSIDE = [
    (slice(0, ROWS), slice(0, 128)),
    (slice(0, ROWS), slice(384, 512)),
    (slice(0, 8), slice(128, 384)),
    (slice(ROWS - 8, ROWS), slice(128, 384)),
]


def last_inner_kernel(solved, weighted, scale, depth, out, ready, sems):
    inner_tiles(last_tile(solved, weighted, scale, depth, None, ready))
    rows, columns = INSIDE
    copy = pltpu.make_async_copy(
        ready.at[:, rows, columns], out.at[:, rows, columns], sems.at[0]
    )
    copy.start()
    copy.wait()


def last_edges_kernel(meta, got, here, solved, weighted_in, scale, depth, _, out, weighted, strips,
                      ready, sems):
    place_halo(meta, got, here, weighted, strips)
    tile = last_tile(solved, weighted, scale, depth, strips, ready)

    def copy(i):
        rows, columns = OUTSIDE[i]
        return pltpu.make_async_copy(
            ready.at[:, rows, columns], out.at[:, rows, columns], sems.at[i]
        )

    def column(quarter):
        def step(block, carry):
            tile(block, quarter)
            return carry

        lax.fori_loop(0, ROWS // 8, step, 0, unroll=4)

    column(0)
    copy(0).start()
    column(3)
    copy(1).start()
    for i, block in ((2, 0), (3, ROWS // 8 - 1)):
        tile(block, 1)
        tile(block, 2)
        copy(i).start()
    for i in range(4):
        copy(i).wait()


READY = [pltpu.VMEM((PLANES, ROWS, COLS), jnp.float32), pltpu.SemaphoreType.DMA((4,))]
ANY = pl.BlockSpec(memory_space=pl.ANY)


def last_inner(*given):
    return pl.pallas_call(
        last_inner_kernel,
        out_shape=f32(PLANES, ROWS, COLS),
        in_specs=[VMEM] * 4,
        out_specs=ANY,
        scratch_shapes=READY,
        compiler_params=params(6),
        cost_estimate=cost(20000000),
        name="last_inner",
    )(*given)


def last_edges(meta, halos, *given):
    return pl.pallas_call(
        last_edges_kernel,
        out_shape=(f32(PLANES, ROWS, COLS), BIG[1]),
        in_specs=[SMEM] + [VMEM] * 6 + [ANY],
        out_specs=(ANY, VMEM),
        input_output_aliases={7: 0, 4: 1},
        scratch_shapes=[SIDES] + READY,
        compiler_params=params(8),
        cost_estimate=cost(20000000),
        name="last_edges",
    )(meta, *halos, *given)[0]


def body(
    adjoint_final,
    diff_scale,
    vert_coupling,
    column_depth,
    seam_table,
    tile_owner,
    prof_face,
    prof_cell,
    prof_time,
    misfit,
):
    rows = prof_face.shape[0]
    slots, meta = pack(
        tile_owner,
        jnp.transpose(seam_table, (2, 1, 0)),
        prof_face.reshape(1, rows),
        prof_cell.reshape(1, rows),
        prof_time.reshape(1, rows),
        misfit.reshape(PLANES, rows),
    )
    slots = lax.all_to_all(slots, ("tile", "sub"), split_axis=0, concat_axis=0, tiled=True)
    adjoint = adjoint_final.reshape(PLANES * ROWS, COLS)
    scale = diff_scale.reshape(LEVELS * ROWS, COLS)
    coupling = vert_coupling.reshape((LEVELS - 1) * ROWS, COLS)
    late = forcing(slots, 1)
    given = (adjoint, late, coupling, scale, column_depth)
    solved, weighted, *edges = first_edges(meta, *given)

    def beside_z():
        return (forcing(slots, 0),)

    def beside_y(depth, early):
        whole = first_inner(solved, weighted, *given[:-1], depth)
        return *whole, early, *second_inner(*whole, early, coupling, scale, depth)

    halos, (solved, weighted, early, *begun) = exchange(
        meta, column_depth, beside_z, beside_y, *edges
    )
    solved, weighted, *edges, _ = second_edges(
        meta, halos, solved, weighted, early, coupling, scale, column_depth, *begun
    )
    halos, begun = exchange(
        meta,
        column_depth,
        lambda: (),
        lambda depth: (last_inner(solved, weighted, scale, depth),),
        *edges,
    )
    out = last_edges(meta, halos, solved, weighted, scale, column_depth, *begun)
    return out.reshape(adjoint_final.shape)


def solution(mesh):
    return jax.shard_map(
        body,
        mesh=mesh,
        in_specs=(
            P(None, None, ("tile", "sub"), None),
            P(None, ("tile", "sub"), None),
            P(None, ("tile", "sub"), None),
            P(("tile", "sub"), None),
            P(),
            P(),
            P(("tile", "sub")),
            P(("tile", "sub")),
            P(("tile", "sub")),
            P(None, None, ("tile", "sub")),
        ),
        out_specs=P(None, None, ("tile", "sub"), None),
        check_vma=False,
    )
```

```python
import functools

import jax
import jax.numpy as jnp
from jax import lax
from jax.experimental import pallas as pl
from jax.experimental.pallas import tpu as pltpu
from jax.sharding import PartitionSpec as P

CAP = 4
LEVELS = 16
PLANES = 2 * LEVELS
ROWS = 64
COLS = 512
CELLS = ROWS * COLS
N_TILE = 16
N_SUB = 8
DEVICES = N_TILE * N_SUB
FACES = 16
explicit_rate = 0.2
HIGHEST = lax.Precision.HIGHEST
VMEM = pl.BlockSpec(memory_space=pltpu.VMEM)
SMEM = pl.BlockSpec(memory_space=pltpu.SMEM)
META = 16
PARTS = 2


def iota(shape, axis):
    return lax.broadcasted_iota(jnp.int32, shape, axis)


def params(mib):
    return pltpu.CompilerParams(vmem_limit_bytes=mib * 1024 * 1024)


def f32(*shape):
    return jax.ShapeDtypeStruct(shape, jnp.float32)


def pack_kernel(owner_in, seam_in, face_in, cell_in, time_in, misfit_in, out, meta, owners, seams,
                face, cell, time, misfit, sems):
    copies = [
        pltpu.make_async_copy(source, target, sems.at[i])
        for i, (source, target) in enumerate(
            (
                (owner_in, owners),
                (seam_in, seams),
                (face_in, face),
                (cell_in, cell),
                (time_in, time),
                (misfit_in, misfit),
            )
        )
    ]
    for copy in copies:
        copy.start()
    for copy in copies:
        copy.wait()

    def owner(f):
        return owners[f]

    def seam(part, edge, f):
        return seams[part, edge, f]


    tile = lax.axis_index("tile")
    sub = lax.axis_index("sub")
    my_face = jnp.int32(0)
    for f in range(FACES):
        my_face = my_face + jnp.where(owner(f) == tile, f, 0)
    meta[12] = tile
    meta[13] = sub
    for edge in range(4):
        other = owner(seam(0, edge, my_face))
        steps = (((tile >> 1) & 3) + 4 - ((other >> 1) & 3)) & 3
        away = (
            ((other & 1) ^ (tile & 1)) * 8
            + (((other >> 3) & 1) ^ ((tile >> 3) & 1)) * 4
            + (steps ^ (steps >> 1))
        )
        meta[3 * edge] = away
        meta[3 * edge + 1] = seam(1, edge, my_face)
        meta[3 * edge + 2] = seam(2, edge, my_face)

    rows = face.shape[1]
    faces = face[...]
    home = jnp.zeros_like(faces)
    for f in range(FACES):
        home = jnp.where(faces == f, owner(f), home)
    cells = cell[...]
    tile_row = cells >> 9
    target = home * N_SUB + (tile_row >> 6)
    code = (time[...] - 1) * CELLS + (tile_row & (ROWS - 1)) * COLS + (cells & (COLS - 1))
    first = iota((rows, rows), 0)
    second = iota((rows, rows), 1)
    target_row = jnp.broadcast_to(target.astype(jnp.float32), (rows, rows))
    target_col = jnp.sum(jnp.where(first == second, target_row, 0.0), axis=1, keepdims=True)
    rank = jnp.sum(
        jnp.where((target_col == target_row) & (first < second), 1.0, 0.0), axis=0, keepdims=True
    )
    rank = rank.astype(jnp.int32)
    values = misfit[...]
    tag = code.astype(jnp.float32) + 1.0
    dest = iota((DEVICES, rows), 0)
    total = jnp.zeros((DEVICES, 2 * DEVICES), jnp.float32)
    for k in range(CAP):
        hit = jnp.where((dest == target) & (rank == k), 1.0, 0.0)
        pieces = []
        if k > 0:
            pieces.append(jnp.zeros((PLANES * k, rows), jnp.float32))
        pieces.append(values)
        if k < CAP - 1:
            pieces.append(jnp.zeros((PLANES * (CAP - 1 - k), rows), jnp.float32))
        pieces.append(jnp.where(dest == k, tag, 0.0))
        stacked = jnp.concatenate(pieces, axis=0)
        total = total + lax.dot_general(
            hit, stacked, (((1,), (1,)), ((), ())), precision=HIGHEST,
            preferred_element_type=jnp.float32,
        )
    out[:, 0, :] = total[:, :DEVICES]
    out[:, 1, :] = total[:, DEVICES:] - 1.0


def pack(owner, seam, face, cell, time, misfit):
    line = pltpu.VMEM(face.shape, jnp.int32)
    return pl.pallas_call(
        pack_kernel,
        out_shape=(f32(DEVICES, 2, DEVICES), jax.ShapeDtypeStruct((META,), jnp.int32)),
        in_specs=[pl.BlockSpec(memory_space=pl.ANY)] * 6,
        out_specs=(VMEM, SMEM),
        scratch_shapes=[
            pltpu.SMEM(owner.shape, jnp.int32),
            pltpu.SMEM(seam.shape, jnp.int32),
            line,
            line,
            line,
            pltpu.VMEM(misfit.shape, jnp.float32),
            pltpu.SemaphoreType.DMA((6,)),
        ],
        compiler_params=pltpu.CompilerParams(vmem_limit_bytes=66000000),
        name="pack",
    )(owner, seam, face, cell, time, misfit)


def forcing_kernel(moment, slots, out, parts, place):
    values = jnp.transpose(slots[:, 0, :])
    tags = (slots[:, 1, :] + 0.5).astype(jnp.int32)
    tags = jnp.where(slots[:, 1, :] < 0.0, -1, tags)
    tags_t = jnp.transpose(tags.astype(jnp.float32)).astype(jnp.int32)
    tag_row = jnp.concatenate([tags_t[k : k + 1, :] for k in range(CAP)], axis=1)
    valid = (tag_row >= moment * CELLS) & (tag_row < (moment + 1) * CELLS)
    row_of = jnp.where(valid, (tag_row & (CELLS - 1)) >> 9, -1)
    on_row = iota((ROWS, CAP * DEVICES), 0) == row_of
    wide = jnp.concatenate([values[PLANES * k : PLANES * (k + 1), :] for k in range(CAP)], axis=1)
    high = wide.astype(jnp.bfloat16).astype(jnp.float32)
    parts[0] = high
    parts[1] = wide - high
    for k in range(CAP):
        col = tags[:, k : k + 1] & (COLS - 1)
        place[k * DEVICES : (k + 1) * DEVICES, :] = jnp.where(
            iota((DEVICES, COLS), 1) == col, 1.0, 0.0
        ).astype(jnp.bfloat16)
    group = 16

    def step(g, carry):
        total = None
        for part in range(PARTS):
            left = []
            for q in range(group):
                row = parts[part, pl.ds(g * group + q, 1), :]
                left.append(jnp.where(on_row, row, 0.0).astype(jnp.bfloat16))
            got = jnp.dot(
                jnp.concatenate(left, axis=0), place[...], preferred_element_type=jnp.float32
            )
            total = got if total is None else total + got
        out[pl.ds(pl.multiple_of(g * group * ROWS, 8), group * ROWS), :] = total
        return carry

    lax.fori_loop(0, PLANES // group, step, 0)


def forcing(slots, moment):
    return pl.pallas_call(
        functools.partial(forcing_kernel, moment),
        out_shape=f32(PLANES * ROWS, COLS),
        in_specs=[VMEM],
        out_specs=VMEM,
        scratch_shapes=[
            pltpu.VMEM((PARTS, PLANES, CAP * DEVICES), jnp.float32),
            pltpu.VMEM((CAP * DEVICES, COLS), jnp.bfloat16),
        ],
        compiler_params=params(16),
        cost_estimate=pl.CostEstimate(flops=8000000000, bytes_accessed=4325376, transcendentals=0),
        name=f"forcing_{moment}",
    )(slots)


QUARTER = PLANES * ROWS


def tile_rows(quarter, plane, block):
    return pl.ds(pl.multiple_of(quarter * QUARTER + plane * ROWS + block * 8, 8), 8)


PITCH = ROWS + 16


def wide_rows(quarter, plane, block, shift=0):
    start = (quarter * PLANES + plane) * PITCH + 8
    if shift:
        return pl.ds(start + shift + block * 8, 8)
    return pl.ds(pl.multiple_of(start + block * 8, 8), 8)


def edge_tiles(tile):
    def sides(block, carry):
        tile(block, 0)
        tile(block, 3)
        return carry

    def ends(end, carry):
        tile(end * (ROWS // 8 - 1), 1)
        tile(end * (ROWS // 8 - 1), 2)
        return carry

    lax.fori_loop(0, ROWS // 8, sides, 0, unroll=8)
    lax.fori_loop(0, 2, ends, 0, unroll=2)


def inner_tiles(tile):
    def step(block, carry):
        tile(block, 1)
        tile(block, 2)
        return carry

    lax.fori_loop(1, ROWS // 8 - 1, step, 0)


def eliminate(value, coupling, depth, at):
    links = []
    for k in range(LEVELS - 1):
        links.append(jnp.where(k + 1 < depth, coupling[at(k)], 0.0))
    ratio = []
    partial = [[], []]
    for k in range(LEVELS):
        pivot = jnp.float32(1.0)
        if k > 0:
            pivot = pivot + links[k - 1]
        if k < LEVELS - 1:
            pivot = pivot + links[k]
        if k > 0:
            pivot = pivot - links[k - 1] * ratio[k - 1]
        inverse = 1.0 / pivot
        for tracer in range(2):
            right = value(tracer * LEVELS + k)
            if k > 0:
                right = right + links[k - 1] * partial[tracer][k - 1]
            partial[tracer].append(right * inverse)
        if k < LEVELS - 1:
            ratio.append(links[k] * inverse)
    for k in range(LEVELS - 2, -1, -1):
        for tracer in range(2):
            partial[tracer][k] = partial[tracer][k] + ratio[k] * partial[tracer][k + 1]
    return partial


def solve_tile(value, coupling, scale, depth_ref, solved, weighted, sides, block, quarter):
    columns = slice(quarter * 128, (quarter + 1) * 128)

    def at(plane):
        return (pl.ds(pl.multiple_of(plane * ROWS + block * 8, 8), 8), columns)

    depth = depth_ref[pl.ds(pl.multiple_of(block * 8, 8), 8), columns]
    result = eliminate(value, coupling, depth, at)
    lane = iota((8, 128), 1)
    column = jnp.zeros((8, 128), jnp.float32)
    for k in range(LEVELS):
        weight = jnp.where(k < depth, scale[at(k)], 0.0)
        for tracer in range(2):
            plane = tracer * LEVELS + k
            found = result[tracer][k]
            heavy = weight * found
            solved[tile_rows(quarter, plane, block), :] = found
            weighted[wide_rows(quarter, plane, block), :] = heavy
            if quarter == 0:
                moved = heavy if plane == 0 else pltpu.roll(heavy, plane, 1)
                column = jnp.where(lane == plane, moved, column)
            if quarter == 3:
                column = jnp.where(lane == plane, pltpu.roll(heavy, plane + 1, 1), column)
    if quarter == 0:
        sides[pl.ds(pl.multiple_of(block * 8, 8), 8), :] = column
    if quarter == 3:
        sides[pl.ds(pl.multiple_of(ROWS + block * 8, 8), 8), :] = column


def send_edges(meta, weighted, sides, payload, first_row, last_row):
    sub = meta[13]
    payload[0] = jnp.transpose(sides[...])[:PLANES, :]
    for b in range(4):
        top = weighted[pl.ds(b * PLANES * PITCH + 8, PLANES, stride=PITCH), :]
        bottom = weighted[pl.ds(b * PLANES * PITCH + ROWS + 7, PLANES, stride=PITCH), :]
        payload[1 + b] = jnp.where(sub == N_SUB - 1, bottom, top)
        first_row[b] = top
        last_row[b] = bottom


BIG = (f32(4 * QUARTER, 128), f32(4 * PLANES * PITCH, 128))
EDGES = (f32(5, PLANES, 128), f32(4, PLANES, 128), f32(4, PLANES, 128))


def first_tile(adjoint, force, coupling, scale, depth, solved, weighted, sides):
    def tile(block, quarter):
        columns = slice(quarter * 128, (quarter + 1) * 128)

        def value(plane):
            at = (pl.ds(pl.multiple_of(plane * ROWS + block * 8, 8), 8), columns)
            return adjoint[at] + force[at]

        solve_tile(value, coupling, scale, depth, solved, weighted, sides, block, quarter)

    return tile


def first_edges_kernel(meta, adjoint, force, coupling, scale, depth, solved, weighted, payload,
                       first_row, last_row, sides):
    edge_tiles(first_tile(adjoint, force, coupling, scale, depth, solved, weighted, sides))
    send_edges(meta, weighted, sides, payload, first_row, last_row)


def first_inner_kernel(adjoint, force, coupling, scale, depth, _, __, solved, weighted):
    inner_tiles(first_tile(adjoint, force, coupling, scale, depth, solved, weighted, None))


SIDES = pltpu.VMEM((128, 128), jnp.float32)


def cost(flops):
    return pl.CostEstimate(flops=flops, bytes_accessed=10000000, transcendentals=0)


def first_edges(meta, *given):
    return pl.pallas_call(
        first_edges_kernel,
        out_shape=BIG + EDGES,
        in_specs=[SMEM] + [VMEM] * 5,
        out_specs=(VMEM,) * 5,
        scratch_shapes=[SIDES],
        compiler_params=params(8),
        cost_estimate=cost(30000000),
        name="first_edges",
    )(meta, *given)


def first_inner(solved, weighted, *given):
    return pl.pallas_call(
        first_inner_kernel,
        out_shape=BIG,
        in_specs=[VMEM] * 7,
        out_specs=(VMEM,) * 2,
        input_output_aliases={5: 0, 6: 1},
        compiler_params=params(4),
        cost_estimate=cost(20000000),
        name="first_inner",
    )(*given, solved, weighted)


SLOT_ROWS = PLANES + LEVELS


def route_kernel(meta, gathered, first_row, last_row, send, here):
    sub = meta[13]
    lane = iota((PLANES, 128), 1)

    def half(edge, dest, wanted):
        place, other_edge, turned = meta[3 * edge], meta[3 * edge + 1], meta[3 * edge + 2]
        chunk = jnp.where(turned == 1, N_SUB - 1 - dest, dest)
        block = jnp.where(other_edge < 2, 1 + (chunk >> 1), 0)
        side = jnp.where(other_edge < 2, chunk & 1, other_edge - 2)
        found = gathered[place, block]
        return jnp.where(side == wanted, found, pltpu.roll(found, 64, 1))

    for dest in range(N_SUB):
        send[dest, :PLANES, :] = jnp.where(lane < 64, half(2, dest, 0), half(3, dest, 1))
        send[dest, PLANES : PLANES + LEVELS, :] = jnp.zeros((LEVELS, 128), jnp.float32)
    for edge, dest in ((0, 0), (1, N_SUB - 1)):
        found = gathered[meta[3 * edge], 0]
        turned = pltpu.roll(found, 64, 1)
        low = jnp.where(meta[3 * edge + 1] == 2, found, turned)
        high = jnp.where(meta[3 * edge + 1] == 2, turned, found)
        send[dest, PLANES : PLANES + LEVELS, :] = jnp.where(
            lane[:LEVELS] < 64, low[:LEVELS], high[LEVELS:]
        )
    own = jnp.where(sub == N_SUB - 1, 1, 0)
    place_here = meta[3 * own]
    place_across = meta[3 * (1 - own)]
    for b in range(4):
        here[b] = gathered[place_here, 1 + b]
        across = gathered[place_across, 1 + b]
        first = first_row[b]
        last = last_row[b]
        for dest in range(N_SUB):
            if dest == 0:
                row = jnp.where(sub == N_SUB - 1, across, first)
            elif dest == N_SUB - 1:
                row = jnp.where(sub == 0, across, last)
            else:
                row = jnp.where(sub == dest - 1, last, first)
            send[dest, SLOT_ROWS + b * PLANES : SLOT_ROWS + (b + 1) * PLANES, :] = row


def route(meta, gathered, first_row, last_row):
    return pl.pallas_call(
        route_kernel,
        out_shape=(f32(N_SUB, SLOT_ROWS + 4 * PLANES, 128), f32(4, PLANES, 128)),
        in_specs=[SMEM] + [VMEM] * 3,
        out_specs=(VMEM,) * 2,
        compiler_params=params(8),
        cost_estimate=pl.CostEstimate(flops=1000000, bytes_accessed=1000000, transcendentals=0),
        name="route",
    )(meta, gathered, first_row, last_row)


def exchange(meta, depth, beside_z, beside_y, payload, first_row, last_row):
    def turn(k):
        return [
            (y * 8 + z * 2 + c, y * 8 + ((z + k) % 4) * 2 + c)
            for y in range(2)
            for z in range(4)
            for c in range(2)
        ]

    all_parts = payload[None]
    all_parts = jnp.concatenate(
        [all_parts] + [lax.ppermute(all_parts, "tile", turn(k)) for k in (1, 3, 2)], axis=0
    )
    all_parts, depth, *extra = lax.optimization_barrier((all_parts, depth, *beside_z()))
    all_parts = jnp.concatenate(
        [all_parts, lax.ppermute(all_parts, "tile", [(i, i ^ 8) for i in range(N_TILE)])], axis=0
    )
    extra = beside_y(depth, *extra)
    all_parts, *extra = lax.optimization_barrier((all_parts, *extra))
    all_parts = jnp.concatenate(
        [all_parts, lax.ppermute(all_parts, "tile", [(i, i ^ 1) for i in range(N_TILE)])], axis=0
    )
    send, here = route(meta, all_parts, first_row, last_row)
    got = lax.all_to_all(send, "sub", split_axis=0, concat_axis=0, tiled=True)
    return (got, here), extra


def place_halo(meta, got, here, weighted, strips):
    sub = meta[13]
    before = jnp.maximum(sub - 1, 0)
    after = jnp.minimum(sub + 1, N_SUB - 1)
    opposite = jnp.where(sub == 0, N_SUB - 1, 0)
    lane = iota((PLANES, 128), 1)

    def source(edge):
        other_edge, turned = meta[3 * edge + 1], meta[3 * edge + 2]
        same = jnp.where(turned == 1, N_SUB - 1 - sub, sub)
        return jnp.where(other_edge == 0, 0, jnp.where(other_edge == 1, N_SUB - 1, same))

    sides = jnp.where(lane < 64, got[source(2), :PLANES, :], got[source(3), :PLANES, :])
    to = iota((128, 128), 0)
    of = iota((128, 128), 1)
    turned = jnp.where(to < 64, meta[8], meta[11])
    wanted = jnp.where(turned == 1, (to & 64) + 63 - (to & 63), to)
    pick = jnp.where(of == wanted, 1.0, 0.0)
    strips[:, :PLANES] = lax.dot_general(
        pick, sides, (((1,), (1,)), ((), ())), precision=HIGHEST, preferred_element_type=jnp.float32
    )

    own = jnp.where(sub == N_SUB - 1, 1, 0)
    other_edge, turned = meta[3 * own + 1], meta[3 * own + 2]
    flip = jnp.where(of == jnp.where(turned == 1, 127 - to, to), 1.0, 0.0)
    row = []
    for b in range(4):
        part = slice(SLOT_ROWS + b * PLANES, SLOT_ROWS + (b + 1) * PLANES)
        even = got[2 * b, PLANES:SLOT_ROWS, :]
        odd = got[2 * b + 1, PLANES:SLOT_ROWS, :]
        joined = jnp.concatenate(
            [
                jnp.where(lane[:LEVELS] < 64, even, pltpu.roll(odd, 64, 1)),
                jnp.where(lane[:LEVELS] < 64, pltpu.roll(even, 64, 1), odd),
            ],
            axis=0,
        )
        joined = jnp.where(other_edge < 2, got[opposite, part, :], joined)
        row.append(jnp.where(other_edge == own, here[b], joined))
    ordered = [jnp.where(turned == 1, row[3 - b], row[b]) for b in range(4)]
    strips_in_order = jnp.dot(
        jnp.concatenate(ordered, axis=0),
        flip,
        precision=HIGHEST,
        preferred_element_type=jnp.float32,
    )
    for b in range(4):
        strip = strips_in_order[b * PLANES : (b + 1) * PLANES]
        at = b * PLANES * PITCH
        part = slice(SLOT_ROWS + b * PLANES, SLOT_ROWS + (b + 1) * PLANES)
        above_row = jnp.where(sub == 0, strip, got[before, part, :])
        below_row = jnp.where(sub == N_SUB - 1, strip, got[after, part, :])
        weighted[pl.ds(at + 7, PLANES, stride=PITCH), :] = above_row
        weighted[pl.ds(at + ROWS + 8, PLANES, stride=PITCH), :] = below_row


def stepped(solved, weighted, scale, depth_ref, strips, block, quarter):
    columns = slice(quarter * 128, (quarter + 1) * 128)
    lane = iota((8, 128), 1)
    here = pl.ds(pl.multiple_of(block * 8, 8), 8)
    depth = depth_ref[here, columns]
    if quarter == 0:
        west = strips[here, :]
    if quarter == 3:
        east = strips[pl.ds(pl.multiple_of(ROWS + block * 8, 8), 8), :]
    weights = {}

    def value(plane):
        level = plane % LEVELS
        if level not in weights:
            at = pl.ds(pl.multiple_of(level * ROWS + block * 8, 8), 8)
            weights[level] = jnp.where(level < depth, scale[at, columns], 0.0) * explicit_rate
        center = weighted[wide_rows(quarter, plane, block), :]
        total = weighted[wide_rows(quarter, plane, block, -1), :]
        total = total + weighted[wide_rows(quarter, plane, block, 1), :]
        if quarter == 0:
            edge = west if plane == 0 else pltpu.roll(west, 128 - plane, 1)
            total = total + jnp.where(lane == 0, edge, pltpu.roll(center, 1, 1))
        else:
            left = weighted[wide_rows(quarter - 1, plane, block), :]
            total = total + pltpu.roll(jnp.where(lane == 127, left, center), 1, 1)
        if quarter == 3:
            edge = pltpu.roll(east, 127 - plane, 1)
            total = total + jnp.where(lane == 127, edge, pltpu.roll(center, 127, 1))
        else:
            right = weighted[wide_rows(quarter + 1, plane, block), :]
            total = total + pltpu.roll(jnp.where(lane == 0, right, center), 127, 1)
        return solved[tile_rows(quarter, plane, block), :] + weights[level] * (
            total - 4.0 * center
        )

    return value


def second_tile(solved_in, weighted_in, force, coupling, scale, depth, solved, weighted, strips,
                sides):
    def tile(block, quarter):
        columns = slice(quarter * 128, (quarter + 1) * 128)
        late = stepped(solved_in, weighted_in, scale, depth, strips, block, quarter)

        def value(plane):
            at = (pl.ds(pl.multiple_of(plane * ROWS + block * 8, 8), 8), columns)
            return late(plane) + force[at]

        solve_tile(value, coupling, scale, depth, solved, weighted, sides, block, quarter)

    return tile


def second_inner_kernel(solved_in, weighted_in, force, coupling, scale, depth, solved, weighted):
    inner_tiles(
        second_tile(
            solved_in, weighted_in, force, coupling, scale, depth, solved, weighted, None, None
        )
    )


def second_edges_kernel(meta, got, here, solved_in, weighted_in, force, coupling, scale, depth, _,
                        __, solved, weighted, payload, first_row, last_row, weighted_late, sides,
                        strips, late):
    place_halo(meta, got, here, weighted_late, strips)

    def right_side(block, quarter):
        columns = slice(quarter * 128, (quarter + 1) * 128)
        value = stepped(solved_in, weighted_late, scale, depth, strips, block, quarter)
        for level in range(LEVELS):
            for plane in (level, LEVELS + level):
                at = (pl.ds(pl.multiple_of(plane * ROWS + block * 8, 8), 8), columns)
                late[at] = value(plane) + force[at]

    def solve(block, quarter):
        columns = slice(quarter * 128, (quarter + 1) * 128)

        def value(plane):
            return late[pl.ds(pl.multiple_of(plane * ROWS + block * 8, 8), 8), columns]

        solve_tile(value, coupling, scale, depth, solved, weighted, sides, block, quarter)

    edge_tiles(right_side)
    edge_tiles(solve)
    send_edges(meta, weighted, sides, payload, first_row, last_row)


def second_inner(*given):
    return pl.pallas_call(
        second_inner_kernel,
        out_shape=BIG,
        in_specs=[VMEM] * 6,
        out_specs=(VMEM,) * 2,
        compiler_params=params(4),
        cost_estimate=cost(30000000),
        name="second_inner",
    )(*given)


def second_edges(meta, halos, *given):
    return pl.pallas_call(
        second_edges_kernel,
        out_shape=BIG + EDGES + BIG[1:],
        in_specs=[SMEM] + [VMEM] * 10,
        out_specs=(VMEM,) * 6,
        input_output_aliases={9: 0, 10: 1, 4: 5},
        scratch_shapes=[SIDES] * 2 + [pltpu.VMEM((PLANES * ROWS, COLS), jnp.float32)],
        compiler_params=params(12),
        cost_estimate=cost(40000000),
        name="second_edges",
    )(meta, *halos, *given)


def last_tile(solved, weighted, scale, depth, strips, ready):
    def tile(block, quarter):
        columns = slice(quarter * 128, (quarter + 1) * 128)
        value = stepped(solved, weighted, scale, depth, strips, block, quarter)
        for level in range(LEVELS):
            for plane in (level, LEVELS + level):
                ready[plane, pl.ds(pl.multiple_of(block * 8, 8), 8), columns] = value(plane)

    return tile


INSIDE = (slice(8, ROWS - 8), slice(128, 384))
OUTSIDE = [
    (slice(0, ROWS), slice(0, 128)),
    (slice(0, ROWS), slice(384, 512)),
    (slice(0, 8), slice(128, 384)),
    (slice(ROWS - 8, ROWS), slice(128, 384)),
]


def last_inner_kernel(solved, weighted, scale, depth, out, ready, sems):
    inner_tiles(last_tile(solved, weighted, scale, depth, None, ready))
    rows, columns = INSIDE
    copy = pltpu.make_async_copy(
        ready.at[:, rows, columns], out.at[:, rows, columns], sems.at[0]
    )
    copy.start()
    copy.wait()


def last_edges_kernel(meta, got, here, solved, weighted_in, scale, depth, _, out, weighted, strips,
                      ready, sems):
    place_halo(meta, got, here, weighted, strips)
    tile = last_tile(solved, weighted, scale, depth, strips, ready)

    def copy(i):
        rows, columns = OUTSIDE[i]
        return pltpu.make_async_copy(
            ready.at[:, rows, columns], out.at[:, rows, columns], sems.at[i]
        )

    def column(quarter):
        def step(block, carry):
            tile(block, quarter)
            return carry

        lax.fori_loop(0, ROWS // 8, step, 0, unroll=8)

    column(0)
    copy(0).start()
    column(3)
    copy(1).start()
    for i, block in ((2, 0), (3, ROWS // 8 - 1)):
        tile(block, 1)
        tile(block, 2)
        copy(i).start()
    for i in range(4):
        copy(i).wait()


READY = [pltpu.VMEM((PLANES, ROWS, COLS), jnp.float32), pltpu.SemaphoreType.DMA((4,))]
ANY = pl.BlockSpec(memory_space=pl.ANY)


def last_inner(*given):
    return pl.pallas_call(
        last_inner_kernel,
        out_shape=f32(PLANES, ROWS, COLS),
        in_specs=[VMEM] * 4,
        out_specs=ANY,
        scratch_shapes=READY,
        compiler_params=params(6),
        cost_estimate=cost(20000000),
        name="last_inner",
    )(*given)


def last_edges(meta, halos, *given):
    return pl.pallas_call(
        last_edges_kernel,
        out_shape=(f32(PLANES, ROWS, COLS), BIG[1]),
        in_specs=[SMEM] + [VMEM] * 6 + [ANY],
        out_specs=(ANY, VMEM),
        input_output_aliases={7: 0, 4: 1},
        scratch_shapes=[SIDES] + READY,
        compiler_params=params(8),
        cost_estimate=cost(20000000),
        name="last_edges",
    )(meta, *halos, *given)[0]


def body(
    adjoint_final,
    diff_scale,
    vert_coupling,
    column_depth,
    seam_table,
    tile_owner,
    prof_face,
    prof_cell,
    prof_time,
    misfit,
):
    rows = prof_face.shape[0]
    slots, meta = pack(
        tile_owner,
        jnp.transpose(seam_table, (2, 1, 0)),
        prof_face.reshape(1, rows),
        prof_cell.reshape(1, rows),
        prof_time.reshape(1, rows),
        misfit.reshape(PLANES, rows),
    )
    slots = lax.all_to_all(slots, ("tile", "sub"), split_axis=0, concat_axis=0, tiled=True)
    adjoint = adjoint_final.reshape(PLANES * ROWS, COLS)
    scale = diff_scale.reshape(LEVELS * ROWS, COLS)
    coupling = vert_coupling.reshape((LEVELS - 1) * ROWS, COLS)
    late = forcing(slots, 1)
    given = (adjoint, late, coupling, scale, column_depth)
    solved, weighted, *edges = first_edges(meta, *given)

    def beside_z():
        return (forcing(slots, 0),)

    def beside_y(depth, early):
        whole = first_inner(solved, weighted, *given[:-1], depth)
        return *whole, early, *second_inner(*whole, early, coupling, scale, depth)

    halos, (solved, weighted, early, *begun) = exchange(
        meta, column_depth, beside_z, beside_y, *edges
    )
    solved, weighted, *edges, _ = second_edges(
        meta, halos, solved, weighted, early, coupling, scale, column_depth, *begun
    )
    halos, begun = exchange(
        meta,
        column_depth,
        lambda: (),
        lambda depth: (last_inner(solved, weighted, scale, depth),),
        *edges,
    )
    out = last_edges(meta, halos, solved, weighted, scale, column_depth, *begun)
    return out.reshape(adjoint_final.shape)


def solution(mesh):
    return jax.shard_map(
        body,
        mesh=mesh,
        in_specs=(
            P(None, None, ("tile", "sub"), None),
            P(None, ("tile", "sub"), None),
            P(None, ("tile", "sub"), None),
            P(("tile", "sub"), None),
            P(),
            P(),
            P(("tile", "sub")),
            P(("tile", "sub")),
            P(("tile", "sub")),
            P(None, None, ("tile", "sub")),
        ),
        out_specs=P(None, None, ("tile", "sub"), None),
        check_vma=False,
    )
```
